128 devices in a mesh: fsdp: 16 (over x, y_hi, core), rep: 8 (over y_lo, z).
Axes of the slice: x: 4, y: 4 (y_hi: 2, y_lo: 2; y = y_hi * 2 + y_lo), z: 4, core: 2. Of those that a mesh axis runs over, the one named last changes fastest.
Arguments:
- tokens: bfloat16 [16384, 1024], P(('fsdp', 'rep')), may hold values from -6 to 6
- out_grad: bfloat16 [16384, 1024], P(('fsdp', 'rep')), may hold values from -6 to 6
- qkv_weight: bfloat16 [1024, 3072], P(('fsdp', 'rep')), may hold values from -0.1875 to 0.1875
- qkv_bias: float32 [3072], replicated, may hold values from -1.75 to 1.75
- out_weight: bfloat16 [1024, 1024], P(('fsdp', 'rep')), may hold values from -1.5 to 1.5
- out_bias: float32 [1024], replicated, may hold values from -1.75 to 1.75
- up_weight: bfloat16 [1024, 4096], P(('fsdp', 'rep')), may hold values from -0.1875 to 0.1875
- up_bias: float32 [4096], replicated, may hold values from -1.75 to 1.75
- down_weight: bfloat16 [4096, 1024], P(('fsdp', 'rep')), may hold values from -0.375 to 0.375
- down_bias: float32 [1024], replicated, may hold values from -1.75 to 1.75
- attn_gain: float32 [1024], replicated, may hold values from 0.5 to 1.5
- attn_shift: float32 [1024], replicated, may hold values from -3 to 3
- ffn_gain: float32 [1024], replicated, may hold values from 0.5 to 1.5
- ffn_shift: float32 [1024], replicated, may hold values from -3 to 3
- head_router_in: bfloat16 [1024, 1024], replicated, may hold values from -0.1875 to 0.1875
- head_router_out: bfloat16 [1024, 4], replicated, may hold values from -0.25 to 0.25
- width_router_in: bfloat16 [1024, 1024], replicated, may hold values from -0.1875 to 0.1875
- width_router_out: bfloat16 [1024, 4], replicated, may hold values from -0.25 to 0.25
- head_choice: int32 [16384], P(('fsdp', 'rep')), may hold values from 0 to 3, as said below
- width_choice: int32 [16384], P(('fsdp', 'rep')), may hold values from 0 to 3, as said below
- seq_ids: int32 [16384], P(('fsdp', 'rep')), may hold values from 0 to 31, as said below
Outputs:
- block_out: bfloat16 [16384, 1024], P(('fsdp', 'rep'))
- balance: float32 [], replicated
- tokens_grad: float32 [16384, 1024], P(('fsdp', 'rep'))
- qkv_weight_grad: float32 [1024, 3072], P(('fsdp', 'rep'))
- out_weight_grad: float32 [1024, 1024], P(('fsdp', 'rep'))
- up_weight_grad: float32 [1024, 4096], P(('fsdp', 'rep'))
- down_weight_grad: float32 [4096, 1024], P(('fsdp', 'rep'))
- qkv_bias_grad: float32 [3072], replicated
- out_bias_grad: float32 [1024], replicated
- up_bias_grad: float32 [4096], replicated
- down_bias_grad: float32 [1024], replicated
- attn_gain_grad: float32 [1024], replicated
- attn_shift_grad: float32 [1024], replicated
- ffn_gain_grad: float32 [1024], replicated
- ffn_shift_grad: float32 [1024], replicated
- head_router_in_grad: float32 [1024, 1024], replicated
- head_router_out_grad: float32 [1024, 4], replicated
- width_router_in_grad: float32 [1024, 1024], replicated
- width_router_out_grad: float32 [1024, 4], replicated
The draws below stay inside these ranges and needn't reach their ends.
Inputs may be any that keep to these rules, and one draw needn't show every extreme that they name: A token uses the first 4 (head_choice + 1) heads. A token uses the first 1024 (width_choice + 1) hidden units. `seq_ids`: tokens form aligned groups of 1024; group g carries 2 g in all its tokens, or 2 g in its first half and 2 g + 1 in its second half; both kinds occur in every draw.
All inputs are finite; a program needn't handle non-finite values.
Results may differ from the reference program's by a relative error of at most 0.015.
Values may be sent and summed in bfloat16 or wider, within the bound.
No kernel may reach another device: no remote copies, remote signals or barrier semaphores. Data moves between devices by JAX's collectives and lax.ppermute only.
A program may use at most 192 MiB of HBM per device.

```python
import jax
import jax.numpy as jnp
from jax import lax

D = 1024
HEADS = 16
HEAD_DIM = 64
FF = 4096
RH = 1024
CHOICES = 4
TOK_DEV = 128
GROUP = 1024
TOKENS = 16384


def skewed_choice(key):
    token_place = jnp.arange(TOKENS)
    device = token_place // TOK_DEV
    devices_all = TOKENS // TOK_DEV
    offset = (2 * CHOICES - 2) * device // devices_all - (CHOICES - 1)
    drawn = jax.random.randint(key, (TOKENS,), 0, CHOICES) + offset
    return jnp.clip(drawn, 0, CHOICES - 1).astype(jnp.int32)


def draw_head_choice(key, part):
    return skewed_choice(jax.random.fold_in(key, 11))


def draw_width_choice(key, part):
    return skewed_choice(jax.random.fold_in(key, 23))


def draw_seq_ids(key, part):
    groups = TOKENS // GROUP
    group_index = jnp.arange(groups)
    halves = jax.random.randint(jax.random.fold_in(key, 37), (groups,), 0, 2)
    halves = jnp.where(group_index == 0, 0, jnp.where(group_index == groups - 1, 1, halves))
    token_place = jnp.arange(TOKENS)
    group_of = token_place // GROUP
    upper = (token_place % GROUP >= GROUP // 2).astype(jnp.int32)
    return (2 * group_of + halves[group_of] * upper).astype(jnp.int32)


def steps_of(own_key, dims, pieces, smallest, largest):
    def one(dim, blocks):
        heights = jax.random.uniform(jax.random.fold_in(jax.random.fold_in(own_key, 6), dim), (blocks,), jnp.float32, smallest / len(pieces), largest / len(pieces))
        return jnp.repeat(jnp.exp(heights), dims[dim] // blocks).reshape((-1,) + (1,) * (len(dims) - dim - 1))

    loudness = one(*pieces[0])
    for cut in pieces[1:]:
        loudness = loudness * one(*cut)
    return loudness


def bell_draw(key, dims, spread, reach, shards=(), kind=jnp.bfloat16):
    factor_of = steps_of(key, dims, shards, -0.22, 0.18) if shards else 1.0
    values = jax.random.normal(key, dims, jnp.float32) * spread * factor_of
    return jnp.minimum(jnp.maximum(values, -reach), reach).astype(kind)


def setup_inputs(seed: int = 0) -> dict:
    key_of = jax.random.split(jax.random.key(seed), 22)
    return {
        "tokens": bell_draw(key_of[0], (TOKENS, D), 1.0, 6.0, ((0, 128),)),
        "out_grad": bell_draw(key_of[1], (TOKENS, D), 1.0, 6.0, ((0, 128),)),
        "qkv_weight": bell_draw(key_of[2], (D, 3 * D), D ** -0.5, 0.1875, ((0, 128),)),
        "qkv_bias": bell_draw(key_of[3], (3 * D,), 0.3, 1.75, (), jnp.float32),
        "out_weight": bell_draw(key_of[4], (D, D), (D // 64) ** -0.5, 1.5, ((0, 128),)),
        "out_bias": bell_draw(key_of[5], (D,), 0.3, 1.75, (), jnp.float32),
        "up_weight": bell_draw(key_of[6], (D, FF), D ** -0.5, 0.1875, ((0, 128),)),
        "up_bias": bell_draw(key_of[7], (FF,), 0.3, 1.75, (), jnp.float32),
        "down_weight": bell_draw(key_of[8], (FF, D), (FF // 16) ** -0.5, 0.375, ((0, 128),)),
        "down_bias": bell_draw(key_of[9], (D,), 0.3, 1.75, (), jnp.float32),
        "attn_gain": jnp.clip(1.0 + 0.1 * jax.random.normal(key_of[10], (D,), jnp.float32), 0.5, 1.5),
        "attn_shift": bell_draw(key_of[11], (D,), 0.5, 3.0, (), jnp.float32),
        "ffn_gain": jnp.clip(1.0 + 0.1 * jax.random.normal(key_of[12], (D,), jnp.float32), 0.5, 1.5),
        "ffn_shift": bell_draw(key_of[13], (D,), 0.5, 3.0, (), jnp.float32),
        "head_router_in": bell_draw(key_of[14], (D, RH), D ** -0.5, 0.1875),
        "head_router_out": bell_draw(key_of[15], (RH, CHOICES), (RH // 2) ** -0.5, 0.25),
        "width_router_in": bell_draw(key_of[16], (D, RH), D ** -0.5, 0.1875),
        "width_router_out": bell_draw(key_of[17], (RH, CHOICES), (RH // 2) ** -0.5, 0.25),
        "head_choice": draw_head_choice(jax.random.fold_in(key_of[21], 71), 0),
        "width_choice": draw_width_choice(jax.random.fold_in(key_of[21], 71), 0),
        "seq_ids": draw_seq_ids(jax.random.fold_in(key_of[21], 71), 0),
    }


EPS = 1e-05
AUX_WEIGHT = 0.1
BLOCKED = -1e+30

@jax.custom_vjp
def low(v):
    return lax.optimization_barrier(v.astype(jnp.bfloat16)).astype(jnp.float32)

@jax.custom_vjp
def low_back(v):
    return v

def low_keep(v):
    return (low(v), None)

def low_pass(kept, grad):
    return (grad,)

def back_keep(v):
    return (v, None)

def back_low(kept, grad):
    return (low(grad),)
low.defvjp(low_keep, low_pass)
low_back.defvjp(back_keep, back_low)

def product(former, latter):
    return jnp.dot(former, latter, precision=lax.Precision.HIGHEST)

def layer_norm(values, gain_vec, shift_vec):
    centred = values - lax.optimization_barrier(jnp.mean(values, axis=-1, keepdims=True))
    inv_std = lax.rsqrt(lax.optimization_barrier(jnp.mean(centred * centred, axis=-1, keepdims=True)) + EPS)
    return centred * inv_std * gain_vec + shift_vec

def rotary(vector, position):
    half = HEAD_DIM // 2
    freqs = 10000.0 ** (-2.0 * jnp.arange(half, dtype=jnp.float32) / HEAD_DIM)
    angle = position.astype(jnp.float32)[:, None] * freqs[None, :]
    cosine = jnp.concatenate([jnp.cos(angle), jnp.cos(angle)], -1)[:, None, :]
    sine = jnp.concatenate([jnp.sin(angle), jnp.sin(angle)], -1)[:, None, :]
    flipped = jnp.concatenate([-vector[..., half:], vector[..., :half]], -1)
    return vector * cosine + flipped * sine

def attend(mixed, group_ids):
    token_place = jnp.arange(GROUP, dtype=jnp.int32)
    same_seq = group_ids[:, None] == group_ids[None, :]
    seg_start = lax.optimization_barrier(jnp.min(jnp.where(same_seq, token_place[None, :], GROUP), axis=1))
    position = token_place - seg_start
    query = rotary(mixed[:, :D].reshape(GROUP, HEADS, HEAD_DIM), position)
    key_part = rotary(mixed[:, D:2 * D].reshape(GROUP, HEADS, HEAD_DIM), position)
    value_part = mixed[:, 2 * D:].reshape(GROUP, HEADS, HEAD_DIM)
    query = low(query)
    key_part = low(key_part)
    value_part = low(value_part)
    raw_score = jnp.einsum('qhd,khd->hqk', query, key_part, precision=lax.Precision.HIGHEST) * HEAD_DIM ** (-0.5)
    raw_score = low_back(raw_score)
    allowed = same_seq & (token_place[None, :] <= token_place[:, None])
    score = jnp.where(allowed[None], raw_score, BLOCKED)
    row_top = lax.optimization_barrier(jnp.max(score, axis=-1, keepdims=True))
    expo = jnp.exp(score - row_top)
    prob = expo / lax.optimization_barrier(jnp.sum(expo, axis=-1, keepdims=True))
    weight = low(prob)
    return jnp.einsum('hqk,khd->qhd', weight, value_part, precision=lax.Precision.HIGHEST)

def route(normed, first_weight, second_weight):
    hidden = low_back(product(normed, first_weight))
    logit = low_back(product(low(jnp.tanh(hidden)), second_weight))
    return jax.nn.softmax(logit, axis=-1)

def layer(inputs, qkv_weight, qkv_bias, out_weight, out_bias, up_weight, up_bias, down_weight, down_bias, attn_gain, attn_shift, ffn_gain, ffn_shift, head_router_in, head_router_out, width_router_in, width_router_out, head_pick, width_pick, head_keep, unit_keep, seq_ids):
    groups = TOKENS // GROUP
    normed1 = low(layer_norm(inputs, attn_gain, attn_shift))
    mixed = low_back(product(normed1, qkv_weight) + qkv_bias)
    per_group = jax.checkpoint(lambda pair: attend(pair[0], pair[1]))
    attended = lax.map(per_group, (mixed.reshape(groups, GROUP, 3 * D), seq_ids.reshape(groups, GROUP)))
    attended = attended.reshape(TOKENS, HEADS, HEAD_DIM) * head_keep[:, :, None]
    attended = low_back(low(attended.reshape(TOKENS, D)))
    attn_pre = low_back(product(attended, out_weight) + out_bias)
    head_prob = route(normed1, head_router_in, head_router_out)
    middle = inputs + lax.optimization_barrier(jnp.sum(head_prob * head_pick, axis=1, keepdims=True)) * attn_pre
    normed2 = low(layer_norm(middle, ffn_gain, ffn_shift))
    upward = low_back(product(normed2, up_weight) + up_bias)
    active = low(jnp.square(jax.nn.relu(upward)) * unit_keep)
    ffn_pre = low_back(product(active, down_weight) + down_bias)
    width_prob = route(normed2, width_router_in, width_router_out)
    result = middle + lax.optimization_barrier(jnp.sum(width_prob * width_pick, axis=1, keepdims=True)) * ffn_pre
    balance = CHOICES * (jnp.sum(lax.optimization_barrier(jnp.mean(head_pick, axis=0)) * lax.optimization_barrier(jnp.mean(head_prob, axis=0))) + jnp.sum(lax.optimization_barrier(jnp.mean(width_pick, axis=0)) * lax.optimization_barrier(jnp.mean(width_prob, axis=0))))
    return (result, balance)

def reference(tokens, out_grad, qkv_weight, qkv_bias, out_weight, out_bias, up_weight, up_bias, down_weight, down_bias, attn_gain, attn_shift, ffn_gain, ffn_shift, head_router_in, head_router_out, width_router_in, width_router_out, head_choice, width_choice, seq_ids):
    floats = [array.astype(jnp.float32) for array in (tokens, qkv_weight, qkv_bias, out_weight, out_bias, up_weight, up_bias, down_weight, down_bias, attn_gain, attn_shift, ffn_gain, ffn_shift, head_router_in, head_router_out, width_router_in, width_router_out)]
    options = jnp.arange(CHOICES, dtype=jnp.int32)
    head_pick = (head_choice[:, None] == options[None, :]).astype(jnp.float32)
    width_pick = (width_choice[:, None] == options[None, :]).astype(jnp.float32)
    head_keep = (jnp.arange(HEADS, dtype=jnp.int32)[None, :] < HEADS // CHOICES * (head_choice[:, None] + 1)).astype(jnp.float32)
    unit_keep = (jnp.arange(FF, dtype=jnp.int32)[None, :] < FF // CHOICES * (width_choice[:, None] + 1)).astype(jnp.float32)

    def forward(*params):
        return layer(*params, head_pick, width_pick, head_keep, unit_keep, seq_ids)
    (result, balance), pull = jax.vjp(forward, *floats)
    grads = pull((out_grad.astype(jnp.float32), jnp.asarray(AUX_WEIGHT, jnp.float32)))
    return (result.astype(jnp.bfloat16), balance, grads[0], grads[1], grads[3], grads[5], grads[7], grads[2], grads[4], grads[6], grads[8], grads[9], grads[10], grads[11], grads[12], grads[13], grads[14], grads[15], grads[16])
```

```python
import jax
import jax.numpy as jnp
import numpy as np
from jax import lax
from jax.sharding import Mesh
from jax.sharding import PartitionSpec as P


AXES = ("x", "yh", "c", "yl", "z")
CHIPS = ("x", "yh", "yl")
RING = 4
HEADS = 16
HEAD_DIM = 64
CHOICES = 4
EPS = 1e-05
AUX_WEIGHT = 0.1
BLOCKED = -1e30
bf16 = jnp.bfloat16
f32 = jnp.float32


def dot(former, latter):
    return jnp.dot(former, latter, preferred_element_type=f32)


def against(former, latter):
    return lax.dot_general(former, latter, (((1,), (1,)), ((), ())), preferred_element_type=f32)


def across(former, latter):
    return lax.dot_general(former, latter, (((0,), (0,)), ((), ())), preferred_element_type=f32)


def swap(value, axes):
    return lax.all_to_all(value, axes, split_axis=0, concat_axis=0, tiled=True)


def spread(value, axes, count):
    return swap(jnp.broadcast_to(value[None], (count,) + value.shape), axes)


def other_core(value):
    return lax.ppermute(value, "c", [(0, 1), (1, 0)])


def ring_gather(value):
    blocks = [value]
    for shift in range(1, RING):
        blocks.append(lax.ppermute(value, "z", [(k, (k + shift) % RING) for k in range(RING)]))
    return jnp.concatenate(blocks, axis=0)


def ring_scatter(value, rows):
    total = value[:rows]
    for shift in range(1, RING):
        part = value[shift * rows : (shift + 1) * rows].astype(bf16)
        total = total + lax.ppermute(part, "z", [(k, (k - shift) % RING) for k in range(RING)]).astype(f32)
    return total


def gather_rows(value, core):
    mine = spread(value, CHIPS, 16).reshape((4, 2, 2) + value.shape)
    theirs = other_core(mine)
    first = core == 0
    return jnp.stack([jnp.where(first, mine, theirs), jnp.where(first, theirs, mine)], axis=2)


def scatter_rows(value, core):
    split = value.reshape((4, 2, 2, 2) + value.shape[1:])
    mine = lax.dynamic_index_in_dim(split, core, 2, keepdims=False)
    theirs = lax.dynamic_index_in_dim(split, 1 - core, 2, keepdims=False).astype(bf16)
    pair = (mine + other_core(theirs).astype(f32)).astype(bf16)
    pieces = swap(pair.reshape((16,) + value.shape[1:]), CHIPS)
    return jnp.sum(pieces.astype(f32), axis=0)


def normalize(values):
    centred = values - jnp.mean(values, axis=-1, keepdims=True)
    inv_std = lax.rsqrt(jnp.mean(centred * centred, axis=-1, keepdims=True) + EPS)
    return (centred * inv_std, inv_std)


def normalize_back(gradient, unit_part, inv_std, gain_vec):
    scaled = gradient * gain_vec
    inner = (
        scaled
        - jnp.mean(scaled, axis=-1, keepdims=True)
        - unit_part * jnp.mean(scaled * unit_part, axis=-1, keepdims=True)
    )
    return (inner * inv_std, jnp.sum(gradient * unit_part, axis=0), jnp.sum(gradient, axis=0))


def rotary_tables(position):
    half = HEAD_DIM // 2
    freqs = 10000.0 ** (-2.0 * jnp.arange(half, dtype=f32) / HEAD_DIM)
    angle = position.astype(f32)[:, None] * freqs[None, :]
    cosine = jnp.concatenate([jnp.cos(angle), jnp.cos(angle)], -1)[:, None, :]
    sine = jnp.concatenate([jnp.sin(angle), jnp.sin(angle)], -1)[:, None, :]
    return (cosine, sine)


def turn(vector, cosine, sine):
    half = vector.shape[-1] // 2
    flipped = jnp.concatenate([-vector[..., half:], vector[..., :half]], -1)
    return vector * cosine + flipped * sine


def turn_back(gradient, cosine, sine):
    half = gradient.shape[-1] // 2
    moved = gradient * sine
    flipped = jnp.concatenate([moved[..., half:], -moved[..., :half]], -1)
    return gradient * cosine + flipped


def route_back(d_prob, prob):
    return (prob * (d_prob - jnp.sum(prob * d_prob, axis=-1, keepdims=True))).astype(bf16)


def two_parts(value):
    upper = value.astype(bf16)
    return upper, (value - upper.astype(f32)).astype(bf16)


def local(
    tokens,
    out_grad,
    qkv_weight,
    qkv_bias,
    out_weight,
    out_bias,
    up_weight,
    up_bias,
    down_weight,
    down_bias,
    attn_gain,
    attn_shift,
    ffn_gain,
    ffn_shift,
    head_router_in,
    head_router_out,
    width_router_in,
    width_router_out,
    head_choice,
    width_choice,
    seq_ids,
):
    rows, width = tokens.shape
    half_rows = RING * rows
    own_heads = HEADS // RING
    head_width = own_heads * HEAD_DIM
    units = up_weight.shape[1] // RING
    router_width = head_router_in.shape[1]
    router_slice = router_width // RING
    all_rows = rows * 128
    score_scale = HEAD_DIM ** (-0.5)
    core = lax.axis_index("c")
    upper_half = lax.axis_index("yl")
    place = lax.axis_index("z")

    options = jnp.arange(CHOICES)
    head_pick = (head_choice[:, None] == options[None, :]).astype(f32)
    width_pick = (width_choice[:, None] == options[None, :]).astype(f32)
    counts = jnp.concatenate([jnp.sum(head_pick, axis=0), jnp.sum(width_pick, axis=0)])[None]
    counts = jnp.sum(spread(counts, AXES, 128).reshape(128, 2 * CHOICES), axis=0)
    head_share = counts[:CHOICES] / all_rows
    width_share = counts[CHOICES:] / all_rows
    aux_factor = AUX_WEIGHT * CHOICES / all_rows

    qkv_piece = qkv_weight.reshape(8, 3, RING, head_width).transpose(2, 0, 1, 3).reshape(RING, 8, 3 * head_width)
    up_piece = up_weight.reshape(8, 32, RING, 32).transpose(2, 0, 1, 3).reshape(RING, 8, units)
    choice_rows = jnp.stack([head_choice, width_choice] + [jnp.zeros_like(head_choice)] * 6).astype(bf16)
    pieces = swap(
        jnp.concatenate(
            [qkv_piece, up_piece, jnp.broadcast_to(choice_rows[None], (RING, 8, rows))], axis=-1
        ),
        "z",
    )
    ring_order = (place - jnp.arange(RING)) % RING
    choices = jnp.take(pieces[:, :2, 3 * head_width + units :], ring_order, axis=0).astype(f32)
    head_half = choices[:, 0].reshape(half_rows, 1)
    width_half = choices[:, 1].reshape(half_rows, 1)
    pieces = pieces.reshape(8 * RING, -1)
    out_piece = lax.ppermute(out_weight, ("x", "z"), [(a * 4 + b, b * 4 + a) for a in range(4) for b in range(4)])

    tokens_half = ring_gather(tokens)
    qkv_slice = gather_rows(pieces[:, : 3 * head_width], core).reshape(width, 3 * head_width)
    up_slice = gather_rows(pieces[:, 3 * head_width : 3 * head_width + units], core).reshape(width, units)
    rest = gather_rows(jnp.concatenate([down_weight, out_piece], axis=0), core)
    down_slice = rest[..., :32, :].reshape(units, width)
    out_slice = rest[..., 32:, :].transpose(1, 2, 3, 0, 4, 5).reshape(head_width, width)

    inputs = tokens.astype(f32)
    grad_out = out_grad.astype(f32)
    unit1_half, _ = normalize(tokens_half.astype(f32))
    low1_half = (unit1_half * attn_gain + attn_shift).astype(bf16)
    unit1, inv1 = normalize(inputs)
    low1 = (unit1 * attn_gain + attn_shift).astype(bf16)
    own_qkv_bias = lax.dynamic_index_in_dim(qkv_bias.reshape(3, RING, head_width), place, 1, keepdims=False)
    mixed = dot(low1_half, qkv_slice) + own_qkv_bias.reshape(3 * head_width)
    one_sequence = (upper_half == 1) & (seq_ids[0] % 2 == 0)
    order = (ring_order[:, None] * rows + jnp.arange(rows)[None, :]).reshape(half_rows)
    cosine, sine = rotary_tables(order + jnp.where(one_sequence, half_rows, 0))
    heads = (half_rows, own_heads, HEAD_DIM)
    query = turn(mixed[:, :head_width].reshape(heads), cosine, sine).astype(bf16)
    key_own = turn(mixed[:, head_width : 2 * head_width].reshape(heads), cosine, sine).astype(bf16)
    value_own = mixed[:, 2 * head_width :].astype(bf16)
    lower = lax.ppermute(
        jnp.concatenate([key_own.reshape(half_rows, head_width), value_own], axis=1), "yl", [(0, 1)]
    )
    key_all = jnp.concatenate([lower[:, :head_width].reshape(heads), key_own], axis=0)
    value_all = jnp.concatenate([lower[:, head_width:], value_own], axis=0).reshape((2 * half_rows,) + heads[1:])
    allowed = jnp.concatenate(
        [jnp.broadcast_to(one_sequence, (half_rows, half_rows)), order[None, :] <= order[:, None]], axis=1
    )[None]

    def scores():
        score = jnp.einsum("qhd,khd->hqk", query, key_all, preferred_element_type=f32) * score_scale
        return jnp.where(allowed, score, BLOCKED)

    score = scores()
    row_top = jnp.max(score, axis=-1, keepdims=True)
    log_total = row_top + jnp.log(jnp.sum(jnp.exp(score - row_top), axis=-1, keepdims=True))
    weight = jnp.exp(score - log_total).astype(bf16)
    head_keep = (head_half >= place).astype(f32)
    attended = jnp.einsum("hqk,khd->qhd", weight, value_all, preferred_element_type=f32)
    attended = (attended.reshape(half_rows, head_width) * head_keep).astype(bf16)
    attn_pre = ring_scatter(dot(attended, out_slice), rows) + out_bias

    head_squash = jnp.tanh(dot(low1, head_router_in))
    head_squash_low = head_squash.astype(bf16)
    head_prob = jax.nn.softmax(dot(head_squash_low, head_router_out), axis=-1)
    head_gate = jnp.sum(head_prob * head_pick, axis=1, keepdims=True)
    middle = inputs + head_gate * attn_pre
    unit2, inv2 = normalize(middle)
    low2 = (unit2 * ffn_gain + ffn_shift).astype(bf16)

    grad_half = ring_gather(out_grad).astype(f32)
    low2_half = ring_gather(low2)
    upward = dot(low2_half, up_slice) + lax.dynamic_index_in_dim(
        up_bias.reshape(32, RING, 32), place, 1, keepdims=False
    ).reshape(units)
    unit_keep = jnp.broadcast_to(
        (width_half >= jnp.arange(RING)[None, :]).astype(f32)[:, :, None], (half_rows, RING, units // RING)
    ).reshape(half_rows, units)
    active = jax.nn.relu(upward)
    active_low = (active * active * unit_keep).astype(bf16)
    ffn_part = dot(active_low, down_slice)
    width_dgate_part = jnp.sum(grad_half * ffn_part, axis=1, keepdims=True)
    ffn_pre = ring_scatter(ffn_part, rows) + down_bias
    width_squash_half = jnp.tanh(dot(low2_half, width_router_in))
    width_squash_low_half = width_squash_half.astype(bf16)
    width_prob_half = jax.nn.softmax(dot(width_squash_low_half, width_router_out), axis=-1)
    width_gate_half = jnp.sum(
        width_prob_half * (width_half == options[None, :].astype(f32)).astype(f32), axis=1, keepdims=True
    )
    width_squash = width_squash_half[:rows]
    width_squash_low = width_squash_low_half[:rows]
    width_prob = width_prob_half[:rows]
    width_gate = width_gate_half[:rows]
    result = (middle + width_gate * ffn_pre).astype(bf16)

    d_ffn_half = (width_gate_half * grad_half).astype(bf16)
    d_active = against(d_ffn_half, down_slice)
    d_up = (d_active * unit_keep * 2.0 * active).astype(bf16)
    d_normed2_part = against(d_up, up_slice)
    down_part = across(active_low, d_ffn_half).reshape(32, 32, width)
    up_part = across(low2_half, d_up).reshape(32, 32, units)
    dgate_upper, dgate_lower = two_parts(width_dgate_part)
    dgate_lanes = jnp.concatenate(
        [dgate_upper.astype(f32), dgate_lower.astype(f32), jnp.zeros((half_rows, 126), f32)], axis=1
    )
    scattered = ring_scatter(jnp.concatenate([d_normed2_part, dgate_lanes], axis=1), rows)
    d_normed2 = scattered[:, :width]
    width_dgate = (
        scattered[:, width : width + 1]
        + scattered[:, width + 1 : width + 2]
        + jnp.sum(grad_out * down_bias, axis=1, keepdims=True)
    )
    d_logit_width = route_back(width_pick * width_dgate + aux_factor * width_share[None, :], width_prob)
    width_out_grad = across(width_squash_low, d_logit_width)
    d_hidden_width = (against(d_logit_width, width_router_out) * (1.0 - width_squash * width_squash)).astype(bf16)
    d_middle, ffn_gain_grad, ffn_shift_grad = normalize_back(
        d_normed2 + against(d_hidden_width, width_router_in), unit2, inv2, ffn_gain
    )
    d_middle = d_middle + grad_out

    head_dgate = jnp.sum(d_middle * attn_pre, axis=1, keepdims=True)
    d_attn = (head_gate * d_middle).astype(bf16)
    d_logit_head = route_back(head_pick * head_dgate + aux_factor * head_share[None, :], head_prob)
    head_out_grad = across(head_squash_low, d_logit_head)
    d_hidden_head = (against(d_logit_head, head_router_out) * (1.0 - head_squash * head_squash)).astype(bf16)
    router_term1 = against(d_hidden_head, head_router_in)
    gathered = ring_gather(
        jnp.concatenate([d_attn, d_logit_width, d_logit_head, jnp.zeros((rows, 120), bf16)], axis=1)
    )
    d_attn_half = gathered[:, :width]
    d_logit_width_half = gathered[:, width : width + CHOICES]
    d_logit_head_half = gathered[:, width + CHOICES : width + 2 * CHOICES]

    own_columns = place * router_slice

    def columns(value):
        return lax.dynamic_slice_in_dim(value, own_columns, router_slice, 1)

    def out_rows(value):
        return lax.dynamic_slice_in_dim(value, own_columns, router_slice, 0)

    width_slice = columns(width_squash_half)
    d_width_slice = (
        against(d_logit_width_half, out_rows(width_router_out)) * (1.0 - width_slice * width_slice)
    ).astype(bf16)
    width_in_part = across(low2_half, d_width_slice).reshape(32, 32, router_slice)
    head_slice = jnp.tanh(dot(low1_half, columns(head_router_in)))
    d_head_slice = (
        against(d_logit_head_half, out_rows(head_router_out)) * (1.0 - head_slice * head_slice)
    ).astype(bf16)
    head_in_part = across(low1_half, d_head_slice).reshape(32, 32, router_slice)

    out_part = across(attended, d_attn_half)
    out_part = out_part.reshape(2, 2, 2, 4, 8, width).transpose(3, 0, 1, 2, 4, 5).reshape(32, 8, width)
    d_attended = (against(d_attn_half, out_slice) * head_keep).astype(bf16).reshape(heads)
    prob = jnp.exp(scores() - log_total)
    prob_low = prob.astype(bf16)
    d_prob = jnp.einsum("qhd,khd->hqk", d_attended, value_all, preferred_element_type=f32)
    d_score = (prob * (d_prob - jnp.sum(prob * d_prob, axis=-1, keepdims=True))).astype(bf16)
    d_query = jnp.einsum("hqk,khd->qhd", d_score, key_all, preferred_element_type=f32) * score_scale
    d_keys = jnp.einsum("hqk,qhd->khd", d_score, query, preferred_element_type=f32) * score_scale
    d_values = jnp.einsum("hqk,qhd->khd", prob_low, d_attended, preferred_element_type=f32)
    d_keys = d_keys.reshape(2 * half_rows, head_width)
    d_values = d_values.reshape(2 * half_rows, head_width)
    back = lax.ppermute(
        jnp.concatenate([d_keys[:half_rows], d_values[:half_rows]], axis=1).astype(bf16), "yl", [(1, 0)]
    ).astype(f32)
    d_key_own = d_keys[half_rows:] + back[:, :head_width]
    d_value_own = d_values[half_rows:] + back[:, head_width:]
    d_mixed = jnp.concatenate(
        [
            turn_back(d_query, cosine, sine).reshape(half_rows, head_width),
            turn_back(d_key_own.reshape(heads), cosine, sine).reshape(half_rows, head_width),
            d_value_own,
        ],
        axis=1,
    ).astype(bf16)
    qkv_part = across(low1_half, d_mixed).reshape(32, 32, 3 * head_width)
    d_normed1 = ring_scatter(against(d_mixed, qkv_slice), rows)
    d_inputs, attn_gain_grad, attn_shift_grad = normalize_back(d_normed1 + router_term1, unit1, inv1, attn_gain)
    d_inputs = d_inputs + d_middle

    feed_rows = scatter_rows(jnp.concatenate([up_part, down_part], axis=1), core)
    down_grad = feed_rows[32:]
    mixer_rows = scatter_rows(
        jnp.concatenate(
            [
                jnp.concatenate([qkv_part, width_in_part, head_in_part], axis=2),
                jnp.pad(out_part, ((0, 0), (0, 0), (0, 2 * router_slice - (width - 3 * head_width)))),
            ],
            axis=1,
        ),
        core,
    )
    out_grad_rows = lax.ppermute(
        mixer_rows[32:, :width], ("x", "z"), [(a * 4 + b, b * 4 + a) for a in range(4) for b in range(4)]
    )
    to_owner = jnp.concatenate([mixer_rows[:32, : 3 * head_width], feed_rows[:32]], axis=1).reshape(RING, 8, -1)
    owned = swap(to_owner, "z")
    qkv_grad = (
        owned[:, :, : 3 * head_width].reshape(RING, 8, 3, head_width).transpose(1, 2, 0, 3).reshape(8, 3 * width)
    )
    up_grad = owned[:, :, 3 * head_width :].reshape(RING, 8, 32, 32).transpose(1, 2, 0, 3).reshape(8, RING * units)
    routers = spread(mixer_rows[:32, 3 * head_width :].astype(bf16), "z", RING)
    routers = gather_rows(routers.reshape(RING * 32, 2 * router_slice), core)
    routers = routers.reshape(32, RING, 32, 2, router_slice).transpose(3, 0, 2, 1, 4)
    routers = routers.reshape(2, width, router_width).astype(f32)

    own_place = (jnp.arange(RING) == place).astype(f32)
    d_mixed_sum = jnp.sum(d_mixed, axis=0, dtype=f32).reshape(3, 1, head_width) * own_place[None, :, None]
    d_up_sum = jnp.sum(d_up, axis=0, dtype=f32).reshape(32, 1, 32) * own_place[None, :, None]
    d_ffn = (width_gate * grad_out).astype(bf16)
    smalls = [
        d_mixed_sum.reshape(-1),
        jnp.sum(d_attn, axis=0, dtype=f32),
        d_up_sum.reshape(-1),
        jnp.sum(d_ffn, axis=0, dtype=f32),
        attn_gain_grad,
        attn_shift_grad,
        ffn_gain_grad,
        ffn_shift_grad,
        head_out_grad.reshape(-1),
        width_out_grad.reshape(-1),
        jnp.sum(head_prob, axis=0),
        jnp.sum(width_prob, axis=0),
    ]
    sizes = [value.shape[0] for value in smalls]
    padded = -(-sum(sizes) // (128 * 128)) * 128
    flat = jnp.concatenate(smalls + [jnp.zeros((128 * padded - sum(sizes),), f32)])
    flat = jnp.sum(swap(flat.reshape(128, padded), AXES), axis=0)
    flat = spread(flat[None], AXES, 128).reshape(128 * padded)
    bounds = np.cumsum([0] + sizes)
    summed = [flat[bounds[k] : bounds[k + 1]] for k in range(len(sizes))]
    balance = CHOICES * (
        jnp.sum(head_share * summed[10] / all_rows) + jnp.sum(width_share * summed[11] / all_rows)
    )
    return (
        result,
        balance,
        d_inputs,
        qkv_grad,
        out_grad_rows,
        up_grad,
        down_grad,
        summed[0],
        summed[1],
        summed[2],
        summed[3],
        summed[4],
        summed[5],
        summed[6],
        summed[7],
        routers[1],
        summed[8].reshape(router_width, CHOICES),
        routers[0],
        summed[9].reshape(router_width, CHOICES),
    )


def solution(mesh):
    fine = Mesh(mesh.devices.reshape(4, 2, 2, 2, 4), AXES)
    whole = P(AXES, None)
    vector = P(AXES)
    in_specs = (
        whole, whole, whole, P(), whole, P(), whole, P(), whole, P(),
        P(), P(), P(), P(), P(), P(), P(), P(), vector, vector, vector,
    )
    out_specs = (whole, P(), whole, whole, whole, whole, whole) + (P(),) * 12
    return jax.shard_map(local, mesh=fine, in_specs=in_specs, out_specs=out_specs, check_vma=False)
```

```python
import jax
import jax.numpy as jnp
import numpy as np
from jax import lax
from jax.experimental import pallas as pl
from jax.experimental.pallas import tpu as pltpu
from jax.sharding import Mesh
from jax.sharding import PartitionSpec as P


AXES = ("x", "yh", "c", "yl", "z")
CHIPS = ("x", "yh", "yl")
RING = 4
HEADS = 16
HEAD_DIM = 64
CHOICES = 4
EPS = 1e-05
AUX_WEIGHT = 0.1
BLOCKED = -1e30
bf16 = jnp.bfloat16
f32 = jnp.float32
INTERPRET = False
QUERIES = 256


def dot(former, latter):
    return jnp.dot(former, latter, preferred_element_type=f32)


def against(former, latter):
    return lax.dot_general(former, latter, (((1,), (1,)), ((), ())), preferred_element_type=f32)


def across(former, latter):
    return lax.dot_general(former, latter, (((0,), (0,)), ((), ())), preferred_element_type=f32)


def swap(value, axes):
    return lax.all_to_all(value, axes, split_axis=0, concat_axis=0, tiled=True)


def spread(value, axes, count):
    return swap(jnp.broadcast_to(value[None], (count,) + value.shape), axes)


def other_core(value):
    return lax.ppermute(value, "c", [(0, 1), (1, 0)])


def tie(value, *others):
    for other in others:
        value = value + (other[(0,) * other.ndim].astype(f32) * 0.0).astype(value.dtype)
    return value


def ring_blocks(value):
    return [value] + [
        lax.ppermute(value, "z", [(k, (k + shift) % RING) for k in range(RING)]) for shift in range(1, RING)
    ]


def to_sender(value, shift):
    return lax.ppermute(value, "z", [(k, (k - shift) % RING) for k in range(RING)])


def ring_product(former, latter, product, rows):
    sent = [
        to_sender(product(former[k * rows : (k + 1) * rows], latter).astype(bf16), k) for k in range(1, RING)
    ]
    total = product(former[:rows], latter)
    for part in sent:
        total = total + part.astype(f32)
    return total


def spread_chips(value):
    mine = spread(value, CHIPS, 16)
    return mine, other_core(mine)


def both_cores(mine, theirs, core):
    mine = mine.reshape((4, 2, 2) + mine.shape[1:])
    theirs = theirs.reshape((4, 2, 2) + theirs.shape[1:])
    first = core == 0
    return jnp.stack([jnp.where(first, mine, theirs), jnp.where(first, theirs, mine)], axis=2)


def pair_sum(mine, theirs):
    return mine + other_core(theirs).astype(f32)


def block_sum(pieces):
    return jnp.sum(pieces.astype(f32), axis=0)


def normalize(values):
    centred = values - jnp.mean(values, axis=-1, keepdims=True)
    inv_std = lax.rsqrt(jnp.mean(centred * centred, axis=-1, keepdims=True) + EPS)
    return (centred * inv_std, inv_std)


def normalize_back(gradient, unit_part, inv_std, gain_vec):
    scaled = gradient * gain_vec
    inner = (
        scaled
        - jnp.mean(scaled, axis=-1, keepdims=True)
        - unit_part * jnp.mean(scaled * unit_part, axis=-1, keepdims=True)
    )
    return (inner * inv_std, jnp.sum(gradient * unit_part, axis=0), jnp.sum(gradient, axis=0))


def rotary_tables(position):
    lane = jnp.arange(2 * HEAD_DIM)
    half = HEAD_DIM // 2
    freqs = 10000.0 ** (-2.0 * (lane % half).astype(f32) / HEAD_DIM)
    angle = position.astype(f32)[:, None] * freqs[None, :]
    return (jnp.cos(angle), jnp.sin(angle) * jnp.where(lane % HEAD_DIM < half, -1.0, 1.0)[None, :])


def call(body, outs, args, scratch=(), scalars=0, flops=0, waits=(), room=24):
    given, taken = len(args), len(args) + len(waits)

    def large(value):
        return int(np.prod(value.shape)) * value.dtype.itemsize >= 65536

    copied_in = [k for k in range(scalars, given) if large(args[k])]
    copied_out = [k for k in range(len(outs)) if large(outs[k])]
    copies = len(copied_in) + len(copied_out)

    def whole(*refs):
        ins, results = list(refs[:given]), list(refs[taken : taken + len(outs)])
        rest = refs[taken + len(outs) :]
        semaphores, buffers, own = rest[0], rest[1 : 1 + copies], rest[1 + copies :]
        moves = []
        for j, k in enumerate(copied_in):
            moves.append(pltpu.make_async_copy(ins[k], buffers[j], semaphores.at[j]))
            moves[-1].start()
            ins[k] = buffers[j]
        for move in moves:
            move.wait()
        targets = list(results)
        for j, k in enumerate(copied_out, len(copied_in)):
            results[k] = buffers[j]
        body(*ins, *results, *own)
        moves = []
        for j, k in enumerate(copied_out, len(copied_in)):
            moves.append(pltpu.make_async_copy(buffers[j], targets[k], semaphores.at[j]))
            moves[-1].start()
        for move in moves:
            move.wait()

    def spec(k, copied):
        return pl.BlockSpec(memory_space=pltpu.HBM if k in copied else pltpu.VMEM)

    spaces = [pl.BlockSpec(memory_space=pltpu.SMEM)] * scalars
    spaces += [spec(k, copied_in) for k in range(scalars, given)]
    spaces += [pl.BlockSpec(memory_space=pl.ANY)] * len(waits)
    buffers = [pltpu.VMEM(args[k].shape, args[k].dtype) for k in copied_in]
    buffers += [pltpu.VMEM(outs[k].shape, outs[k].dtype) for k in copied_out]
    moved = sum(int(np.prod(value.shape)) * value.dtype.itemsize for value in list(args) + list(outs))
    shapes = [pltpu.HBM(v.shape, v.dtype) if k in copied_out else v for k, v in enumerate(outs)]
    args = [pltpu.with_memory_space_constraint(v, pltpu.HBM) if k in copied_in else v for k, v in enumerate(args)]
    return pl.pallas_call(
        whole,
        out_shape=tuple(shapes),
        in_specs=spaces,
        out_specs=tuple(spec(k, copied_out) for k in range(len(outs))),
        scratch_shapes=[pltpu.SemaphoreType.DMA((copies,))] + buffers + list(scratch),
        compiler_params=pltpu.CompilerParams(vmem_limit_bytes=room << 20),
        cost_estimate=pl.CostEstimate(flops=flops, bytes_accessed=moved, transcendentals=0),
        interpret=INTERPRET,
    )(*args, *waits)


def shaped(shape, kind):
    return jax.ShapeDtypeStruct(shape, kind)


def turned(value, cosine, sine):
    lane = lax.broadcasted_iota(jnp.int32, value.shape, 1)
    width = value.shape[1]
    half = HEAD_DIM // 2
    flipped = jnp.where(
        lane % HEAD_DIM < half, pltpu.roll(value, width - half, 1), pltpu.roll(value, half, 1)
    )
    return value * cosine + flipped * sine


def turned_back(value, cosine, sine):
    lane = lax.broadcasted_iota(jnp.int32, value.shape, 1)
    width = value.shape[1]
    half = HEAD_DIM // 2
    moved = value * sine
    flipped = jnp.where(
        lane % HEAD_DIM < half, pltpu.roll(moved, width - half, 1), pltpu.roll(moved, half, 1)
    )
    return value * cosine + flipped


def project_body(core_ref, t0, t1, t2, t3, gain, shift, mine, theirs, bias, cosine, sine, low_ref, query_ref, kv_ref, weight_ref):
    core = core_ref[0]
    weight_ref[:, pl.ds(core, 1)] = mine[...][:, None]
    weight_ref[:, pl.ds(1 - core, 1)] = theirs[...][:, None]
    weight = weight_ref[...].reshape(-1, weight_ref.shape[-1])
    rows = t0.shape[0]
    heads = query_ref.shape[1]
    for k, block in enumerate((t0, t1, t2, t3)):
        at = slice(k * rows, (k + 1) * rows)
        unit, _ = normalize(block[...].astype(f32))
        low = (unit * gain[...] + shift[...]).astype(bf16)
        low_ref[at, :] = low
        mixed = dot(low, weight) + bias[...]
        for j in range(heads // 128):
            lanes = slice(128 * j, 128 * (j + 1))
            query_ref[at, lanes] = turned(mixed[:, lanes], cosine[at, :], sine[at, :]).astype(bf16)
            key = mixed[:, heads + 128 * j : heads + 128 * (j + 1)]
            kv_ref[at, lanes] = turned(key, cosine[at, :], sine[at, :]).astype(bf16)
        kv_ref[at, heads:] = mixed[:, 2 * heads :].astype(bf16)


def scores_of(h, q_block, flag, key_ref, query, order_column, order_row_ref):
    lane = lax.broadcasted_iota(jnp.int32, query.shape, 1)
    own = jnp.where(lane // HEAD_DIM == h, query, jnp.zeros_like(query)) * jnp.asarray(HEAD_DIM ** (-0.5), bf16)
    score = against(key_ref[...], own)
    half = score.shape[0] // 2
    lower = jnp.where(flag, score[:half], BLOCKED)
    upper = jnp.where(order_column[...] <= order_row_ref[q_block], score[half:], BLOCKED)
    return lower, upper, own


def attend_body(
    flag_ref, query_ref, kv_ref, low_kv_ref, order_column, order_row_ref, keep_ref,
    out_ref, total_ref, key_all, value_turned, out_turned,
):
    heads = query_ref.shape[1]
    half = kv_ref.shape[0]
    blocks = query_ref.shape[0] // QUERIES
    key_all[:half] = low_kv_ref[:, :heads]
    key_all[half:] = kv_ref[:, :heads]
    value_turned[:, :half] = low_kv_ref[:, heads:].T
    value_turned[:, half:] = kv_ref[:, heads:].T
    flag = flag_ref[0] == 1

    def step(at, carry):
        h, q_block = at // blocks, at % blocks
        query = query_ref[pl.ds(pl.multiple_of(q_block * QUERIES, QUERIES), QUERIES), :]
        lower, upper, _ = scores_of(h, q_block, flag, key_all, query, order_column, order_row_ref)
        top = jnp.maximum(jnp.max(lower, axis=0, keepdims=True), jnp.max(upper, axis=0, keepdims=True))
        lower = jnp.exp(lower - top)
        upper = jnp.exp(upper - top)
        total = jnp.sum(lower, axis=0, keepdims=True) + jnp.sum(upper, axis=0, keepdims=True)
        scale = 1.0 / total
        total_ref[at] = top + jnp.log(total)
        rows = pl.ds(pl.multiple_of(h * HEAD_DIM, HEAD_DIM), HEAD_DIM)
        value = value_turned[rows, :]
        out_turned[q_block, rows, :] = dot(value[:, :half], (lower * scale).astype(bf16)) + dot(
            value[:, half:], (upper * scale).astype(bf16)
        )
        return carry

    lax.fori_loop(0, blocks * (heads // HEAD_DIM), step, 0)
    for k in range(blocks):
        at = slice(k * QUERIES, (k + 1) * QUERIES)
        out_ref[at, :] = (out_turned[k].T * keep_ref[at, :]).astype(bf16)


def attend_back_body(
    flag_ref, g0, g1, g2, g3, out_slice, query_ref, kv_ref, low_kv_ref, order_column, order_row_ref, keep_ref,
    total_ref, cosine, sine, d_query_ref, send_ref, own_ref, key_all, value_all, key_turned, d_out, d_query_turned,
    d_key, d_value,
):
    heads = query_ref.shape[1]
    half = kv_ref.shape[0]
    rows = g0.shape[0]
    blocks = query_ref.shape[0] // QUERIES
    key_all[:half] = low_kv_ref[:, :heads]
    key_all[half:] = kv_ref[:, :heads]
    value_all[:half] = low_kv_ref[:, heads:]
    value_all[half:] = kv_ref[:, heads:]
    key_turned[:, :half] = low_kv_ref[:, :heads].T
    key_turned[:, half:] = kv_ref[:, :heads].T
    d_key[...] = jnp.zeros_like(d_key)
    d_value[...] = jnp.zeros_like(d_value)
    for k, block in enumerate((g0, g1, g2, g3)):
        at = slice(k * rows, (k + 1) * rows)
        part = against(block[...], out_slice[...]).astype(bf16).astype(f32)
        d_out[at, :] = (part * keep_ref[at, :]).astype(bf16)
    flag = flag_ref[0] == 1

    def step(at, carry):
        h, q_block = at // blocks, at % blocks
        here = pl.ds(pl.multiple_of(q_block * QUERIES, QUERIES), QUERIES)
        query = query_ref[here, :]
        lower, upper, own = scores_of(h, q_block, flag, key_all, query, order_column, order_row_ref)
        total = total_ref[at]
        lower = jnp.exp(lower - total)
        upper = jnp.exp(upper - total)
        lane = lax.broadcasted_iota(jnp.int32, query.shape, 1)
        gradient = d_out[here, :]
        gradient = jnp.where(lane // HEAD_DIM == h, gradient, jnp.zeros_like(gradient))
        d_value[:half] += dot(lower.astype(bf16), gradient)
        d_value[half:] += dot(upper.astype(bf16), gradient)
        d_lower = against(value_all[:half], gradient)
        d_upper = against(value_all[half:], gradient)
        mean = jnp.sum(lower * d_lower, axis=0, keepdims=True) + jnp.sum(upper * d_upper, axis=0, keepdims=True)
        d_lower = (lower * (d_lower - mean)).astype(bf16)
        d_upper = (upper * (d_upper - mean)).astype(bf16)
        d_key[:half] += dot(d_lower, own)
        d_key[half:] += dot(d_upper, own)
        features = pl.ds(pl.multiple_of(h * HEAD_DIM, HEAD_DIM), HEAD_DIM)
        key = key_turned[features, :]
        d_query_turned[q_block, features, :] = (dot(key[:, :half], d_lower) + dot(key[:, half:], d_upper)) * (
            HEAD_DIM ** (-0.5)
        )
        return carry

    lax.fori_loop(0, blocks * (heads // HEAD_DIM), step, 0)
    send_ref[:, :heads] = d_key[:half].astype(bf16)
    send_ref[:, heads:] = d_value[:half].astype(bf16)
    own_ref[:, :heads] = d_key[half:]
    own_ref[:, heads:] = d_value[half:]
    for k in range(blocks):
        at = slice(k * QUERIES, (k + 1) * QUERIES)
        value = d_query_turned[k].T
        for j in range(heads // 128):
            lanes = slice(128 * j, 128 * (j + 1))
            d_query_ref[at, lanes] = turned_back(value[:, lanes], cosine[at, :], sine[at, :]).astype(bf16)


def project_back_body(
    back_ref, own_ref, d_query_ref, weight, cosine, sine, t0, t1, t2, t3, term_ref,
    mixed_ref, total_ref, sums_ref, bias_ref, p1, p2, p3,
):
    heads = d_query_ref.shape[1]
    rows = t0.shape[0]
    gain_sum = jnp.zeros((1, t0.shape[1]), f32)
    shift_sum = jnp.zeros((1, t0.shape[1]), f32)
    bias_sum = jnp.zeros((1, 3 * heads), f32)
    for k, (block, part) in enumerate(((t1, p1), (t2, p2), (t3, p3), (t0, total_ref)), 1):
        k = k % RING
        at = slice(k * rows, (k + 1) * rows)
        mixed_ref[at, :heads] = d_query_ref[at, :]
        for j in range(heads // 128):
            lanes = slice(128 * j, 128 * (j + 1))
            value = own_ref[at, lanes] + back_ref[at, lanes].astype(f32)
            mixed_ref[at, heads + 128 * j : heads + 128 * (j + 1)] = turned_back(
                value, cosine[at, :], sine[at, :]
            ).astype(bf16)
        mixed_ref[at, 2 * heads :] = (own_ref[at, heads:] + back_ref[at, heads:].astype(f32)).astype(bf16)
        mixed = mixed_ref[at, :]
        bias_sum += jnp.sum(mixed.astype(f32), axis=0, keepdims=True)
        gradient = against(mixed, weight[...])
        if k == 0:
            gradient = gradient + term_ref[...]
        part[...] = gradient.astype(part.dtype)
        unit, _ = normalize(block[...].astype(f32))
        gain_sum += jnp.sum(gradient * unit, axis=0, keepdims=True)
        shift_sum += jnp.sum(gradient, axis=0, keepdims=True)
    sums_ref[0:1, :] = gain_sum
    sums_ref[1:2, :] = shift_sum
    bias_ref[...] = bias_sum


def halves(core, part):
    half = part.shape[0] // 2
    first, second = part[:half], part[half:]
    return jnp.where(core == 0, first, second), jnp.where(core == 0, second, first)


def project_weight_body(core_ref, low_ref, mixed_ref, late_ref, mine_ref, theirs_ref):
    core = core_ref[0]
    lanes = mixed_ref.shape[1]
    for k in range(8):
        turned_low = low_ref[:, 128 * k : 128 * (k + 1)].T
        mine, theirs = halves(core, dot(turned_low, mixed_ref[...]))
        mine_ref[k, :, :lanes] = mine
        theirs_ref[k, :, :lanes] = theirs.astype(bf16)
        mine, theirs = halves(core, late_ref[k])
        for j in range(8):
            at = slice(8 * j, 8 * (j + 1))
            rows = slice(8 * (j // RING), 8 * (j // RING + 1))
            mine_ref[k, at, lanes:] = mine[rows]
            theirs_ref[k, at, lanes:] = theirs[rows].astype(bf16)


def assemble(core, target, mine, theirs):
    target[:, pl.ds(core, 1)] = mine[...][:, None]
    target[:, pl.ds(1 - core, 1)] = theirs[...][:, None]
    return target[...].reshape(-1, target.shape[-1])


def feed_body(
    scalars, n0, n1, n2, n3, g0, g1, g2, g3, up_mine, up_theirs, down_mine, down_theirs, up_bias, choice,
    router_in, router_out,
    f0, f1, f2, f3, d0, d1, d2, d3, dgate_ref, low_ref, d_up_ref, active_ref, d_ffn_ref, up_sum_ref,
    prob_ref, gate_ref, squash_ref, slice_ref, up_full, down_full,
):
    core, place = scalars[0], scalars[1]
    up = assemble(core, up_full, up_mine, up_theirs)
    down = assemble(core, down_full, down_mine, down_theirs)
    rows = n0.shape[0]
    units = up_bias.shape[1]
    router_slice = slice_ref.shape[1]
    up_sum = jnp.zeros((1, units), f32)
    for k, (normed, grad, ffn, d_normed) in enumerate(
        ((n1, g1, f1, d1), (n2, g2, f2, d2), (n3, g3, f3, d3), (n0, g0, f0, d0)), 1
    ):
        k = k % RING
        at = slice(k * rows, (k + 1) * rows)
        low = normed[...]
        low_ref[at, :] = low
        chosen = choice[at, :]
        upward = dot(low, up) + up_bias[...]
        quarter = lax.broadcasted_iota(jnp.int32, upward.shape, 1) // (units // CHOICES)
        active = jnp.where(quarter.astype(f32) <= chosen, jnp.maximum(upward, 0.0), 0.0)
        active_low = (active * active).astype(bf16)
        active_ref[at, :] = active_low
        squash = jnp.tanh(dot(low, router_in[...]))
        if k == 0:
            squash_ref[...] = squash
        logit = dot(squash.astype(bf16), router_out[...])
        expo = jnp.exp(logit - jnp.max(logit, axis=-1, keepdims=True))
        prob = expo / jnp.sum(expo, axis=-1, keepdims=True)
        option = lax.broadcasted_iota(jnp.int32, prob.shape, 1).astype(f32)
        gate = jnp.sum(jnp.where(option == chosen, prob, 0.0), axis=-1, keepdims=True)
        if k == 0:
            prob_ref[...] = prob
            gate_ref[...] = gate
        part = slice_of(squash, place, router_slice)
        slice_ref[at, :] = part
        ffn_part = dot(active_low, down)
        ffn[...] = ffn_part.astype(ffn.dtype)
        grad_out = grad[...].astype(f32)
        dgate = jnp.sum(grad_out * ffn_part, axis=-1, keepdims=True)
        dgate_ref[k] = jnp.broadcast_to(dgate, (rows, rows)).T[:1]
        d_ffn = (gate * grad_out).astype(bf16)
        d_ffn_ref[at, :] = d_ffn
        d_up = (against(d_ffn, down) * 2.0 * active).astype(bf16)
        d_up_ref[at, :] = d_up
        up_sum += jnp.sum(d_up.astype(f32), axis=0, keepdims=True)
        d_normed[...] = against(d_up, up).astype(d_normed.dtype)
    up_sum_ref[...] = up_sum


def slice_of(value, place, size):
    part = value[:, :size]
    for k in range(1, RING):
        part = jnp.where(place == k, value[:, k * size : (k + 1) * size], part)
    return part


def feed_weight_body(
    core_ref, low_ref, d_up_ref, active_ref, d_ffn_ref, p1, p2, p3, mine_ref, theirs_ref, f1, f2, f3
):
    core = core_ref[0]
    for ffn, part in ((f1, p1), (f2, p2), (f3, p3)):
        ffn[...] = part[...]
    for first, former, latter in ((0, low_ref, d_up_ref), (32, active_ref, d_ffn_ref)):
        for k in range(8):
            turned_former = former[:, 128 * k : 128 * (k + 1)].T
            mine, theirs = halves(core, dot(turned_former, latter[...]))
            for j in range(2):
                mine_ref[2 * k + j, first : first + 32, :] = mine[32 * j : 32 * (j + 1)]
                theirs_ref[2 * k + j, first : first + 32, :] = theirs[32 * j : 32 * (j + 1)].astype(bf16)


def mixer_weight_body(
    core_ref, low1, low2, width_slice, head_slice, d_logit, width_out, head_out, attended, g0, g1, g2, g3, early,
    mine_ref, theirs_ref, d_width, d_head, part_ref,
):
    core = core_ref[0]
    rows = g0.shape[0]
    size = width_slice.shape[1]
    logit = d_logit[...]
    squash = width_slice[...]
    d_width[...] = (against(logit[:, :CHOICES], width_out[...]) * (1.0 - squash * squash)).astype(bf16)
    squash = head_slice[...]
    d_head[...] = (against(logit[:, CHOICES:], head_out[...]) * (1.0 - squash * squash)).astype(bf16)
    for k in range(8):
        lanes = slice(128 * k, 128 * (k + 1))
        for first, former, latter in ((0, low2, d_width), (size, low1, d_head)):
            mine, theirs = halves(core, dot(former[:, lanes].T, latter[...]))
            for j in range(2):
                for half in range(2):
                    at = slice(32 * j + 16 * half, 32 * j + 16 * (half + 1))
                    to = slice(2 * size * half + first, 2 * size * half + first + size)
                    mine_ref[2 * k + j, 0:16, to] = mine[at]
                    theirs_ref[2 * k + j, 0:16, to] = theirs[at].astype(bf16)
    turned_out = attended[...].T
    part = dot(turned_out[:, :rows], g0[...])
    for k, block in ((1, g1), (2, g2), (3, g3)):
        part += dot(turned_out[:, k * rows : (k + 1) * rows], block[...])
    part_ref[...] = part
    for x in range(4):
        for yh in range(2):
            for yl in range(2):
                to = (x * 2 + yh) * 2 + yl
                base = 2 * yh * 64 + (4 * yl + x) * 8
                mine_ref[to, 16:24, :] = part_ref[pl.ds(pl.multiple_of(base + core * 64, 8), 8), :]
                theirs_ref[to, 16:24, :] = part_ref[pl.ds(pl.multiple_of(base + (1 - core) * 64, 8), 8), :].astype(bf16)
                at = (x * 2 + yh) * 4 + yl
                first = jnp.broadcast_to(early[at : at + 1, :], (8, early.shape[1]))
                second = jnp.broadcast_to(early[at + 2 : at + 3, :], (8, early.shape[1]))
                mine_ref[to, 24:32, :] = jnp.where(core == 0, first, second)
                theirs_ref[to, 24:32, :] = jnp.where(core == 0, second, first).astype(bf16)


def route_back(d_prob, prob):
    return (prob * (d_prob - jnp.sum(prob * d_prob, axis=-1, keepdims=True))).astype(bf16)


def two_parts(value):
    upper = value.astype(bf16)
    return upper, (value - upper.astype(f32)).astype(bf16)


def local(
    tokens,
    out_grad,
    qkv_weight,
    qkv_bias,
    out_weight,
    out_bias,
    up_weight,
    up_bias,
    down_weight,
    down_bias,
    attn_gain,
    attn_shift,
    ffn_gain,
    ffn_shift,
    head_router_in,
    head_router_out,
    width_router_in,
    width_router_out,
    head_choice,
    width_choice,
    seq_ids,
):
    rows, width = tokens.shape
    half_rows = RING * rows
    own_heads = HEADS // RING
    head_width = own_heads * HEAD_DIM
    units = up_weight.shape[1] // RING
    router_width = head_router_in.shape[1]
    router_slice = router_width // RING
    all_rows = rows * 128
    score_scale = HEAD_DIM ** (-0.5)
    core = lax.axis_index("c")
    upper_half = lax.axis_index("yl")
    place = lax.axis_index("z")

    options = jnp.arange(CHOICES)
    head_pick = (head_choice[:, None] == options[None, :]).astype(f32)
    width_pick = (width_choice[:, None] == options[None, :]).astype(f32)
    aux_factor = AUX_WEIGHT * CHOICES / all_rows

    qkv_piece = qkv_weight.reshape(8, 3, RING, head_width).transpose(2, 0, 1, 3).reshape(RING, 8, 3 * head_width)
    up_piece = up_weight.reshape(8, 32, RING, 32).transpose(2, 0, 1, 3).reshape(RING, 8, units)
    choice_rows = jnp.stack([head_choice, width_choice] + [jnp.zeros_like(head_choice)] * 6).astype(bf16)
    pieces = swap(
        jnp.concatenate(
            [qkv_piece, up_piece, jnp.broadcast_to(choice_rows[None], (RING, 8, rows))], axis=-1
        ),
        "z",
    )
    ring_order = (place - jnp.arange(RING)) % RING
    choices = jnp.take(pieces[:, :2, 3 * head_width + units :], ring_order, axis=0).astype(f32)
    head_half = choices[:, 0].reshape(half_rows, 1)
    width_half = choices[:, 1].reshape(half_rows, 1)
    pieces = pieces.reshape(8 * RING, -1)
    out_piece = lax.ppermute(out_weight, ("x", "z"), [(a * 4 + b, b * 4 + a) for a in range(4) for b in range(4)])

    token_blocks = ring_blocks(tokens)
    qkv_mine = spread(pieces[:, : 3 * head_width], CHIPS, 16)
    qkv_theirs = other_core(qkv_mine)

    inputs = tokens.astype(f32)
    grad_out = out_grad.astype(f32)
    unit1, inv1 = normalize(inputs)
    low1 = (unit1 * attn_gain + attn_shift).astype(bf16)
    own_qkv_bias = lax.dynamic_index_in_dim(qkv_bias.reshape(3, RING, head_width), place, 1, keepdims=False)
    one_sequence = (upper_half == 1) & (seq_ids[0] % 2 == 0)
    order = (ring_order[:, None] * rows + jnp.arange(rows)[None, :]).reshape(half_rows)
    cosine, sine = rotary_tables(order + jnp.where(one_sequence, half_rows, 0))
    core_scalar = core.astype(jnp.int32).reshape(1)
    flag = one_sequence.astype(jnp.int32).reshape(1)
    low1_half, query, kv_own, qkv_slice = call(
        project_body,
        [
            shaped((half_rows, width), bf16),
            shaped((half_rows, head_width), bf16),
            shaped((half_rows, 2 * head_width), bf16),
            shaped((8, 2, 64, 3 * head_width), bf16),
        ],
        [core_scalar] + token_blocks
        + [
            attn_gain.reshape(1, width), attn_shift.reshape(1, width),
            qkv_mine.reshape(8, 64, -1), qkv_theirs.reshape(8, 64, -1),
            own_qkv_bias.reshape(1, -1), cosine, sine,
        ],
        scalars=1,
        flops=2 * half_rows * width * 3 * head_width,
    )
    qkv_slice = qkv_slice.reshape(width, 3 * head_width)

    counts = jnp.concatenate(
        [jnp.sum((half == options[None, :]).astype(f32), axis=0) for half in (head_half, width_half)]
    )
    count_pairs = jnp.floor(counts / 2)
    count_lanes = jnp.concatenate([count_pairs, counts - 2 * count_pairs])[None].astype(bf16)
    count_rows = jnp.pad(count_lanes, ((0, 7), (0, width - 4 * CHOICES)))
    out_mine, out_theirs = spread_chips(tie(jnp.concatenate([out_piece, count_rows], axis=0), query))
    down_mine, down_theirs = spread_chips(tie(down_weight, out_mine))
    up_mine, up_theirs = spread_chips(tie(pieces[:, 3 * head_width : 3 * head_width + units], down_mine))
    out_all = both_cores(out_mine, out_theirs, core)
    out_slice = out_all[..., :8, :].transpose(1, 2, 3, 0, 4, 5).reshape(head_width, width)
    counts = jnp.sum((out_mine[:, 8, : 4 * CHOICES].astype(f32) + out_theirs[:, 8, : 4 * CHOICES].astype(f32)), axis=0)
    counts = 2 * counts[: 2 * CHOICES] + counts[2 * CHOICES :]
    head_share = counts[:CHOICES] / all_rows
    width_share = counts[CHOICES:] / all_rows

    kv_lower = lax.ppermute(kv_own, "yl", [(0, 1)])
    order_column = order.reshape(half_rows, 1)
    order_rows = order.reshape(half_rows // QUERIES, 1, QUERIES)
    head_keep = (head_half >= place).astype(f32)
    score_flops = 2 * half_rows * 2 * half_rows * head_width * own_heads
    attended, log_total = call(
        attend_body,
        [
            shaped((half_rows, head_width), bf16),
            shaped((own_heads * half_rows // QUERIES, 1, QUERIES), f32),
        ],
        [flag, query, kv_own, kv_lower, order_column, order_rows, head_keep],
        [
            pltpu.VMEM((2 * half_rows, head_width), bf16),
            pltpu.VMEM((head_width, 2 * half_rows), bf16),
            pltpu.VMEM((half_rows // QUERIES, head_width, QUERIES), f32),
        ],
        scalars=1,
        flops=2 * score_flops,
    )
    attn_pre = ring_product(attended, out_slice, dot, rows) + out_bias

    head_squash = jnp.tanh(dot(low1, head_router_in))
    head_squash_low = head_squash.astype(bf16)
    head_prob = jax.nn.softmax(dot(head_squash_low, head_router_out), axis=-1)
    head_gate = jnp.sum(head_prob * head_pick, axis=1, keepdims=True)
    middle = inputs + head_gate * attn_pre
    unit2, inv2 = normalize(middle)
    low2 = (unit2 * ffn_gain + ffn_shift).astype(bf16)

    grad_blocks = ring_blocks(out_grad)
    own_up_bias = lax.dynamic_index_in_dim(up_bias.reshape(32, RING, 32), place, 1, keepdims=False)
    scalars = jnp.stack([core.astype(jnp.int32), place.astype(jnp.int32)])
    own_shape, part_shape, half_shape = (
        shaped((rows, width), f32), shaped((rows, width), bf16), shaped((half_rows, width), bf16)
    )
    (
        ffn_pre, f1, f2, f3, d_normed2, d1, d2, d3, width_dgate_part, low2_half, d_up, active_low, d_ffn_half,
        d_up_sum, width_prob, width_gate, width_squash, width_slice,
    ) = call(
        feed_body,
        [own_shape] + [part_shape] * 3 + [own_shape] + [part_shape] * 3
        + [shaped((RING, 1, rows), f32), half_shape, shaped((half_rows, units), bf16)]
        + [shaped((half_rows, units), bf16), half_shape, shaped((1, units), f32)]
        + [shaped((rows, CHOICES), f32), shaped((rows, 1), f32), shaped((rows, router_width), f32)]
        + [shaped((half_rows, router_slice), f32)],
        [scalars] + ring_blocks(low2) + grad_blocks
        + [up_mine.reshape(8, 64, units), up_theirs.reshape(8, 64, units)]
        + [down_mine.reshape(8, 64, width), down_theirs.reshape(8, 64, width)]
        + [own_up_bias.reshape(1, units), width_half, width_router_in, width_router_out],
        [pltpu.VMEM((8, 2, 64, units), bf16), pltpu.VMEM((8, 2, 64, width), bf16)],
        scalars=1,
        flops=10 * half_rows * width * units,
        room=44,
    )
    width_dgate = width_dgate_part[0, 0] + jnp.sum(grad_out * down_bias, axis=1)
    received = []
    for k, part in ((1, d1), (2, d2), (3, d3)):
        received.append(to_sender(part, k))
        d_normed2 = d_normed2 + received[-1].astype(f32)
        width_dgate = width_dgate + to_sender(width_dgate_part[k], k)[0]
    width_dgate = width_dgate[:, None]
    feed_mine, feed_theirs, f1, f2, f3 = call(
        feed_weight_body,
        [shaped((16, 64, width), f32), shaped((16, 64, width), bf16)] + [part_shape] * 3,
        [core_scalar, low2_half, d_up, active_low, d_ffn_half, f1, f2, f3],
        scalars=1,
        flops=4 * half_rows * width * units,
        waits=received[:1],
    )
    feed_pieces = swap(pair_sum(feed_mine, feed_theirs).astype(bf16), CHIPS)
    ffn_pre = ffn_pre + down_bias
    for k, part in ((1, f1), (2, f2), (3, f3)):
        ffn_pre = ffn_pre + to_sender(part, k).astype(f32)
    result = (middle + width_gate * ffn_pre).astype(bf16)

    d_logit_width = route_back(width_pick * width_dgate + aux_factor * width_share[None, :], width_prob)
    width_out_grad = across(d_logit_width, width_squash.astype(bf16))
    d_hidden_width = (against(d_logit_width, width_router_out) * (1.0 - width_squash * width_squash)).astype(bf16)
    d_middle, ffn_gain_grad, ffn_shift_grad = normalize_back(
        d_normed2 + against(d_hidden_width, width_router_in), unit2, inv2, ffn_gain
    )
    d_middle = d_middle + grad_out

    head_dgate = jnp.sum(d_middle * attn_pre, axis=1, keepdims=True)
    d_attn = (head_gate * d_middle).astype(bf16)
    d_logit_head = route_back(head_pick * head_dgate + aux_factor * head_share[None, :], head_prob)
    head_out_grad = across(d_logit_head, head_squash_low)
    d_hidden_head = (against(d_logit_head, head_router_out) * (1.0 - head_squash * head_squash)).astype(bf16)
    router_term1 = against(d_hidden_head, head_router_in)
    d_attn_blocks = ring_blocks(d_attn)
    d_logit_half = jnp.concatenate(ring_blocks(jnp.concatenate([d_logit_width, d_logit_head], axis=1)), axis=0)
    own_columns = place * router_slice

    def columns(value):
        return lax.dynamic_slice_in_dim(value, own_columns, router_slice, 1)

    def out_rows(value):
        return lax.dynamic_slice_in_dim(value, own_columns, router_slice, 0)

    head_slice = jnp.tanh(dot(low1_half, columns(head_router_in)))
    own_place = (jnp.arange(RING) == place).astype(f32)
    d_up_sum = d_up_sum.reshape(32, 1, 32) * own_place[None, :, None]
    d_ffn = (width_gate * grad_out).astype(bf16)
    early = [
        jnp.sum(d_attn, axis=0, dtype=f32)[None],
        jnp.sum(d_ffn, axis=0, dtype=f32)[None],
        ffn_gain_grad[None],
        ffn_shift_grad[None],
        head_out_grad,
        width_out_grad,
        d_up_sum.reshape(RING, units),
        jnp.pad(
            jnp.concatenate([jnp.sum(head_prob, axis=0), jnp.sum(width_prob, axis=0)])[None],
            ((0, 15), (0, width - 2 * CHOICES)),
        ),
    ]
    mixer_mine, mixer_theirs = call(
        mixer_weight_body,
        [shaped((16, 32, width), f32), shaped((16, 32, width), bf16)],
        [core_scalar, low1_half, low2_half, width_slice, head_slice, d_logit_half]
        + [out_rows(width_router_out), out_rows(head_router_out), attended]
        + d_attn_blocks
        + [jnp.concatenate(early, axis=0)],
        [
            pltpu.VMEM((half_rows, router_slice), bf16),
            pltpu.VMEM((half_rows, router_slice), bf16),
            pltpu.VMEM((head_width, width), f32),
        ],
        scalars=1,
        flops=6 * half_rows * width * router_slice,
    )
    mixer_pieces = swap(tie(pair_sum(mixer_mine, mixer_theirs), feed_pieces).astype(bf16), CHIPS)

    d_query, d_lower, d_kv_own = call(
        attend_back_body,
        [
            shaped((half_rows, head_width), bf16),
            shaped((half_rows, 2 * head_width), bf16),
            shaped((half_rows, 2 * head_width), f32),
        ],
        [flag] + d_attn_blocks
        + [out_slice, query, kv_own, kv_lower, order_column, order_rows, head_keep, log_total, cosine, sine],
        [
            pltpu.VMEM((2 * half_rows, head_width), bf16),
            pltpu.VMEM((2 * half_rows, head_width), bf16),
            pltpu.VMEM((head_width, 2 * half_rows), bf16),
            pltpu.VMEM((half_rows, head_width), bf16),
            pltpu.VMEM((half_rows // QUERIES, head_width, QUERIES), f32),
            pltpu.VMEM((2 * half_rows, head_width), f32),
            pltpu.VMEM((2 * half_rows, head_width), f32),
        ],
        scalars=1,
        flops=5 * score_flops,
        room=28,
    )
    back = lax.ppermute(d_lower, "yl", [(1, 0)])
    d_mixed, d_own, gain_shift, d_mixed_sum, *d_sent = call(
        project_back_body,
        [
            shaped((half_rows, 3 * head_width), bf16),
            shaped((rows, width), f32),
            shaped((2, width), f32),
            shaped((1, 3 * head_width), f32),
        ]
        + [shaped((rows, width), bf16)] * 3,
        [back, d_kv_own, d_query, qkv_slice, cosine, sine] + token_blocks + [router_term1],
        flops=2 * half_rows * width * 3 * head_width,
    )

    feed_rows = block_sum(feed_pieces)
    down_grad = feed_rows[32:]
    mixer_rows = block_sum(mixer_pieces)
    out_grad_rows = lax.ppermute(
        mixer_rows[16:24], ("x", "z"), [(a * 4 + b, b * 4 + a) for a in range(4) for b in range(4)]
    )
    shared = jnp.concatenate([mixer_rows[:16], mixer_rows[24:]], axis=0).astype(bf16)
    up_rows = feed_rows[:32].reshape(RING, 8, units).astype(bf16)
    from_ring = []
    for shift in range(RING):
        rows_of = lax.dynamic_index_in_dim(up_rows, (place + shift) % RING, 0, keepdims=False)
        block = jnp.concatenate([shared, rows_of], axis=0)
        if shift:
            block = lax.ppermute(block, "z", [(k, (k + shift) % RING) for k in range(RING)])
        from_ring.append(block)
    from_ring = jnp.take(jnp.stack(from_ring), ring_order, axis=0)
    early_sum = jnp.sum(from_ring[:, 16:24].astype(f32), axis=0).astype(bf16)
    up_grad = from_ring[:, 24:].reshape(RING, 8, 32, 32).transpose(1, 2, 0, 3).reshape(8, RING * units).astype(f32)

    d_mixed_sum = d_mixed_sum.reshape(3, 1, head_width) * own_place[None, :, None]
    for k in range(1, RING):
        d_own = d_own + to_sender(d_sent[k - 1], k).astype(f32)
    d_inputs, _, _ = normalize_back(d_own, unit1, inv1, attn_gain)
    d_inputs = d_inputs + d_middle
    late = jnp.concatenate([d_mixed_sum.reshape(-1), gain_shift.reshape(-1)])
    late_size = late.shape[0] // 32
    late = jnp.pad(late.reshape(32, 1, late_size), ((0, 0), (0, 7), (0, 256 - late_size)))
    mine, theirs = call(
        project_weight_body,
        [shaped((8, 64, 3 * head_width + 256), f32), shaped((8, 64, 3 * head_width + 256), bf16)],
        [core_scalar, low1_half, d_mixed, late.reshape(8, 32, 256)],
        scalars=1,
        flops=2 * half_rows * width * 3 * head_width,
    )
    qkv_part = tie(pair_sum(mine, theirs), from_ring).astype(bf16)
    qkv_part = swap(qkv_part.reshape(64, 8, -1), CHIPS + ("z",))
    qkv_part = jnp.sum(qkv_part.reshape(16, RING, 8, -1).astype(f32), axis=0)
    qkv_grad = jnp.concatenate(
        [
            qkv_part[k, :, j * head_width : (j + 1) * head_width]
            for j in range(3)
            for k in range(RING)
        ],
        axis=1,
    )
    late = jnp.sum(qkv_part[:, :, 3 * head_width :], axis=0).astype(bf16)

    lanes = router_slice
    routers = jnp.concatenate(
        [
            jnp.concatenate([from_ring[k, :16, j * lanes : (j + 1) * lanes] for k in range(RING)], axis=1)
            for j in (0, 2, 1, 3)
        ]
        + [jnp.concatenate([early_sum[:1], jnp.pad(late[:1], ((0, 6), (0, width - 256)))], axis=0)],
        axis=0,
    )
    mine, theirs = spread_chips(routers)
    routers = both_cores(mine, theirs, core)
    width_in_grad = routers[..., :32, :].reshape(width, router_width).astype(f32)
    head_in_grad = routers[..., 32:64, :].reshape(width, router_width).astype(f32)
    summed = routers[..., 64, :].reshape(32, width).astype(f32)
    late = routers[..., 65, :late_size].reshape(-1).astype(f32)
    balance = CHOICES * (
        jnp.sum(head_share * summed[16, :CHOICES] / all_rows)
        + jnp.sum(width_share * summed[16, CHOICES : 2 * CHOICES] / all_rows)
    )
    return (
        result,
        balance,
        d_inputs,
        qkv_grad,
        out_grad_rows,
        up_grad,
        down_grad,
        late[: 3 * width],
        summed[0],
        summed[12:16].reshape(RING * units),
        summed[1],
        late[3 * width : 4 * width],
        late[4 * width :],
        summed[2],
        summed[3],
        head_in_grad,
        summed[4:8].T,
        width_in_grad,
        summed[8:12].T,
    )


def solution(mesh):
    fine = Mesh(mesh.devices.reshape(4, 2, 2, 2, 4), AXES)
    whole = P(AXES, None)
    vector = P(AXES)
    in_specs = (
        whole, whole, whole, P(), whole, P(), whole, P(), whole, P(),
        P(), P(), P(), P(), P(), P(), P(), P(), vector, vector, vector,
    )
    out_specs = (whole, P(), whole, whole, whole, whole, whole) + (P(),) * 12
    return jax.shard_map(local, mesh=fine, in_specs=in_specs, out_specs=out_specs, check_vma=False)
```

```python
import jax
import jax.numpy as jnp
import numpy as np
from jax import lax
from jax.experimental import pallas as pl
from jax.experimental.pallas import tpu as pltpu
from jax.sharding import Mesh
from jax.sharding import PartitionSpec as P


AXES = ("x", "yh", "c", "yl", "z")
CHIPS = ("x", "yh", "yl")
RING = 4
HEADS = 16
HEAD_DIM = 64
CHOICES = 4
EPS = 1e-05
AUX_WEIGHT = 0.1
BLOCKED = -1e30
bf16 = jnp.bfloat16
f32 = jnp.float32
INTERPRET = False
QUERIES = 256
LONG = 10**10


def dot(former, latter):
    return jnp.dot(former, latter, preferred_element_type=f32)


def against(former, latter):
    return lax.dot_general(former, latter, (((1,), (1,)), ((), ())), preferred_element_type=f32)


def across(former, latter):
    return lax.dot_general(former, latter, (((0,), (0,)), ((), ())), preferred_element_type=f32)


def swap(value, axes):
    return lax.all_to_all(value, axes, split_axis=0, concat_axis=0, tiled=True)


def spread(value, axes, count):
    return swap(jnp.broadcast_to(value[None], (count,) + value.shape), axes)


def other_core(value):
    return lax.ppermute(value, "c", [(0, 1), (1, 0)])


def ring_blocks(value):
    return [value] + [
        lax.ppermute(value, "z", [(k, (k + shift) % RING) for k in range(RING)]) for shift in range(1, RING)
    ]


def to_sender(value, shift):
    return lax.ppermute(value, "z", [(k, (k - shift) % RING) for k in range(RING)])


def ring_product(former, latter, product, rows):
    sent = [
        to_sender(product(former[k * rows : (k + 1) * rows], latter).astype(bf16), k) for k in range(1, RING)
    ]
    total = product(former[:rows], latter)
    for part in sent:
        total = total + part.astype(f32)
    return total


def spread_chips(value):
    mine = spread(value, CHIPS, 16)
    return mine, other_core(mine)


def block_sum(pieces):
    return jnp.sum(pieces.astype(f32), axis=0)


def normalize(values):
    centred = values - jnp.mean(values, axis=-1, keepdims=True)
    inv_std = lax.rsqrt(jnp.mean(centred * centred, axis=-1, keepdims=True) + EPS)
    return (centred * inv_std, inv_std)


def rotary_tables(position):
    lane = jnp.arange(2 * HEAD_DIM)
    half = HEAD_DIM // 2
    freqs = 10000.0 ** (-2.0 * (lane % half).astype(f32) / HEAD_DIM)
    angle = position.astype(f32)[:, None] * freqs[None, :]
    return (jnp.cos(angle), jnp.sin(angle) * jnp.where(lane % HEAD_DIM < half, -1.0, 1.0)[None, :])


def call(body, outs, args, scratch=(), scalars=0, cost=LONG, waits=(), room=24, windows=None, passes=(), near=()):
    outs = list(outs) + [shaped((8, 128), f32)]
    given, taken = len(args), len(args) + len(waits) + len(passes)

    def large(value):
        return int(np.prod(value.shape)) * value.dtype.itemsize >= 65536

    windows = windows or {}

    def shape_in(k):
        if k not in windows:
            return args[k].shape
        return tuple(part.stop - part.start for part in windows[k])

    copied_in = [k for k in range(scalars, given) if large(args[k]) and k not in near]
    copied_out = [k for k in range(len(outs)) if large(outs[k])]
    copies = len(copied_in) + len(copied_out)

    def whole(*refs):
        ins, results = list(refs[:given]), list(refs[taken : taken + len(outs)])
        rest = refs[taken + len(outs) + len(passes) :]
        semaphores, buffers, own = rest[0], rest[1 : 1 + copies], rest[1 + copies :]
        moves = []
        for j, k in enumerate(copied_in):
            source = ins[k].at[windows[k]] if k in windows else ins[k]
            move = pltpu.make_async_copy(source, buffers[j], semaphores.at[j])
            move.start()
            moves.append(move)
            ins[k] = buffers[j]
        for move in moves:
            move.wait()
        targets = list(results)
        for j, k in enumerate(copied_out, len(copied_in)):
            results[k] = buffers[j]
        body(*ins, *results[:-1], *own)
        results[-1][...] = jnp.zeros((8, 128), f32)
        moves = []
        for j, k in enumerate(copied_out, len(copied_in)):
            moves.append(pltpu.make_async_copy(buffers[j], targets[k], semaphores.at[j]))
            moves[-1].start()
        for move in moves:
            move.wait()

    def spec(k, copied):
        return pl.BlockSpec(memory_space=pltpu.HBM if k in copied else pltpu.VMEM)

    spaces = [pl.BlockSpec(memory_space=pltpu.SMEM)] * scalars
    spaces += [spec(k, copied_in) for k in range(scalars, given)]
    spaces += [pl.BlockSpec(memory_space=pl.ANY)] * (len(waits) + len(passes))
    buffers = [pltpu.VMEM(shape_in(k), args[k].dtype) for k in copied_in]
    buffers += [pltpu.VMEM(outs[k].shape, outs[k].dtype) for k in copied_out]
    moved = sum(int(np.prod(value.shape)) * value.dtype.itemsize for value in list(args) + list(outs))
    shapes = list(outs) + [shaped(value.shape, value.dtype) for value in passes]
    if not INTERPRET:
        shapes = [
            pltpu.HBM(v.shape, v.dtype) if k in copied_out or k >= len(outs) else v for k, v in enumerate(shapes)
        ]
        args = [pltpu.with_memory_space_constraint(v, pltpu.HBM) if k in copied_in else v for k, v in enumerate(args)]
        passes = [pltpu.with_memory_space_constraint(v, pltpu.HBM) for v in passes]
    results = pl.pallas_call(
        whole,
        out_shape=tuple(shapes),
        in_specs=spaces,
        out_specs=tuple(spec(k, copied_out) for k in range(len(outs)))
        + tuple(pl.BlockSpec(memory_space=pl.ANY) for _ in passes),
        scratch_shapes=[pltpu.SemaphoreType.DMA((max(copies, 1),))] + buffers + list(scratch),
        input_output_aliases={given + len(waits) + k: len(outs) + k for k in range(len(passes))},
        compiler_params=pltpu.CompilerParams(vmem_limit_bytes=room << 20),
        cost_estimate=pl.CostEstimate(flops=cost, bytes_accessed=moved if cost else 0, transcendentals=0),
        interpret=INTERPRET,
    )(*args, *waits, *passes)
    last = len(outs) - 1
    return (*results[:last], *results[last + 1 :], results[last])


def shaped(shape, kind):
    return jax.ShapeDtypeStruct(shape, kind)


def turned(value, cosine, sine):
    lane = lax.broadcasted_iota(jnp.int32, value.shape, 1)
    width = value.shape[1]
    half = HEAD_DIM // 2
    flipped = jnp.where(
        lane % HEAD_DIM < half, pltpu.roll(value, width - half, 1), pltpu.roll(value, half, 1)
    )
    return value * cosine + flipped * sine


def turned_back(value, cosine, sine):
    lane = lax.broadcasted_iota(jnp.int32, value.shape, 1)
    width = value.shape[1]
    half = HEAD_DIM // 2
    moved = value * sine
    flipped = jnp.where(
        lane % HEAD_DIM < half, pltpu.roll(moved, width - half, 1), pltpu.roll(moved, half, 1)
    )
    return value * cosine + flipped


def project_body(core_ref, t0, t1, t2, t3, gain, shift, mine, theirs, bias, cosine, sine, low_ref, query_ref, kv_ref, weight_ref):
    core = core_ref[0]
    weight_ref[:, pl.ds(core, 1)] = mine[...][:, None]
    weight_ref[:, pl.ds(1 - core, 1)] = theirs[...][:, None]
    weight = weight_ref[...].reshape(-1, weight_ref.shape[-1])
    rows = t0.shape[0]
    heads = query_ref.shape[1]
    for k, block in enumerate((t0, t1, t2, t3)):
        at = slice(k * rows, (k + 1) * rows)
        unit, _ = normalize(block[...].astype(f32))
        low = (unit * gain[...] + shift[...]).astype(bf16)
        low_ref[at, :] = low
        mixed = dot(low, weight) + bias[...]
        for j in range(heads // 128):
            lanes = slice(128 * j, 128 * (j + 1))
            query_ref[at, lanes] = turned(mixed[:, lanes], cosine[at, :], sine[at, :]).astype(bf16)
            key = mixed[:, heads + 128 * j : heads + 128 * (j + 1)]
            kv_ref[at, lanes] = turned(key, cosine[at, :], sine[at, :]).astype(bf16)
        kv_ref[at, heads:] = mixed[:, 2 * heads :].astype(bf16)


def kept_row(choice_ref, which, place, k):
    chosen = choice_ref[(place + RING - k) % RING, which : which + 1, :].astype(f32)
    return jnp.where(chosen >= place.astype(f32), 1.0, 0.0)


def column(row):
    return jnp.broadcast_to(row, (row.shape[1], row.shape[1])).T[:, :1]


def order_of(shape, axis, place, first=0):
    at = lax.broadcasted_iota(jnp.int32, shape, axis) + first
    return ((place + RING - at // 128) % RING) * 128 + at % 128


def own_part(h, query):
    lane = lax.broadcasted_iota(jnp.int32, query.shape, 1)
    return jnp.where(lane // HEAD_DIM == h, query, jnp.zeros_like(query)) * jnp.asarray(HEAD_DIM ** (-0.5), bf16)


def masked(score, own, flag, place, q_block):
    if not own:
        return jnp.where(flag, score, BLOCKED)
    keys = order_of((score.shape[0], 1), 0, place)
    return jnp.where(keys <= order_of((1, score.shape[1]), 1, place, q_block * QUERIES), score, BLOCKED)


def loop(heads, queries, step):
    blocks = queries // QUERIES

    def one(at, carry):
        h, q_block = at // blocks, at % blocks
        here = pl.ds(pl.multiple_of(q_block * QUERIES, QUERIES), QUERIES)
        features = pl.ds(pl.multiple_of(h * HEAD_DIM, HEAD_DIM), HEAD_DIM)
        step(at, h, q_block, here, features)
        return carry

    lax.fori_loop(0, blocks * (heads // HEAD_DIM), one, 0)


def attend_own_body(scalars, query_ref, kv_ref, top_ref, total_ref, out_ref, value_turned):
    heads = query_ref.shape[1]
    value_turned[...] = kv_ref[:, heads:].T
    flag, place = scalars[2] == 1, scalars[1]

    def step(at, h, q_block, here, features):
        score = against(kv_ref[:, :heads], own_part(h, query_ref[here, :]))
        score = masked(score, True, flag, place, q_block)
        top = jnp.max(score, axis=0, keepdims=True)
        expo = jnp.exp(score - top)
        top_ref[at] = top
        total_ref[at] = jnp.sum(expo, axis=0, keepdims=True)
        out_ref[q_block, features, :] = dot(value_turned[features, :], expo.astype(bf16))

    loop(heads, query_ref.shape[0], step)


def attend_body(
    scalars, query_ref, kv_ref, own_top, own_total, own_out, choice_ref, out_ref, total_ref, value_turned, out_turned,
):
    heads = query_ref.shape[1]
    value_turned[...] = kv_ref[:, heads:].T
    flag, place = scalars[2] == 1, scalars[1]

    def step(at, h, q_block, here, features):
        score = against(kv_ref[:, :heads], own_part(h, query_ref[here, :]))
        score = masked(score, False, flag, place, q_block)
        top = jnp.maximum(jnp.max(score, axis=0, keepdims=True), own_top[at])
        expo = jnp.exp(score - top)
        factor = jnp.exp(own_top[at] - top)
        total = jnp.sum(expo, axis=0, keepdims=True) + factor * own_total[at]
        total_ref[at] = top + jnp.log(total)
        out = dot(value_turned[features, :], expo.astype(bf16)) + factor * own_out[q_block, features, :]
        out_turned[q_block, features, :] = out / total

    loop(heads, query_ref.shape[0], step)
    for k in range(query_ref.shape[0] // QUERIES):
        at = slice(k * QUERIES, (k + 1) * QUERIES)
        keep = jnp.concatenate([kept_row(choice_ref, 0, place, 2 * k + j) for j in range(2)], axis=1)
        out_ref[at, :] = (out_turned[k] * keep).T.astype(bf16)


def back_step(own, scalars, query_ref, kv_ref, total_ref, d_out, mean_ref, key_turned, d_query_turned, d_key, d_value):
    heads = query_ref.shape[1]
    flag, place = scalars[2] == 1, scalars[1]

    def step(at, h, q_block, here, features):
        query = own_part(h, query_ref[here, :])
        score = masked(against(kv_ref[:, :heads], query), own, flag, place, q_block)
        prob = jnp.exp(score - total_ref[at])
        gradient = d_out[here, :]
        lane = lax.broadcasted_iota(jnp.int32, gradient.shape, 1)
        gradient = jnp.where(lane // HEAD_DIM == h, gradient, jnp.zeros_like(gradient))
        d_value[...] += dot(prob.astype(bf16), gradient)
        d_score = (prob * (against(kv_ref[:, heads:], gradient) - mean_ref[at])).astype(bf16)
        d_key[...] += dot(d_score, query)
        d_query = dot(key_turned[features, :], d_score) * (HEAD_DIM ** (-0.5))
        if own:
            d_query += d_query_turned[q_block, features, :]
        d_query_turned[q_block, features, :] = d_query

    return step


def attend_back_body(
    scalars, g0, g1, g2, g3, out_slice, query_ref, kv_ref, choice_ref, total_ref, attended,
    send_ref, d_out, mean_ref, d_query_turned, key_turned, d_key, d_value,
):
    heads = query_ref.shape[1]
    rows = query_ref.shape[0] // RING
    place = scalars[1]
    blocks = query_ref.shape[0] // QUERIES
    key_turned[...] = kv_ref[:, :heads].T
    d_key[...] = jnp.zeros_like(d_key)
    d_value[...] = jnp.zeros_like(d_value)
    for k, block in enumerate((g0, g1, g2, g3)):
        at = slice(k * rows, (k + 1) * rows)
        part = against(block[:rows, :], out_slice[...])
        d_out[at, :] = (part * column(kept_row(choice_ref, 0, place, k))).astype(bf16)
    for k in range(blocks):
        at = slice(k * QUERIES, (k + 1) * QUERIES)
        product = (d_out[at, :].astype(f32) * attended[at, :].astype(f32)).T
        for h in range(heads // HEAD_DIM):
            part = product[h * HEAD_DIM : (h + 1) * HEAD_DIM]
            mean_ref[h * blocks + k] = jnp.sum(part, axis=0, keepdims=True)
    loop(
        heads,
        query_ref.shape[0],
        back_step(
            False, scalars, query_ref, kv_ref, total_ref, d_out, mean_ref, key_turned, d_query_turned, d_key, d_value
        ),
    )
    send_ref[:, :heads] = d_key[...].astype(bf16)
    send_ref[:, heads:] = d_value[...].astype(bf16)


def attend_back_own_body(
    scalars, query_ref, kv_ref, total_ref, d_out, mean_ref, lower, cosine, sine,
    d_query_ref, own_ref, key_turned, d_query_turned, d_key, d_value,
):
    heads = query_ref.shape[1]
    key_turned[...] = kv_ref[:, :heads].T
    d_query_turned[...] = lower[...]
    d_key[...] = jnp.zeros_like(d_key)
    d_value[...] = jnp.zeros_like(d_value)
    loop(
        heads,
        query_ref.shape[0],
        back_step(
            True, scalars, query_ref, kv_ref, total_ref, d_out, mean_ref, key_turned, d_query_turned, d_key, d_value
        ),
    )
    own_ref[:, :heads] = d_key[...]
    own_ref[:, heads:] = d_value[...]
    for k in range(query_ref.shape[0] // QUERIES):
        at = slice(k * QUERIES, (k + 1) * QUERIES)
        value = d_query_turned[k].T
        for j in range(heads // 128):
            lanes = slice(128 * j, 128 * (j + 1))
            d_query_ref[at, lanes] = turned_back(value[:, lanes], cosine[at, :], sine[at, :]).astype(bf16)


def head_slice_body(scalars, low, router_in, slice_ref):
    size = slice_ref.shape[1]
    lanes = pl.ds(pl.multiple_of(scalars[1] * size, size), size)
    slice_ref[...] = jnp.tanh(dot(low[...], router_in[:, lanes]))


def project_back_body(
    back_ref, own_ref, d_query_ref, weight, cosine, sine, t0, t1, t2, t3, term_ref,
    mixed_ref, total_ref, sums_ref, bias_ref, p1, p2, p3,
):
    heads = d_query_ref.shape[1]
    rows = t0.shape[0]
    gain_sum = jnp.zeros((1, t0.shape[1]), f32)
    shift_sum = jnp.zeros((1, t0.shape[1]), f32)
    bias_sum = jnp.zeros((1, 3 * heads), f32)
    for k, (block, part) in enumerate(((t1, p1), (t2, p2), (t3, p3), (t0, total_ref)), 1):
        k = k % RING
        at = slice(k * rows, (k + 1) * rows)
        mixed_ref[at, :heads] = d_query_ref[at, :]
        for j in range(heads // 128):
            lanes = slice(128 * j, 128 * (j + 1))
            value = own_ref[at, lanes] + back_ref[at, lanes].astype(f32)
            mixed_ref[at, heads + 128 * j : heads + 128 * (j + 1)] = turned_back(
                value, cosine[at, :], sine[at, :]
            ).astype(bf16)
        mixed_ref[at, 2 * heads :] = (own_ref[at, heads:] + back_ref[at, heads:].astype(f32)).astype(bf16)
        mixed = mixed_ref[at, :]
        bias_sum += jnp.sum(mixed.astype(f32), axis=0, keepdims=True)
        gradient = against(mixed, weight[...])
        if k == 0:
            gradient = gradient + term_ref[...]
        part[...] = gradient.astype(part.dtype)
        unit, _ = normalize(block[...].astype(f32))
        gain_sum += jnp.sum(gradient * unit, axis=0, keepdims=True)
        shift_sum += jnp.sum(gradient, axis=0, keepdims=True)
    sums_ref[0:1, :] = gain_sum
    sums_ref[1:2, :] = shift_sum
    bias_ref[...] = bias_sum


def project_weight_body(scalars, low_ref, mixed_ref, bias_ref, sums_ref, mine_ref, theirs_ref):
    core, place = scalars[0], scalars[1]
    size = bias_ref.shape[1] // 3
    row = lax.broadcasted_iota(jnp.int32, (8, size), 0)
    late = [jnp.where(row == place, bias_ref[:, size * k : size * (k + 1)], 0.0) for k in range(3)]
    for k in range(2):
        block = jnp.zeros((8, size), f32)
        for j in range(RING):
            block = jnp.where(row == j, sums_ref[k : k + 1, size * j : size * (j + 1)], block)
        late.append(block)
    late += [jnp.zeros((8, size), f32)] * 3
    lanes = mixed_ref.shape[1]
    for k in range(8):
        turned_low = low_ref[:, 128 * k : 128 * (k + 1)].T
        mine, theirs = halves(core, dot(turned_low, mixed_ref[...]))
        mine_ref[k, :, :lanes] = mine.astype(bf16)
        theirs_ref[k, :, :lanes] = theirs.astype(bf16)
        for j in range(2):
            at = slice(32 * j, 32 * (j + 1))
            if k >= 2:
                mine_ref[k, at, lanes:] = jnp.zeros((32, size), bf16)
                theirs_ref[k, at, lanes:] = jnp.zeros((32, size), bf16)
                continue
            mine, theirs = halves(core, jnp.concatenate([late[4 * k + j], late[4 * k + 2 + j]], axis=0))
            mine_ref[k, at, lanes:] = jnp.concatenate([mine] * RING, axis=0).astype(bf16)
            theirs_ref[k, at, lanes:] = jnp.concatenate([theirs] * RING, axis=0).astype(bf16)


def halves(core, part):
    half = part.shape[0] // 2
    first, second = part[:half], part[half:]
    return jnp.where(core == 0, first, second), jnp.where(core == 0, second, first)


def assemble(core, target, mine, theirs):
    target[:, pl.ds(core, 1)] = mine[...][:, None]
    target[:, pl.ds(1 - core, 1)] = theirs[...][:, None]
    return target[...].reshape(-1, target.shape[-1])


def pack_body(qkv, up, head_choice, width_choice, packed_ref):
    heads = qkv.shape[1] // 3 // RING
    units = up.shape[1] // RING
    row = lax.broadcasted_iota(jnp.int32, (8, head_choice.shape[1]), 0)
    choices = jnp.where(
        row == 0, head_choice[...].astype(f32), jnp.where(row == 1, width_choice[...].astype(f32), 0.0)
    ).astype(bf16)
    for z in range(RING):
        for j in range(3):
            packed_ref[z, :, j * heads : (j + 1) * heads] = qkv[:, (j * RING + z) * heads : (j * RING + z + 1) * heads]
        packed_ref[z, :, 3 * heads : 3 * heads + units] = up[:, z * units : (z + 1) * units]
        packed_ref[z, :, 3 * heads + units :] = choices


def head_body(tokens, gain, shift, router_in, router_out, choice, squash_ref, prob_ref, gate_ref):
    unit, _ = normalize(tokens[...].astype(f32))
    low = (unit * gain[...] + shift[...]).astype(bf16)
    squash = jnp.tanh(dot(low, router_in[...]))
    squash_ref[...] = squash
    logit = dot(squash.astype(bf16), router_out[...])
    lane = lax.broadcasted_iota(jnp.int32, logit.shape, 1)
    logit = jnp.where(lane < CHOICES, logit, BLOCKED)
    expo = jnp.exp(logit - jnp.max(logit, axis=-1, keepdims=True))
    prob = expo / jnp.sum(expo, axis=-1, keepdims=True)
    prob_ref[...] = prob
    gate_ref[...] = jnp.sum(
        jnp.where(lane.astype(f32) == column(choice[...].astype(f32)), prob, 0.0), axis=-1, keepdims=True
    )


def mixer_body(pieces, out_rows, mixer_ref):
    size = mixer_ref.shape[2] // RING
    for k in range(mixer_ref.shape[0]):
        for j in range(RING):
            at = slice(8 * j, 8 * (j + 1))
            mixer_ref[k, at, : 3 * size] = pieces[j, :, : 3 * size]
            mixer_ref[k, at, 3 * size :] = out_rows[:, j * size : (j + 1) * size]


def count_body(choice_ref, pieces, down, rest_ref):
    lane = lax.broadcasted_iota(jnp.int32, (1, rest_ref.shape[2]), 1)
    line = jnp.zeros((1, rest_ref.shape[2]), f32)
    for which in range(2):
        chosen = choice_ref[:, which, :].astype(f32)
        for option in range(CHOICES):
            count = jnp.sum(jnp.where(chosen == option, 1.0, 0.0), axis=1, keepdims=True)
            count = jnp.sum(count, axis=0, keepdims=True)
            pairs = jnp.floor(count * 0.5)
            at = which * CHOICES + option
            line = jnp.where(lane == at, pairs, line)
            line = jnp.where(lane == at + 2 * CHOICES, count - 2.0 * pairs, line)
    last = jnp.broadcast_to(line, (8, rest_ref.shape[2])).astype(bf16)
    heads = (pieces.shape[2] - rest_ref.shape[2] - choice_ref.shape[2]) // 3
    for k in range(rest_ref.shape[0]):
        for j in range(RING):
            rest_ref[k, 8 * j : 8 * (j + 1)] = pieces[j, :, 3 * heads : 3 * heads + rest_ref.shape[2]]
        rest_ref[k, 32:64] = down[...]
        rest_ref[k, 64:] = last


def out_body(scalars, attended, mine, theirs, slice_ref, p0, p1, p2, p3, full):
    core = scalars[0]
    size = mine.shape[-1]
    for x in range(4):
        for yh in range(2):
            for yl in range(2):
                at = (x * 2 + yh) * 2 + yl
                for k in range(4):
                    rows, lanes = slice(8 * k, 8 * (k + 1)), slice(size * k, size * (k + 1))
                    full[yh, pl.ds(core, 1), yl, x, :, lanes] = mine[at : at + 1, rows].astype(f32)
                    full[yh, pl.ds(1 - core, 1), yl, x, :, lanes] = theirs[at : at + 1, rows].astype(f32)
    weight = full[...].reshape(slice_ref.shape).astype(bf16)
    slice_ref[...] = weight
    rows = p0.shape[0]
    for k, part in ((1, p1), (2, p2), (3, p3), (0, p0)):
        part[...] = dot(attended[k * rows : (k + 1) * rows, :], weight).astype(part.dtype)


def middle_body(p0, r1, r2, r3, tokens, bias, gate, gain, shift, attn_pre_ref, middle_ref, low_ref):
    total = p0[...]
    for part in (r1, r2, r3):
        total = total + part[...].astype(f32)
    total = total + bias[...]
    attn_pre_ref[...] = total
    middle = tokens[...].astype(f32) + gate[...] * total
    middle_ref[...] = middle
    unit, _ = normalize(middle)
    low_ref[...] = (unit * gain[...] + shift[...]).astype(bf16)


def slice_of(value, place, size):
    part = value[:, :size]
    for k in range(1, RING):
        part = jnp.where(place == k, value[:, k * size : (k + 1) * size], part)
    return part


def feed_body(
    scalars, n0, n1, n2, n3, up_mine, up_theirs, up_bias, router_in, router_out, down_mine, down_theirs,
    g0, g1, g2, g3, choice_ref,
    f0, f1, f2, f3, d0, d1, d2, d3, dgate_ref, low_ref, d_up_ref, active_ref, d_ffn_ref, up_sum_ref,
    prob_ref, gate_ref, squash_ref, slice_ref, up_full, down_full,
):
    core, place = scalars[0], scalars[1]
    up = assemble(core, up_full, up_mine, up_theirs)
    for x in range(4):
        for yh in range(2):
            for yl in range(2):
                down_full[yh, pl.ds(core, 1), yl, x] = down_mine[2 * x + yh, yl : yl + 1]
                down_full[yh, pl.ds(1 - core, 1), yl, x] = down_theirs[2 * x + yh, yl : yl + 1]
    down = down_full[...].reshape(-1, down_full.shape[-1])
    rows = n0.shape[0]
    units = up_bias.shape[1]
    router_slice = slice_ref.shape[1]
    up_sum = jnp.zeros((1, units), f32)
    for blocks in (((1, n1, g1, f1, d1), (2, n2, g2, f2, d2)), ((3, n3, g3, f3, d3), (0, n0, g0, f0, d0))):
        low = jnp.concatenate([block[1][...] for block in blocks], axis=0)
        keep_row = [kept_row(choice_ref, 1, place, block[0]) for block in blocks]
        keep = jnp.concatenate([column(row) for row in keep_row], axis=0)
        chosen = jnp.concatenate(
            [column(choice_ref[(place + RING - block[0]) % RING, 1:2, :].astype(f32)) for block in blocks], axis=0
        )
        upward = dot(low, up) + up_bias[...]
        active = jnp.maximum(upward, 0.0) * keep
        active_low = (active * active).astype(bf16)
        squash = jnp.tanh(dot(low, router_in[...]))
        logit = dot(squash.astype(bf16), router_out[...])
        lane = lax.broadcasted_iota(jnp.int32, logit.shape, 1)
        logit = jnp.where(lane // CHOICES == 1, logit, BLOCKED)
        expo = jnp.exp(logit - jnp.max(logit, axis=-1, keepdims=True))
        prob = expo / jnp.sum(expo, axis=-1, keepdims=True)
        gate = jnp.sum(jnp.where((lane - CHOICES).astype(f32) == chosen, prob, 0.0), axis=-1, keepdims=True)
        part = slice_of(squash, place, router_slice)
        ffn_part = dot(active_low, down)
        grad_out = jnp.concatenate([block[2][...] for block in blocks], axis=0).astype(f32)
        dgate = jnp.sum(grad_out * ffn_part, axis=-1, keepdims=True)
        d_ffn = (gate * grad_out).astype(bf16)
        d_up = (against(d_ffn, down) * 2.0 * active).astype(bf16)
        up_sum += jnp.sum(d_up.astype(f32), axis=0, keepdims=True)
        d_normed = against(d_up, up)
        for j, (k, _, _, ffn, d_block) in enumerate(blocks):
            at, here = slice(k * rows, (k + 1) * rows), slice(j * rows, (j + 1) * rows)
            low_ref[at, :] = low[here]
            active_ref[at, :] = active_low[here]
            slice_ref[at, :] = part[here]
            d_ffn_ref[at, :] = d_ffn[here]
            d_up_ref[at, :] = d_up[here]
            ffn[...] = ffn_part[here].astype(ffn.dtype)
            d_block[:rows, :] = d_normed[here].astype(d_block.dtype)
            line = jnp.broadcast_to(dgate[here], (rows, rows)).T[:1]
            if k == 0:
                dgate_ref[...] = line
                squash_ref[...] = squash[here]
                prob_ref[...] = prob[here]
                gate_ref[...] = gate[here]
            else:
                upper = line.astype(bf16).astype(f32)
                row = lax.broadcasted_iota(jnp.int32, (8, rows), 0)
                lines = jnp.where(row == 0, upper, jnp.where(row == 1, line - upper, 0.0)).astype(bf16)
                d_block[rows:, :] = jnp.concatenate([lines] * (units // rows), axis=1)
    up_sum_ref[...] = up_sum


def feed_weight_body(
    core_ref, low_ref, d_up_ref, active_ref, d_ffn_ref, p1, p2, p3, mine_ref, theirs_ref, f1, f2, f3
):
    core = core_ref[0]
    for ffn, part in ((f1, p1), (f2, p2), (f3, p3)):
        ffn[...] = part[...]
    for k in range(8):
        turned_low = low_ref[:, 128 * k : 128 * (k + 1)].T
        mine, theirs = halves(core, dot(turned_low, d_up_ref[...]))
        for j in range(2):
            mine_ref[2 * k + j, :32, :] = mine[32 * j : 32 * (j + 1)].astype(bf16)
            theirs_ref[2 * k + j, :32, :] = theirs[32 * j : 32 * (j + 1)].astype(bf16)
    for yh in range(2):
        for yl in range(2):
            for target, side in ((mine_ref, core), (theirs_ref, 1 - core)):
                lanes = pl.ds(pl.multiple_of(((yh * 2 + side) * 2 + yl) * 128, 128), 128)
                part = dot(active_ref[:, lanes].T, d_ffn_ref[...]).astype(bf16)
                for x in range(4):
                    target[(x * 2 + yh) * 2 + yl, 32:, :] = part[32 * x : 32 * (x + 1)]


def pair_body(mine, theirs, sum_ref):
    sum_ref[...] = (mine[...].astype(f32) + theirs[...].astype(f32)).astype(bf16)


def nothing(*refs):
    pass


def own_back_body(
    scalars, d0, r1, r2, r3, middle_ref, router_in, grad_ref, squash_ref, head_squash_ref, attn_pre_ref,
    dgate_ref, down_bias, prob_ref, gate_ref, head_prob_ref, head_gate_ref, head_choice, width_choice,
    counts_mine, counts_theirs, width_out, head_out, gain, up_sum,
    payload_ref, d_middle_ref, d_hidden_ref, early_ref, share_ref,
):
    place = scalars[1]
    rows = grad_ref.shape[0]
    units = up_sum.shape[1]
    aux = AUX_WEIGHT * CHOICES / (128.0 * rows)
    grad_out = grad_ref[...].astype(f32)
    d_normed = d0[...]
    line = dgate_ref[...]
    for part in (r1, r2, r3):
        d_normed = d_normed + part[:rows, :].astype(f32)
        lines = part[rows:, :rows].astype(f32)
        line = line + lines[:1] + lines[1:2]
    dgate = column(line) + jnp.sum(grad_out * down_bias[...], axis=-1, keepdims=True)
    pairs = jnp.sum(counts_mine[...].astype(f32) + counts_theirs[...].astype(f32), axis=0)[:1]
    share = (2.0 * pairs + pltpu.roll(pairs, 128 - 2 * CHOICES, 1)) / (128.0 * rows)
    share_ref[...] = share
    at = lax.broadcasted_iota(jnp.int32, share.shape, 1)
    lane = lax.broadcasted_iota(jnp.int32, prob_ref.shape, 1).astype(f32)

    def d_logits(which, prob, choice, dgate):
        picked = jnp.where(lane - which * CHOICES == column(choice[...].astype(f32)), dgate, 0.0)
        d_prob = picked + aux * jnp.where(at // CHOICES == which, share, 0.0)
        return prob * (d_prob - jnp.sum(prob * d_prob, axis=-1, keepdims=True))

    d_width = d_logits(1, prob_ref[...], width_choice, dgate)
    squash = squash_ref[...]
    d_hidden = (against(d_width.astype(bf16), width_out[...]) * (1.0 - squash * squash)).astype(bf16)
    d_normed = d_normed + against(d_hidden, router_in[...])
    unit, inv_std = normalize(middle_ref[...])
    scaled = d_normed * gain[...]
    inner = (
        scaled
        - jnp.mean(scaled, axis=-1, keepdims=True)
        - unit * jnp.mean(scaled * unit, axis=-1, keepdims=True)
    )
    d_middle = inner * inv_std + grad_out
    d_middle_ref[...] = d_middle
    head_dgate = jnp.sum(d_middle * attn_pre_ref[...], axis=-1, keepdims=True)
    d_attn = (head_gate_ref[...] * d_middle).astype(bf16)
    payload_ref[:rows, :] = d_attn
    d_head = d_logits(0, head_prob_ref[...], head_choice, head_dgate)
    head_squash = head_squash_ref[...]
    d_hidden_ref[...] = (against(d_head.astype(bf16), head_out[...]) * (1.0 - head_squash * head_squash)).astype(bf16)
    d_logit = (d_head + d_width).T[:8].astype(bf16)
    payload_ref[rows:, :] = jnp.concatenate([d_logit] * (units // rows), axis=1)
    row = lax.broadcasted_iota(jnp.int32, (8, units), 0)
    d_ffn = (gate_ref[...] * grad_out).astype(bf16).astype(f32)
    vectors = (
        jnp.sum(d_attn.astype(f32), axis=0, keepdims=True),
        jnp.sum(d_ffn, axis=0, keepdims=True),
        jnp.sum(d_normed * unit, axis=0, keepdims=True),
        jnp.sum(d_normed, axis=0, keepdims=True),
    )
    first = dot(d_logit, head_squash.astype(bf16))
    second = dot(d_logit, squash.astype(bf16))
    block = jnp.where(row < CHOICES, first, second)
    early_ref[0:8, :] = block
    block = jnp.zeros((8, units), f32)
    for k, vector in enumerate(vectors):
        block = jnp.where(row == k, vector, block)
    for k in range(RING):
        block = jnp.where(row == RING + k, jnp.where(place == k, up_sum[...], 0.0), block)
    early_ref[8:16, :] = block
    probs = jnp.sum(head_prob_ref[...] + prob_ref[...], axis=0, keepdims=True)
    early_ref[16:24, :] = jnp.broadcast_to(jnp.concatenate([probs] * (units // 128), axis=1), (8, units))
    early_ref[24:32, :] = jnp.zeros((8, units), f32)


def mixer_weight_body(
    scalars, low1, low2, width_slice, head_slice, width_out, head_out, attended, g0, g1, g2, g3, early,
    mine_ref, theirs_ref, d_width, d_head, part_ref, logit_ref,
):
    core, place = scalars[0], scalars[1]
    rows = attended.shape[0] // RING
    size = width_slice.shape[1]
    here = pl.ds(pl.multiple_of(place * size, size), size)
    logit_ref[...] = jnp.zeros_like(logit_ref)
    for k, block in enumerate((g0, g1, g2, g3)):
        at = slice(k * rows, (k + 1) * rows)
        logit_ref[:8, :] = block[rows:, :rows].astype(f32)
        logit = logit_ref[...].T.astype(bf16)
        for target, weight, slices in ((d_width, width_out, width_slice), (d_head, head_out, head_slice)):
            squash = slices[at, :]
            target[at, :] = (against(logit, weight[here, :]) * (1.0 - squash * squash)).astype(bf16)
    for k in range(8):
        lanes = slice(128 * k, 128 * (k + 1))
        for first, former, latter in ((0, low2, d_width), (size, low1, d_head)):
            mine, theirs = halves(core, dot(former[:, lanes].T, latter[...]))
            for j in range(2):
                for half in range(2):
                    at = slice(32 * j + 16 * half, 32 * j + 16 * (half + 1))
                    to = slice(2 * size * half + first, 2 * size * half + first + size)
                    mine_ref[2 * k + j, 0:16, to] = mine[at].astype(bf16)
                    theirs_ref[2 * k + j, 0:16, to] = theirs[at].astype(bf16)
    turned_out = attended[...].T
    part = dot(turned_out[:, :rows], g0[:rows, :])
    for k, block in ((1, g1), (2, g2), (3, g3)):
        part += dot(turned_out[:, k * rows : (k + 1) * rows], block[:rows, :])
    part_ref[...] = part
    for x in range(4):
        for yh in range(2):
            for yl in range(2):
                to = (x * 2 + yh) * 2 + yl
                base = 2 * yh * 64 + (4 * yl + x) * 8
                at = (x * 2 + yh) * 4 + yl
                first = jnp.broadcast_to(early[at : at + 1, :], (8, early.shape[1]))
                second = jnp.broadcast_to(early[at + 2 : at + 3, :], (8, early.shape[1]))
                for target, side in ((mine_ref, core), (theirs_ref, 1 - core)):
                    out = part_ref[pl.ds(pl.multiple_of(base + side * 64, 8), 8), :]
                    vector = jnp.where(side == 0, first, second)
                    target[to, 16:32, :] = jnp.concatenate([out, vector], axis=0).astype(bf16)


def mixer_sum_body(pieces, shared_ref, out_ref):
    rows = jnp.sum(pieces[...].astype(f32), axis=0)
    shared_ref[:16, :] = rows[:16].astype(bf16)
    shared_ref[16:, :] = rows[24:].astype(bf16)
    out_ref[...] = rows[16:24]


def project_sum_body(pieces, grad_ref, late_ref):
    late = jnp.zeros((8, late_ref.shape[1] // RING), f32)
    heads = grad_ref.shape[1] // 3 // RING
    for z in range(RING):
        part = pieces[z].astype(f32)
        for k in range(1, 16):
            part = part + pieces[k * RING + z].astype(f32)
        for j in range(3):
            grad_ref[:, (j * RING + z) * heads : (j * RING + z + 1) * heads] = part[:, j * heads : (j + 1) * heads]
        late = late + part[:, 3 * heads :]
    late_ref[...] = jnp.concatenate([late[k : k + 1] for k in range(RING)], axis=1)


def routers_body(
    core_ref, mine, theirs, width_ref, head_ref, qkv_ref, out_ref, up_ref, down_ref, attn_gain_ref, attn_shift_ref,
    ffn_gain_ref, ffn_shift_ref, head_out_ref, width_out_ref, prob_ref, full,
):
    core = core_ref[0]
    rows = width_ref.shape[0] // 32
    for j in range(16):
        x_yh, yl = j // 2, j % 2
        for source, side in ((mine, core), (theirs, 1 - core)):
            at = pl.multiple_of(((x_yh * 2 + side) * 2 + yl) * rows, rows)
            width_ref[pl.ds(at, rows), :] = source[j, :rows, :].astype(f32)
            head_ref[pl.ds(at, rows), :] = source[j, rows : 2 * rows, :].astype(f32)
            full[x_yh, pl.ds(side, 1), yl] = source[j, 2 * rows :, :].astype(f32)[None]

    def vector(at, late=0):
        return full[at // 4, at // 2 % 2, at % 2, late : late + 1, :]

    size = full.shape[-1]
    for k in range(3):
        qkv_ref[:, k * size : (k + 1) * size] = vector(k, 4)
    attn_gain_ref[...] = vector(3, 4)
    attn_shift_ref[...] = vector(4, 4)
    out_ref[...] = vector(8)
    down_ref[...] = vector(9)
    ffn_gain_ref[...] = vector(10)
    ffn_shift_ref[...] = vector(11)
    for k in range(RING):
        up_ref[:, k * size : (k + 1) * size] = vector(12 + k)
    prob_ref[...] = vector(16)[:, :128]
    options = jnp.concatenate([vector(k) for k in range(8)], axis=0).T
    head_out_ref[...] = options[:, :CHOICES]
    width_out_ref[...] = options[:, CHOICES:]


def inputs_body(d_own, r1, r2, r3, tokens, d_middle, gain, d_inputs_ref):
    gradient = d_own[...]
    for part in (r1, r2, r3):
        gradient = gradient + part[...].astype(f32)
    unit, inv_std = normalize(tokens[...].astype(f32))
    scaled = gradient * gain[...]
    inner = (
        scaled
        - jnp.mean(scaled, axis=-1, keepdims=True)
        - unit * jnp.mean(scaled * unit, axis=-1, keepdims=True)
    )
    d_inputs_ref[...] = inner * inv_std + d_middle[...]


def local(
    tokens,
    out_grad,
    qkv_weight,
    qkv_bias,
    out_weight,
    out_bias,
    up_weight,
    up_bias,
    down_weight,
    down_bias,
    attn_gain,
    attn_shift,
    ffn_gain,
    ffn_shift,
    head_router_in,
    head_router_out,
    width_router_in,
    width_router_out,
    head_choice,
    width_choice,
    seq_ids,
):
    rows, width = tokens.shape
    half_rows = RING * rows
    own_heads = HEADS // RING
    head_width = own_heads * HEAD_DIM
    units = up_weight.shape[1] // RING
    router_width = head_router_in.shape[1]
    router_slice = router_width // RING
    all_rows = rows * 128
    core = lax.axis_index("c").astype(jnp.int32)
    place = lax.axis_index("z").astype(jnp.int32)
    one_sequence = (lax.axis_index("yl") == 1) & (seq_ids[0] % 2 == 0)
    core_scalar = core.reshape(1)
    scalars = jnp.stack([core, place, one_sequence.astype(jnp.int32)])
    flipped = [(a * 4 + b, b * 4 + a) for a in range(4) for b in range(4)]
    own_shape = shaped((rows, width), f32)
    part_shape = shaped((rows, width), bf16)
    half_shape = shaped((half_rows, width), bf16)
    sent_shape = shaped((rows + 8, width), bf16)

    def line(vector):
        return vector.reshape(1, -1)

    out_swapped = lax.ppermute(out_weight, ("x", "z"), flipped)
    down_swapped = lax.ppermute(down_weight, ("x", "z"), flipped)
    packed, _ = call(
        pack_body,
        [shaped((RING, 8, 3 * head_width + units + rows), bf16)],
        [qkv_weight, up_weight, line(head_choice), line(width_choice)],
        room=16,
    )
    ring_order = (place - jnp.arange(RING)) % RING
    order = (ring_order[:, None] * rows + jnp.arange(rows)[None, :]).reshape(half_rows)
    cosine, sine = rotary_tables(order + jnp.where(one_sequence, half_rows, 0))
    head_out = jnp.pad(head_router_out, ((0, 0), (0, 128 - CHOICES)))
    width_out = jnp.pad(width_router_out, ((0, 0), (CHOICES, 128 - 2 * CHOICES)))
    own_up_bias = lax.dynamic_index_in_dim(up_bias.reshape(RING, units), place, 0, keepdims=True)
    own_qkv_bias = lax.dynamic_index_in_dim(qkv_bias.reshape(3, RING, head_width), place, 1, keepdims=False)
    head_squash, head_prob, head_gate, head_done = call(
        head_body,
        [own_shape, shaped((rows, 128), f32), shaped((rows, 1), f32)],
        [tokens, line(attn_gain), line(attn_shift), head_router_in, head_out, line(head_choice)],
        waits=[cosine, width_out, own_up_bias, own_qkv_bias],
    )

    pieces = swap(packed, "z")
    choices = pieces[:, :, 3 * head_width + units :]
    token_blocks = ring_blocks(tokens)
    mixer_all, _ = call(
        mixer_body,
        [shaped((16, 32, width), bf16)],
        [pieces, out_swapped],
        waits=[head_done] + token_blocks[1:],
        room=16,
    )
    mixer_mine = swap(mixer_all, CHIPS)
    mixer_theirs = other_core(mixer_mine)
    rest_all, _ = call(
        count_body,
        [shaped((16, 72, width), bf16)],
        [choices, pieces, down_swapped],
        room=16,
        waits=[mixer_mine],
    )

    qkv_lanes = (slice(0, 8), slice(0, 64), slice(0, 3 * head_width))
    low1_half, query, kv_own, qkv_slice, _ = call(
        project_body,
        [
            half_shape,
            shaped((half_rows, head_width), bf16),
            shaped((half_rows, 2 * head_width), bf16),
            shaped((8, 2, 64, 3 * head_width), bf16),
        ],
        [core_scalar] + token_blocks
        + [
            line(attn_gain), line(attn_shift),
            mixer_mine.reshape(8, 64, -1), mixer_theirs.reshape(8, 64, -1),
            line(own_qkv_bias), cosine, sine,
        ],
        scalars=1,
        windows={7: qkv_lanes, 8: qkv_lanes},
    )
    qkv_slice = qkv_slice.reshape(width, 3 * head_width)
    kv_lower = lax.ppermute(kv_own, "yl", [(0, 1)])
    lines = shaped((own_heads * half_rows // QUERIES, 1, QUERIES), f32)
    turned_shape = shaped((half_rows // QUERIES, head_width, QUERIES), f32)
    own_top, own_total, own_out, own_done = call(
        attend_own_body,
        [lines, lines, turned_shape],
        [scalars, query, kv_own],
        [pltpu.VMEM((head_width, half_rows), bf16)],
        scalars=1,
    )
    head_slice, head_slice_done = call(
        head_slice_body,
        [shaped((half_rows, router_slice), f32)],
        [scalars, low1_half, head_router_in],
        scalars=1,
    )
    rest_all, _ = call(nothing, [], [], waits=[kv_lower, own_done, head_slice_done], passes=[rest_all])
    rest_mine = swap(rest_all, CHIPS)
    grad_blocks = ring_blocks(out_grad)
    attended, log_total, _ = call(
        attend_body,
        [
            shaped((half_rows, head_width), bf16),
            shaped((own_heads * half_rows // QUERIES, 1, QUERIES), f32),
        ],
        [scalars, query, kv_lower, own_top, own_total, own_out, choices],
        [
            pltpu.VMEM((head_width, half_rows), bf16),
            pltpu.VMEM((half_rows // QUERIES, head_width, QUERIES), f32),
        ],
        scalars=1,
        waits=grad_blocks[1:],
    )
    out_lanes = (slice(0, 16), slice(0, 32), slice(3 * head_width, 4 * head_width))
    out_slice, p0, p1, p2, p3, _ = call(
        out_body,
        [shaped((head_width, width), bf16), own_shape] + [part_shape] * 3,
        [scalars, attended, mixer_mine, mixer_theirs],
        [pltpu.VMEM((2, 2, 2, 4, 8, width), f32)],
        scalars=1,
        windows={2: out_lanes, 3: out_lanes},
    )
    attn_pre, middle, low2, rest_mine, _ = call(
        middle_body,
        [own_shape, own_shape, part_shape],
        [p0] + [to_sender(part, k) for k, part in ((1, p1), (2, p2), (3, p3))]
        + [tokens, line(out_bias), head_gate, line(ffn_gain), line(ffn_shift)],
        passes=[rest_mine],
    )
    rest_theirs = other_core(rest_mine)

    up_rows, down_rows = (
        (slice(0, 8), slice(0, 2), slice(*at), slice(0, size))
        for at, size in (((0, 32), width), ((32, 64), width))
    )
    count_rows = (slice(0, 16), slice(64, 72), slice(0, 128))
    rest_mine = rest_mine.reshape(8, 2, 72, width)
    rest_theirs = rest_theirs.reshape(8, 2, 72, width)
    (
        ffn_pre, f1, f2, f3, d_normed2, d1, d2, d3, width_dgate, low2_half, d_up, active_low, d_ffn_half,
        d_up_sum, width_prob, width_gate, width_squash, width_slice, _,
    ) = call(
        feed_body,
        [own_shape] + [part_shape] * 3 + [own_shape] + [sent_shape] * 3
        + [shaped((1, rows), f32), half_shape, shaped((half_rows, units), bf16)]
        + [shaped((half_rows, units), bf16), half_shape, shaped((1, units), f32)]
        + [shaped((rows, 128), f32), shaped((rows, 1), f32), shaped((rows, router_width), f32)]
        + [shaped((half_rows, router_slice), f32)],
        [scalars] + ring_blocks(low2)
        + [rest_mine, rest_theirs, own_up_bias]
        + [width_router_in, width_out]
        + [rest_mine, rest_theirs]
        + grad_blocks + [choices],
        [pltpu.VMEM((8, 2, 2, 32, units), bf16), pltpu.VMEM((2, 2, 2, 4, 32, width), bf16)],
        scalars=1,
        room=48,
        windows={5: up_rows, 6: up_rows, 10: down_rows, 11: down_rows},
    )
    d_received = [to_sender(part, k) for k, part in ((1, d1), (2, d2), (3, d3))]
    payload, d_middle, d_hidden_head, early, share, payload_done = call(
        own_back_body,
        [sent_shape, own_shape, part_shape, shaped((32, width), f32), shaped((1, 128), f32)],
        [scalars, d_normed2] + d_received
        + [middle, width_router_in, out_grad, width_squash, head_squash, attn_pre]
        + [width_dgate, line(down_bias), width_prob, width_gate, head_prob, head_gate]
        + [line(head_choice), line(width_choice), rest_mine.reshape(16, 72, width), rest_theirs.reshape(16, 72, width)]
        + [width_out, head_out, line(ffn_gain), d_up_sum],
        scalars=1,
        windows={19: count_rows, 20: count_rows},
    )
    router_term1 = against(d_hidden_head, head_router_in)

    d_attn_blocks = ring_blocks(payload)
    feed_mine, feed_theirs, f1, f2, f3, _ = call(
        feed_weight_body,
        [shaped((16, 64, width), bf16)] * 2 + [part_shape] * 3,
        [core_scalar, low2_half, d_up, active_low, d_ffn_half, f1, f2, f3],
        scalars=1,
        waits=[payload_done],
    )
    feed_part, feed_done = call(pair_body, [shaped((16, 64, width), bf16)], [feed_mine, other_core(feed_theirs)], cost=0, near=[1])
    feed_pieces = swap(feed_part, CHIPS)
    f_received = [to_sender(part, k) for k, part in ((1, f1), (2, f2), (3, f3))]
    ffn_pre = ffn_pre + down_bias
    for part in f_received:
        ffn_pre = ffn_pre + part.astype(f32)
    result = (middle + width_gate * ffn_pre).astype(bf16)
    mixed_mine, mixed_theirs, mixed_done = call(
        mixer_weight_body,
        [shaped((16, 32, width), bf16)] * 2,
        [scalars, low1_half, low2_half, width_slice, head_slice, width_out, head_out, attended]
        + d_attn_blocks
        + [early],
        [
            pltpu.VMEM((half_rows, router_slice), bf16),
            pltpu.VMEM((half_rows, router_slice), bf16),
            pltpu.VMEM((head_width, width), f32),
            pltpu.VMEM((rows, rows), f32),
        ],
        scalars=1,
        waits=[feed_done],
    )
    gradient_scratch = [pltpu.VMEM((half_rows, head_width), f32)] * 2
    d_lower, d_out, d_mean, d_query_lower, d_lower_done = call(
        attend_back_body,
        [
            shaped((half_rows, 2 * head_width), bf16),
            shaped((half_rows, head_width), bf16),
            lines,
            turned_shape,
        ],
        [scalars] + d_attn_blocks + [out_slice, query, kv_lower, choices, log_total, attended],
        [pltpu.VMEM((head_width, half_rows), bf16)] + gradient_scratch,
        scalars=1,
        cost=0,
        waits=[mixed_done],
    )
    back = lax.ppermute(d_lower, "yl", [(1, 0)])
    d_query, d_kv_own, d_query_done = call(
        attend_back_own_body,
        [shaped((half_rows, head_width), bf16), shaped((half_rows, 2 * head_width), f32)],
        [scalars, query, kv_own, log_total, d_out, d_mean, d_query_lower, cosine, sine],
        [
            pltpu.VMEM((head_width, half_rows), bf16),
            pltpu.VMEM((half_rows // QUERIES, head_width, QUERIES), f32),
        ]
        + gradient_scratch,
        scalars=1,
    )
    mixed_part, mixed_part_done = call(
        pair_body,
        [shaped((16, 32, width), bf16)],
        [mixed_mine, other_core(mixed_theirs)],
        cost=0,
        near=[1],
        waits=[d_query_done, feed_pieces],
    )
    mixer_pieces = swap(mixed_part, CHIPS)
    d_mixed, d_own, gain_shift, d_mixed_sum, *d_sent, _ = call(
        project_back_body,
        [
            shaped((half_rows, 3 * head_width), bf16),
            own_shape,
            shaped((2, width), f32),
            shaped((1, 3 * head_width), f32),
        ]
        + [part_shape] * 3,
        [back, d_kv_own, d_query, qkv_slice, cosine, sine] + token_blocks + [router_term1],
        waits=[mixed_part_done],
    )
    d_sent = [to_sender(part, k) for k, part in enumerate(d_sent, 1)]
    d_inputs, d_inputs_done = call(
        inputs_body,
        [own_shape],
        [d_own] + d_sent + [tokens, d_middle, line(attn_gain)],
        room=16,
    )

    feed_rows = block_sum(feed_pieces)
    down_grad = lax.ppermute(feed_rows[32:], ("x", "z"), flipped)
    shared, out_rows, _ = call(
        mixer_sum_body,
        [shaped((24, width), bf16), shaped((8, width), f32)],
        [mixer_pieces],
        near=[0],
    )
    out_grad_rows = lax.ppermute(out_rows, ("x", "z"), flipped)
    up_rows = feed_rows[:32].reshape(RING, 8, units).astype(bf16)
    from_ring = []
    for shift in range(RING):
        rows_of = lax.dynamic_index_in_dim(up_rows, (place + shift) % RING, 0, keepdims=False)
        block = jnp.concatenate([shared, rows_of], axis=0)
        if shift:
            block = lax.ppermute(block, "z", [(k, (k + shift) % RING) for k in range(RING)])
        from_ring.append(block)
    from_ring = jnp.take(jnp.stack(from_ring), ring_order, axis=0)
    early_sum = jnp.sum(from_ring[:, 16:24].astype(f32), axis=0).astype(bf16)
    up_grad = jnp.concatenate([from_ring[k, 24:] for k in range(RING)], axis=1).astype(f32)

    mine, theirs, _ = call(
        project_weight_body,
        [shaped((8, 64, 3 * head_width + 256), bf16)] * 2,
        [scalars, low1_half, d_mixed, d_mixed_sum, gain_shift],
        waits=f_received,
        scalars=1,
    )
    qkv_part, _ = call(
        pair_body,
        [shaped((8, 64, 3 * head_width + 256), bf16)],
        [mine, other_core(theirs)],
        cost=0,
        near=[1],
        waits=[mixer_pieces] + d_sent,
    )
    qkv_part = swap(qkv_part.reshape(64, 8, -1), CHIPS + ("z",))
    qkv_grad, late, _ = call(
        project_sum_body,
        [shaped((8, 3 * width), f32), shaped((1, width), f32)],
        [qkv_part],
        near=[0],
    )

    lanes = router_slice
    routers = jnp.concatenate(
        [
            jnp.concatenate([from_ring[k, :16, j * lanes : (j + 1) * lanes] for k in range(RING)], axis=1)
            for j in (0, 2, 1, 3)
        ]
        + [early_sum[:4], jnp.broadcast_to(late.astype(bf16), (4, width))],
        axis=0,
    )
    routers_mine = spread(routers, CHIPS, 16)
    routers_mine, _ = call(nothing, [], [], waits=[d_inputs_done], passes=[routers_mine])
    routers_theirs = other_core(routers_mine)
    vectors = [3 * width, width, RING * units, width, width, width, width, width]
    width_in_grad, head_in_grad, *vectors, head_out_grad, width_out_grad, prob_sums, _ = call(
        routers_body,
        [shaped((width, router_width), f32)] * 2
        + [shaped((1, size), f32) for size in vectors]
        + [shaped((router_width, CHOICES), f32)] * 2
        + [shaped((1, 128), f32)],
        [core_scalar, routers_mine, routers_theirs],
        [pltpu.VMEM((8, 2, 2, 8, width), f32)],
        scalars=1,
    )
    balance = CHOICES * jnp.sum(share * prob_sums / all_rows)

    return (
        result,
        balance,
        d_inputs,
        qkv_grad,
        out_grad_rows,
        up_grad,
        down_grad,
        *[vector.reshape(-1) for vector in vectors],
        head_in_grad,
        head_out_grad,
        width_in_grad,
        width_out_grad,
    )


def solution(mesh):
    fine = Mesh(mesh.devices.reshape(4, 2, 2, 2, 4), AXES)
    whole = P(AXES, None)
    vector = P(AXES)
    in_specs = (
        whole, whole, whole, P(), whole, P(), whole, P(), whole, P(),
        P(), P(), P(), P(), P(), P(), P(), P(), vector, vector, vector,
    )
    out_specs = (whole, P(), whole, whole, whole, whole, whole) + (P(),) * 12
    return jax.shard_map(local, mesh=fine, in_specs=in_specs, out_specs=out_specs, check_vma=False)
```

```python
import jax
import jax.numpy as jnp
import numpy as np
from jax import lax
from jax.experimental import pallas as pl
from jax.experimental.pallas import tpu as pltpu
from jax.sharding import Mesh
from jax.sharding import PartitionSpec as P


AXES = ("x", "yh", "c", "yl", "z")
CHIPS = ("x", "yh", "yl")
RING = 4
HEADS = 16
HEAD_DIM = 64
CHOICES = 4
EPS = 1e-05
AUX_WEIGHT = 0.1
BLOCKED = -1e30
bf16 = jnp.bfloat16
f32 = jnp.float32
INTERPRET = False
QUERIES = 256
LONG = 10**10


def dot(former, latter):
    return jnp.dot(former, latter, preferred_element_type=f32)


def against(former, latter):
    return lax.dot_general(former, latter, (((1,), (1,)), ((), ())), preferred_element_type=f32)


def across(former, latter):
    return lax.dot_general(former, latter, (((0,), (0,)), ((), ())), preferred_element_type=f32)


def swap(value, axes):
    return lax.all_to_all(value, axes, split_axis=0, concat_axis=0, tiled=True)


def spread(value, axes, count):
    return swap(jnp.broadcast_to(value[None], (count,) + value.shape), axes)


def other_core(value):
    return lax.ppermute(value, "c", [(0, 1), (1, 0)])


def ring_blocks(value):
    return [value] + [
        lax.ppermute(value, "z", [(k, (k + shift) % RING) for k in range(RING)]) for shift in range(1, RING)
    ]


def to_sender(value, shift):
    return lax.ppermute(value, "z", [(k, (k - shift) % RING) for k in range(RING)])


def ring_product(former, latter, product, rows):
    sent = [
        to_sender(product(former[k * rows : (k + 1) * rows], latter).astype(bf16), k) for k in range(1, RING)
    ]
    total = product(former[:rows], latter)
    for part in sent:
        total = total + part.astype(f32)
    return total


def spread_chips(value):
    mine = spread(value, CHIPS, 16)
    return mine, other_core(mine)


def block_sum(pieces):
    return jnp.sum(pieces.astype(f32), axis=0)


def normalize(values):
    centred = values - jnp.mean(values, axis=-1, keepdims=True)
    inv_std = lax.rsqrt(jnp.mean(centred * centred, axis=-1, keepdims=True) + EPS)
    return (centred * inv_std, inv_std)


def rotary_tables(position):
    lane = jnp.arange(2 * HEAD_DIM)
    half = HEAD_DIM // 2
    freqs = 10000.0 ** (-2.0 * (lane % half).astype(f32) / HEAD_DIM)
    angle = position.astype(f32)[:, None] * freqs[None, :]
    return (jnp.cos(angle), jnp.sin(angle) * jnp.where(lane % HEAD_DIM < half, -1.0, 1.0)[None, :])


def call(body, outs, args, scratch=(), scalars=0, cost=LONG, waits=(), room=24, windows=None, passes=(), near=()):
    outs = list(outs) + [shaped((8, 128), f32)]
    given, taken = len(args), len(args) + len(waits) + len(passes)

    def large(value):
        return int(np.prod(value.shape)) * value.dtype.itemsize >= 65536

    windows = windows or {}

    def shape_in(k):
        if k not in windows:
            return args[k].shape
        return tuple(part.stop - part.start for part in windows[k])

    copied_in = [k for k in range(scalars, given) if large(args[k]) and k not in near]
    copied_out = [k for k in range(len(outs)) if large(outs[k])]
    copies = len(copied_in) + len(copied_out)

    def whole(*refs):
        ins, results = list(refs[:given]), list(refs[taken : taken + len(outs)])
        rest = refs[taken + len(outs) + len(passes) :]
        semaphores, buffers, own = rest[0], rest[1 : 1 + copies], rest[1 + copies :]
        moves = []
        for j, k in enumerate(copied_in):
            source = ins[k].at[windows[k]] if k in windows else ins[k]
            move = pltpu.make_async_copy(source, buffers[j], semaphores.at[j])
            move.start()
            moves.append(move)
            ins[k] = buffers[j]
        for move in moves:
            move.wait()
        targets = list(results)
        for j, k in enumerate(copied_out, len(copied_in)):
            results[k] = buffers[j]
        body(*ins, *results[:-1], *own)
        results[-1][...] = jnp.zeros((8, 128), f32)
        moves = []
        for j, k in enumerate(copied_out, len(copied_in)):
            moves.append(pltpu.make_async_copy(buffers[j], targets[k], semaphores.at[j]))
            moves[-1].start()
        for move in moves:
            move.wait()

    def spec(k, copied):
        return pl.BlockSpec(memory_space=pltpu.HBM if k in copied else pltpu.VMEM)

    spaces = [pl.BlockSpec(memory_space=pltpu.SMEM)] * scalars
    spaces += [spec(k, copied_in) for k in range(scalars, given)]
    spaces += [pl.BlockSpec(memory_space=pl.ANY)] * (len(waits) + len(passes))
    buffers = [pltpu.VMEM(shape_in(k), args[k].dtype) for k in copied_in]
    buffers += [pltpu.VMEM(outs[k].shape, outs[k].dtype) for k in copied_out]
    moved = sum(int(np.prod(value.shape)) * value.dtype.itemsize for value in list(args) + list(outs))
    shapes = list(outs) + [shaped(value.shape, value.dtype) for value in passes]
    if not INTERPRET:
        shapes = [
            pltpu.HBM(v.shape, v.dtype) if k in copied_out or k >= len(outs) else v for k, v in enumerate(shapes)
        ]
        args = [pltpu.with_memory_space_constraint(v, pltpu.HBM) if k in copied_in else v for k, v in enumerate(args)]
        passes = [pltpu.with_memory_space_constraint(v, pltpu.HBM) for v in passes]
    results = pl.pallas_call(
        whole,
        out_shape=tuple(shapes),
        in_specs=spaces,
        out_specs=tuple(spec(k, copied_out) for k in range(len(outs)))
        + tuple(pl.BlockSpec(memory_space=pl.ANY) for _ in passes),
        scratch_shapes=[pltpu.SemaphoreType.DMA((max(copies, 1),))] + buffers + list(scratch),
        input_output_aliases={given + len(waits) + k: len(outs) + k for k in range(len(passes))},
        compiler_params=pltpu.CompilerParams(vmem_limit_bytes=room << 20),
        cost_estimate=pl.CostEstimate(flops=cost, bytes_accessed=moved if cost else 0, transcendentals=0),
        interpret=INTERPRET,
    )(*args, *waits, *passes)
    last = len(outs) - 1
    return (*results[:last], *results[last + 1 :], results[last])


def shaped(shape, kind):
    return jax.ShapeDtypeStruct(shape, kind)


def turned(value, cosine, sine):
    lane = lax.broadcasted_iota(jnp.int32, value.shape, 1)
    width = value.shape[1]
    half = HEAD_DIM // 2
    flipped = jnp.where(
        lane % HEAD_DIM < half, pltpu.roll(value, width - half, 1), pltpu.roll(value, half, 1)
    )
    return value * cosine + flipped * sine


def turned_back(value, cosine, sine):
    lane = lax.broadcasted_iota(jnp.int32, value.shape, 1)
    width = value.shape[1]
    half = HEAD_DIM // 2
    moved = value * sine
    flipped = jnp.where(
        lane % HEAD_DIM < half, pltpu.roll(moved, width - half, 1), pltpu.roll(moved, half, 1)
    )
    return value * cosine + flipped


def project_body(core_ref, t0, t1, t2, t3, gain, shift, mine, theirs, bias, cosine, sine, low_ref, query_ref, kv_ref, weight_ref):
    core = core_ref[0]
    weight_ref[:, pl.ds(core, 1)] = mine[...][:, None]
    weight_ref[:, pl.ds(1 - core, 1)] = theirs[...][:, None]
    weight = weight_ref[...].reshape(-1, weight_ref.shape[-1])
    rows = t0.shape[0]
    heads = query_ref.shape[1]
    for k, block in enumerate((t0, t1, t2, t3)):
        at = slice(k * rows, (k + 1) * rows)
        unit, _ = normalize(block[...].astype(f32))
        low = (unit * gain[...] + shift[...]).astype(bf16)
        low_ref[at, :] = low
        mixed = dot(low, weight) + bias[...]
        for j in range(heads // 128):
            lanes = slice(128 * j, 128 * (j + 1))
            query_ref[at, lanes] = turned(mixed[:, lanes], cosine[at, :], sine[at, :]).astype(bf16)
            key = mixed[:, heads + 128 * j : heads + 128 * (j + 1)]
            kv_ref[at, lanes] = turned(key, cosine[at, :], sine[at, :]).astype(bf16)
        kv_ref[at, heads:] = mixed[:, 2 * heads :].astype(bf16)


def kept_row(choice_ref, which, place, k):
    chosen = choice_ref[(place + RING - k) % RING, which : which + 1, :].astype(f32)
    return jnp.where(chosen >= place.astype(f32), 1.0, 0.0)


def column(row):
    return jnp.broadcast_to(row, (row.shape[1], row.shape[1])).T[:, :1]


def order_of(shape, axis, place, first=0):
    at = lax.broadcasted_iota(jnp.int32, shape, axis) + first
    return ((place + RING - at // 128) % RING) * 128 + at % 128


def own_part(h, query):
    lane = lax.broadcasted_iota(jnp.int32, query.shape, 1)
    return jnp.where(lane // HEAD_DIM == h, query, jnp.zeros_like(query)) * jnp.asarray(HEAD_DIM ** (-0.5), bf16)


def masked(score, own, flag, place, q_block):
    if not own:
        return jnp.where(flag, score, BLOCKED)
    keys = order_of((score.shape[0], 1), 0, place)
    return jnp.where(keys <= order_of((1, score.shape[1]), 1, place, q_block * QUERIES), score, BLOCKED)


def loop(heads, queries, step):
    blocks = queries // QUERIES

    def one(at, carry):
        h, q_block = at // blocks, at % blocks
        here = pl.ds(pl.multiple_of(q_block * QUERIES, QUERIES), QUERIES)
        features = pl.ds(pl.multiple_of(h * HEAD_DIM, HEAD_DIM), HEAD_DIM)
        step(at, h, q_block, here, features)
        return carry

    lax.fori_loop(0, blocks * (heads // HEAD_DIM), one, 0)


def attend_own_body(scalars, query_ref, kv_ref, top_ref, total_ref, out_ref, value_turned):
    heads = query_ref.shape[1]
    value_turned[...] = kv_ref[:, heads:].T
    flag, place = scalars[2] == 1, scalars[1]

    def step(at, h, q_block, here, features):
        score = against(kv_ref[:, :heads], own_part(h, query_ref[here, :]))
        score = masked(score, True, flag, place, q_block)
        top = jnp.max(score, axis=0, keepdims=True)
        expo = jnp.exp(score - top)
        top_ref[at] = top
        total_ref[at] = jnp.sum(expo, axis=0, keepdims=True)
        out_ref[q_block, features, :] = dot(value_turned[features, :], expo.astype(bf16))

    loop(heads, query_ref.shape[0], step)


def attend_body(
    scalars, query_ref, kv_ref, own_top, own_total, own_out, choice_ref, out_ref, total_ref, value_turned, out_turned,
):
    heads = query_ref.shape[1]
    value_turned[...] = kv_ref[:, heads:].T
    flag, place = scalars[2] == 1, scalars[1]

    def step(at, h, q_block, here, features):
        score = against(kv_ref[:, :heads], own_part(h, query_ref[here, :]))
        score = masked(score, False, flag, place, q_block)
        top = jnp.maximum(jnp.max(score, axis=0, keepdims=True), own_top[at])
        expo = jnp.exp(score - top)
        factor = jnp.exp(own_top[at] - top)
        total = jnp.sum(expo, axis=0, keepdims=True) + factor * own_total[at]
        total_ref[at] = top + jnp.log(total)
        out = dot(value_turned[features, :], expo.astype(bf16)) + factor * own_out[q_block, features, :]
        out_turned[q_block, features, :] = out / total

    loop(heads, query_ref.shape[0], step)
    for k in range(query_ref.shape[0] // QUERIES):
        at = slice(k * QUERIES, (k + 1) * QUERIES)
        keep = jnp.concatenate([kept_row(choice_ref, 0, place, 2 * k + j) for j in range(2)], axis=1)
        out_ref[at, :] = (out_turned[k] * keep).T.astype(bf16)


def back_step(own, scalars, query_ref, kv_ref, total_ref, d_out, mean_ref, key_turned, d_query_turned, d_key, d_value):
    heads = query_ref.shape[1]
    flag, place = scalars[2] == 1, scalars[1]

    def step(at, h, q_block, here, features):
        query = own_part(h, query_ref[here, :])
        score = masked(against(kv_ref[:, :heads], query), own, flag, place, q_block)
        prob = jnp.exp(score - total_ref[at])
        gradient = d_out[here, :]
        lane = lax.broadcasted_iota(jnp.int32, gradient.shape, 1)
        gradient = jnp.where(lane // HEAD_DIM == h, gradient, jnp.zeros_like(gradient))
        d_value[...] += dot(prob.astype(bf16), gradient)
        d_score = (prob * (against(kv_ref[:, heads:], gradient) - mean_ref[at])).astype(bf16)
        d_key[...] += dot(d_score, query)
        d_query = dot(key_turned[features, :], d_score) * (HEAD_DIM ** (-0.5))
        if own:
            d_query += d_query_turned[q_block, features, :]
        d_query_turned[q_block, features, :] = d_query

    return step


def attend_back_body(
    scalars, g0, g1, g2, g3, out_slice, query_ref, kv_ref, choice_ref, total_ref, attended,
    send_ref, d_out, mean_ref, d_query_turned, key_turned, d_key, d_value,
):
    heads = query_ref.shape[1]
    rows = query_ref.shape[0] // RING
    place = scalars[1]
    blocks = query_ref.shape[0] // QUERIES
    key_turned[...] = kv_ref[:, :heads].T
    d_key[...] = jnp.zeros_like(d_key)
    d_value[...] = jnp.zeros_like(d_value)
    for k, block in enumerate((g0, g1, g2, g3)):
        at = slice(k * rows, (k + 1) * rows)
        part = against(block[:rows, :], out_slice[...])
        d_out[at, :] = (part * column(kept_row(choice_ref, 0, place, k))).astype(bf16)
    for k in range(blocks):
        at = slice(k * QUERIES, (k + 1) * QUERIES)
        product = (d_out[at, :].astype(f32) * attended[at, :].astype(f32)).T
        for h in range(heads // HEAD_DIM):
            part = product[h * HEAD_DIM : (h + 1) * HEAD_DIM]
            mean_ref[h * blocks + k] = jnp.sum(part, axis=0, keepdims=True)
    loop(
        heads,
        query_ref.shape[0],
        back_step(
            False, scalars, query_ref, kv_ref, total_ref, d_out, mean_ref, key_turned, d_query_turned, d_key, d_value
        ),
    )
    send_ref[:, :heads] = d_key[...].astype(bf16)
    send_ref[:, heads:] = d_value[...].astype(bf16)


def attend_back_own_body(
    scalars, query_ref, kv_ref, total_ref, d_out, mean_ref, lower, cosine, sine,
    d_query_ref, own_ref, key_turned, d_query_turned, d_key, d_value,
):
    heads = query_ref.shape[1]
    key_turned[...] = kv_ref[:, :heads].T
    d_query_turned[...] = lower[...]
    d_key[...] = jnp.zeros_like(d_key)
    d_value[...] = jnp.zeros_like(d_value)
    loop(
        heads,
        query_ref.shape[0],
        back_step(
            True, scalars, query_ref, kv_ref, total_ref, d_out, mean_ref, key_turned, d_query_turned, d_key, d_value
        ),
    )
    own_ref[:, :heads] = d_key[...]
    own_ref[:, heads:] = d_value[...]
    for k in range(query_ref.shape[0] // QUERIES):
        at = slice(k * QUERIES, (k + 1) * QUERIES)
        value = d_query_turned[k].T
        for j in range(heads // 128):
            lanes = slice(128 * j, 128 * (j + 1))
            d_query_ref[at, lanes] = turned_back(value[:, lanes], cosine[at, :], sine[at, :]).astype(bf16)


def head_slice_body(scalars, low, router_in, slice_ref):
    size = slice_ref.shape[1]
    lanes = pl.ds(pl.multiple_of(scalars[1] * size, size), size)
    slice_ref[...] = jnp.tanh(dot(low[...], router_in[:, lanes]))


def project_back_body(
    back_ref, own_ref, d_query_ref, weight, cosine, sine, t0, t1, t2, t3, term_ref,
    mixed_ref, total_ref, sums_ref, bias_ref, p1, p2, p3,
):
    heads = d_query_ref.shape[1]
    rows = t0.shape[0]
    gain_sum = jnp.zeros((1, t0.shape[1]), f32)
    shift_sum = jnp.zeros((1, t0.shape[1]), f32)
    bias_sum = jnp.zeros((1, 3 * heads), f32)
    for k, (block, part) in enumerate(((t1, p1), (t2, p2), (t3, p3), (t0, total_ref)), 1):
        k = k % RING
        at = slice(k * rows, (k + 1) * rows)
        mixed_ref[at, :heads] = d_query_ref[at, :]
        for j in range(heads // 128):
            lanes = slice(128 * j, 128 * (j + 1))
            value = own_ref[at, lanes] + back_ref[at, lanes].astype(f32)
            mixed_ref[at, heads + 128 * j : heads + 128 * (j + 1)] = turned_back(
                value, cosine[at, :], sine[at, :]
            ).astype(bf16)
        mixed_ref[at, 2 * heads :] = (own_ref[at, heads:] + back_ref[at, heads:].astype(f32)).astype(bf16)
        mixed = mixed_ref[at, :]
        bias_sum += jnp.sum(mixed.astype(f32), axis=0, keepdims=True)
        gradient = against(mixed, weight[...])
        if k == 0:
            gradient = gradient + term_ref[...]
        part[...] = gradient.astype(part.dtype)
        unit, _ = normalize(block[...].astype(f32))
        gain_sum += jnp.sum(gradient * unit, axis=0, keepdims=True)
        shift_sum += jnp.sum(gradient, axis=0, keepdims=True)
    sums_ref[0:1, :] = gain_sum
    sums_ref[1:2, :] = shift_sum
    bias_ref[...] = bias_sum


def project_weight_body(scalars, low_ref, mixed_ref, bias_ref, sums_ref, mine_ref, theirs_ref):
    core, place = scalars[0], scalars[1]
    size = bias_ref.shape[1] // 3
    row = lax.broadcasted_iota(jnp.int32, (8, size), 0)
    late = [jnp.where(row == place, bias_ref[:, size * k : size * (k + 1)], 0.0) for k in range(3)]
    for k in range(2):
        block = jnp.zeros((8, size), f32)
        for j in range(RING):
            block = jnp.where(row == j, sums_ref[k : k + 1, size * j : size * (j + 1)], block)
        late.append(block)
    late += [jnp.zeros((8, size), f32)] * 3
    lanes = mixed_ref.shape[1]
    for k in range(8):
        turned_low = low_ref[:, 128 * k : 128 * (k + 1)].T
        mine, theirs = halves(core, dot(turned_low, mixed_ref[...]))
        mine_ref[k, :, :lanes] = mine.astype(bf16)
        theirs_ref[k, :, :lanes] = theirs.astype(bf16)
        for j in range(2):
            at = slice(32 * j, 32 * (j + 1))
            if k >= 2:
                mine_ref[k, at, lanes:] = jnp.zeros((32, size), bf16)
                theirs_ref[k, at, lanes:] = jnp.zeros((32, size), bf16)
                continue
            mine, theirs = halves(core, jnp.concatenate([late[4 * k + j], late[4 * k + 2 + j]], axis=0))
            mine_ref[k, at, lanes:] = jnp.concatenate([mine] * RING, axis=0).astype(bf16)
            theirs_ref[k, at, lanes:] = jnp.concatenate([theirs] * RING, axis=0).astype(bf16)


def halves(core, part):
    half = part.shape[0] // 2
    first, second = part[:half], part[half:]
    return jnp.where(core == 0, first, second), jnp.where(core == 0, second, first)


def assemble(core, target, mine, theirs):
    target[:, pl.ds(core, 1)] = mine[...][:, None]
    target[:, pl.ds(1 - core, 1)] = theirs[...][:, None]
    return target[...].reshape(-1, target.shape[-1])


def pack_body(qkv, up, head_choice, width_choice, packed_ref):
    heads = qkv.shape[1] // 3 // RING
    units = up.shape[1] // RING
    row = lax.broadcasted_iota(jnp.int32, (8, head_choice.shape[1]), 0)
    choices = jnp.where(
        row == 0, head_choice[...].astype(f32), jnp.where(row == 1, width_choice[...].astype(f32), 0.0)
    ).astype(bf16)
    for z in range(RING):
        for j in range(3):
            packed_ref[z, :, j * heads : (j + 1) * heads] = qkv[:, (j * RING + z) * heads : (j * RING + z + 1) * heads]
        packed_ref[z, :, 3 * heads : 3 * heads + units] = up[:, z * units : (z + 1) * units]
        packed_ref[z, :, 3 * heads + units :] = choices


def head_body(tokens, gain, shift, router_in, router_out, choice, squash_ref, prob_ref, gate_ref):
    unit, _ = normalize(tokens[...].astype(f32))
    low = (unit * gain[...] + shift[...]).astype(bf16)
    squash = jnp.tanh(dot(low, router_in[...]))
    squash_ref[...] = squash
    logit = dot(squash.astype(bf16), router_out[...])
    lane = lax.broadcasted_iota(jnp.int32, logit.shape, 1)
    logit = jnp.where(lane < CHOICES, logit, BLOCKED)
    expo = jnp.exp(logit - jnp.max(logit, axis=-1, keepdims=True))
    prob = expo / jnp.sum(expo, axis=-1, keepdims=True)
    prob_ref[...] = prob
    gate_ref[...] = jnp.sum(
        jnp.where(lane.astype(f32) == column(choice[...].astype(f32)), prob, 0.0), axis=-1, keepdims=True
    )


def mixer_body(pieces, out_rows, mixer_ref):
    size = mixer_ref.shape[2] // RING
    for k in range(mixer_ref.shape[0]):
        for j in range(RING):
            at = slice(8 * j, 8 * (j + 1))
            mixer_ref[k, at, : 3 * size] = pieces[j, :, : 3 * size]
            mixer_ref[k, at, 3 * size :] = out_rows[:, j * size : (j + 1) * size]


def count_body(choice_ref, pieces, down, rest_ref):
    lane = lax.broadcasted_iota(jnp.int32, (1, rest_ref.shape[2]), 1)
    line = jnp.zeros((1, rest_ref.shape[2]), f32)
    for which in range(2):
        chosen = choice_ref[:, which, :].astype(f32)
        for option in range(CHOICES):
            count = jnp.sum(jnp.where(chosen == option, 1.0, 0.0), axis=1, keepdims=True)
            count = jnp.sum(count, axis=0, keepdims=True)
            pairs = jnp.floor(count * 0.5)
            at = which * CHOICES + option
            line = jnp.where(lane == at, pairs, line)
            line = jnp.where(lane == at + 2 * CHOICES, count - 2.0 * pairs, line)
    last = jnp.broadcast_to(line, (8, rest_ref.shape[2])).astype(bf16)
    heads = (pieces.shape[2] - rest_ref.shape[2] - choice_ref.shape[2]) // 3
    for k in range(rest_ref.shape[0]):
        for j in range(RING):
            rest_ref[k, 8 * j : 8 * (j + 1)] = pieces[j, :, 3 * heads : 3 * heads + rest_ref.shape[2]]
        rest_ref[k, 32:64] = down[...]
        rest_ref[k, 64:] = last


def out_body(scalars, attended, mine, theirs, slice_ref, p0, p1, p2, p3, full):
    core = scalars[0]
    size = mine.shape[-1]
    for x in range(4):
        for yh in range(2):
            for yl in range(2):
                at = (x * 2 + yh) * 2 + yl
                for k in range(4):
                    rows, lanes = slice(8 * k, 8 * (k + 1)), slice(size * k, size * (k + 1))
                    full[yh, pl.ds(core, 1), yl, x, :, lanes] = mine[at : at + 1, rows].astype(f32)
                    full[yh, pl.ds(1 - core, 1), yl, x, :, lanes] = theirs[at : at + 1, rows].astype(f32)
    weight = full[...].reshape(slice_ref.shape).astype(bf16)
    slice_ref[...] = weight
    rows = p0.shape[0]
    for k, part in ((1, p1), (2, p2), (3, p3), (0, p0)):
        part[...] = dot(attended[k * rows : (k + 1) * rows, :], weight).astype(part.dtype)


def middle_body(p0, r1, r2, r3, tokens, bias, gate, gain, shift, attn_pre_ref, middle_ref, low_ref):
    total = p0[...]
    for part in (r1, r2, r3):
        total = total + part[...].astype(f32)
    total = total + bias[...]
    attn_pre_ref[...] = total
    middle = tokens[...].astype(f32) + gate[...] * total
    middle_ref[...] = middle
    unit, _ = normalize(middle)
    low_ref[...] = (unit * gain[...] + shift[...]).astype(bf16)


def slice_of(value, place, size):
    part = value[:, :size]
    for k in range(1, RING):
        part = jnp.where(place == k, value[:, k * size : (k + 1) * size], part)
    return part


def feed_body(
    scalars, n0, n1, n2, n3, up_mine, up_theirs, up_bias, router_in, router_out, down_mine, down_theirs,
    g0, g1, g2, g3, choice_ref,
    f0, f1, f2, f3, d0, d1, d2, d3, dgate_ref, low_ref, d_up_ref, active_ref, d_ffn_ref, up_sum_ref,
    prob_ref, gate_ref, squash_ref, slice_ref, up_full, down_full,
):
    core, place = scalars[0], scalars[1]
    up = assemble(core, up_full, up_mine, up_theirs)
    for x in range(4):
        for yh in range(2):
            for yl in range(2):
                down_full[yh, pl.ds(core, 1), yl, x] = down_mine[2 * x + yh, yl : yl + 1]
                down_full[yh, pl.ds(1 - core, 1), yl, x] = down_theirs[2 * x + yh, yl : yl + 1]
    down = down_full[...].reshape(-1, down_full.shape[-1])
    rows = n0.shape[0]
    units = up_bias.shape[1]
    router_slice = slice_ref.shape[1]
    up_sum = jnp.zeros((1, units), f32)
    for blocks in (((1, n1, g1, f1, d1), (2, n2, g2, f2, d2)), ((3, n3, g3, f3, d3), (0, n0, g0, f0, d0))):
        low = jnp.concatenate([block[1][...] for block in blocks], axis=0)
        keep_row = [kept_row(choice_ref, 1, place, block[0]) for block in blocks]
        keep = jnp.concatenate([column(row) for row in keep_row], axis=0)
        chosen = jnp.concatenate(
            [column(choice_ref[(place + RING - block[0]) % RING, 1:2, :].astype(f32)) for block in blocks], axis=0
        )
        upward = dot(low, up) + up_bias[...]
        active = jnp.maximum(upward, 0.0) * keep
        active_low = (active * active).astype(bf16)
        squash = jnp.tanh(dot(low, router_in[...]))
        logit = dot(squash.astype(bf16), router_out[...])
        lane = lax.broadcasted_iota(jnp.int32, logit.shape, 1)
        logit = jnp.where(lane // CHOICES == 1, logit, BLOCKED)
        expo = jnp.exp(logit - jnp.max(logit, axis=-1, keepdims=True))
        prob = expo / jnp.sum(expo, axis=-1, keepdims=True)
        gate = jnp.sum(jnp.where((lane - CHOICES).astype(f32) == chosen, prob, 0.0), axis=-1, keepdims=True)
        part = slice_of(squash, place, router_slice)
        ffn_part = dot(active_low, down)
        grad_out = jnp.concatenate([block[2][...] for block in blocks], axis=0).astype(f32)
        dgate = jnp.sum(grad_out * ffn_part, axis=-1, keepdims=True)
        d_ffn = (gate * grad_out).astype(bf16)
        d_up = (against(d_ffn, down) * 2.0 * active).astype(bf16)
        up_sum += jnp.sum(d_up.astype(f32), axis=0, keepdims=True)
        d_normed = against(d_up, up)
        for j, (k, _, _, ffn, d_block) in enumerate(blocks):
            at, here = slice(k * rows, (k + 1) * rows), slice(j * rows, (j + 1) * rows)
            low_ref[at, :] = low[here]
            active_ref[at, :] = active_low[here]
            slice_ref[at, :] = part[here]
            d_ffn_ref[at, :] = d_ffn[here]
            d_up_ref[at, :] = d_up[here]
            ffn[...] = ffn_part[here].astype(ffn.dtype)
            d_block[:rows, :] = d_normed[here].astype(d_block.dtype)
            line = jnp.broadcast_to(dgate[here], (rows, rows)).T[:1]
            if k == 0:
                dgate_ref[...] = line
                squash_ref[...] = squash[here]
                prob_ref[...] = prob[here]
                gate_ref[...] = gate[here]
            else:
                upper = line.astype(bf16).astype(f32)
                row = lax.broadcasted_iota(jnp.int32, (8, rows), 0)
                lines = jnp.where(row == 0, upper, jnp.where(row == 1, line - upper, 0.0)).astype(bf16)
                d_block[rows:, :] = jnp.concatenate([lines] * (units // rows), axis=1)
    up_sum_ref[...] = up_sum


def feed_weight_body(
    core_ref, low_ref, d_up_ref, active_ref, d_ffn_ref, p1, p2, p3, mine_ref, theirs_ref, f1, f2, f3
):
    core = core_ref[0]
    for ffn, part in ((f1, p1), (f2, p2), (f3, p3)):
        ffn[...] = part[...]
    for k in range(8):
        turned_low = low_ref[:, 128 * k : 128 * (k + 1)].T
        mine, theirs = halves(core, dot(turned_low, d_up_ref[...]))
        for j in range(2):
            mine_ref[2 * k + j, :32, :] = mine[32 * j : 32 * (j + 1)].astype(bf16)
            theirs_ref[2 * k + j, :32, :] = theirs[32 * j : 32 * (j + 1)].astype(bf16)
    for yh in range(2):
        for yl in range(2):
            for target, side in ((mine_ref, core), (theirs_ref, 1 - core)):
                lanes = pl.ds(pl.multiple_of(((yh * 2 + side) * 2 + yl) * 128, 128), 128)
                part = dot(active_ref[:, lanes].T, d_ffn_ref[...]).astype(bf16)
                for x in range(4):
                    target[(x * 2 + yh) * 2 + yl, 32:, :] = part[32 * x : 32 * (x + 1)]


def pair_body(mine, theirs, sum_ref):
    sum_ref[...] = (mine[...].astype(f32) + theirs[...].astype(f32)).astype(bf16)


def nothing(*refs):
    pass


def own_back_body(
    scalars, d0, r1, r2, r3, middle_ref, router_in, grad_ref, squash_ref, head_squash_ref, attn_pre_ref,
    dgate_ref, down_bias, prob_ref, gate_ref, head_prob_ref, head_gate_ref, head_choice, width_choice,
    counts_mine, counts_theirs, width_out, head_out, gain, up_sum,
    payload_ref, d_middle_ref, d_hidden_ref, early_ref, share_ref,
):
    place = scalars[1]
    rows = grad_ref.shape[0]
    units = up_sum.shape[1]
    aux = AUX_WEIGHT * CHOICES / (128.0 * rows)
    grad_out = grad_ref[...].astype(f32)
    d_normed = d0[...]
    line = dgate_ref[...]
    for part in (r1, r2, r3):
        d_normed = d_normed + part[:rows, :].astype(f32)
        lines = part[rows:, :rows].astype(f32)
        line = line + lines[:1] + lines[1:2]
    dgate = column(line) + jnp.sum(grad_out * down_bias[...], axis=-1, keepdims=True)
    pairs = jnp.sum(counts_mine[...].astype(f32) + counts_theirs[...].astype(f32), axis=0)[:1]
    share = (2.0 * pairs + pltpu.roll(pairs, 128 - 2 * CHOICES, 1)) / (128.0 * rows)
    share_ref[...] = share
    at = lax.broadcasted_iota(jnp.int32, share.shape, 1)
    lane = lax.broadcasted_iota(jnp.int32, prob_ref.shape, 1).astype(f32)

    def d_logits(which, prob, choice, dgate):
        picked = jnp.where(lane - which * CHOICES == column(choice[...].astype(f32)), dgate, 0.0)
        d_prob = picked + aux * jnp.where(at // CHOICES == which, share, 0.0)
        return prob * (d_prob - jnp.sum(prob * d_prob, axis=-1, keepdims=True))

    d_width = d_logits(1, prob_ref[...], width_choice, dgate)
    squash = squash_ref[...]
    d_hidden = (against(d_width.astype(bf16), width_out[...]) * (1.0 - squash * squash)).astype(bf16)
    d_normed = d_normed + against(d_hidden, router_in[...])
    unit, inv_std = normalize(middle_ref[...])
    scaled = d_normed * gain[...]
    inner = (
        scaled
        - jnp.mean(scaled, axis=-1, keepdims=True)
        - unit * jnp.mean(scaled * unit, axis=-1, keepdims=True)
    )
    d_middle = inner * inv_std + grad_out
    d_middle_ref[...] = d_middle
    head_dgate = jnp.sum(d_middle * attn_pre_ref[...], axis=-1, keepdims=True)
    d_attn = (head_gate_ref[...] * d_middle).astype(bf16)
    payload_ref[:rows, :] = d_attn
    d_head = d_logits(0, head_prob_ref[...], head_choice, head_dgate)
    head_squash = head_squash_ref[...]
    d_hidden_ref[...] = (against(d_head.astype(bf16), head_out[...]) * (1.0 - head_squash * head_squash)).astype(bf16)
    d_logit = (d_head + d_width).T[:8].astype(bf16)
    payload_ref[rows:, :] = jnp.concatenate([d_logit] * (units // rows), axis=1)
    row = lax.broadcasted_iota(jnp.int32, (8, units), 0)
    d_ffn = (gate_ref[...] * grad_out).astype(bf16).astype(f32)
    vectors = (
        jnp.sum(d_attn.astype(f32), axis=0, keepdims=True),
        jnp.sum(d_ffn, axis=0, keepdims=True),
        jnp.sum(d_normed * unit, axis=0, keepdims=True),
        jnp.sum(d_normed, axis=0, keepdims=True),
    )
    first = dot(d_logit, head_squash.astype(bf16))
    second = dot(d_logit, squash.astype(bf16))
    block = jnp.where(row < CHOICES, first, second)
    early_ref[0:8, :] = block
    block = jnp.zeros((8, units), f32)
    for k, vector in enumerate(vectors):
        block = jnp.where(row == k, vector, block)
    for k in range(RING):
        block = jnp.where(row == RING + k, jnp.where(place == k, up_sum[...], 0.0), block)
    early_ref[8:16, :] = block
    probs = jnp.sum(head_prob_ref[...] + prob_ref[...], axis=0, keepdims=True)
    early_ref[16:24, :] = jnp.broadcast_to(jnp.concatenate([probs] * (units // 128), axis=1), (8, units))
    early_ref[24:32, :] = jnp.zeros((8, units), f32)


def mixer_weight_body(
    scalars, low1, low2, width_slice, head_slice, width_out, head_out, attended, g0, g1, g2, g3, early,
    mine_ref, theirs_ref, d_width, d_head, part_ref, logit_ref,
):
    core, place = scalars[0], scalars[1]
    rows = attended.shape[0] // RING
    size = width_slice.shape[1]
    here = pl.ds(pl.multiple_of(place * size, size), size)
    logit_ref[...] = jnp.zeros_like(logit_ref)
    for k, block in enumerate((g0, g1, g2, g3)):
        at = slice(k * rows, (k + 1) * rows)
        logit_ref[:8, :] = block[rows:, :rows].astype(f32)
        logit = logit_ref[...].T.astype(bf16)
        for target, weight, slices in ((d_width, width_out, width_slice), (d_head, head_out, head_slice)):
            squash = slices[at, :]
            target[at, :] = (against(logit, weight[here, :]) * (1.0 - squash * squash)).astype(bf16)
    for k in range(8):
        lanes = slice(128 * k, 128 * (k + 1))
        for first, former, latter in ((0, low2, d_width), (size, low1, d_head)):
            mine, theirs = halves(core, dot(former[:, lanes].T, latter[...]))
            for j in range(2):
                for half in range(2):
                    at = slice(32 * j + 16 * half, 32 * j + 16 * (half + 1))
                    to = slice(2 * size * half + first, 2 * size * half + first + size)
                    mine_ref[2 * k + j, 0:16, to] = mine[at].astype(bf16)
                    theirs_ref[2 * k + j, 0:16, to] = theirs[at].astype(bf16)
    turned_out = attended[...].T
    part = dot(turned_out[:, :rows], g0[:rows, :])
    for k, block in ((1, g1), (2, g2), (3, g3)):
        part += dot(turned_out[:, k * rows : (k + 1) * rows], block[:rows, :])
    part_ref[...] = part
    for x in range(4):
        for yh in range(2):
            for yl in range(2):
                to = (x * 2 + yh) * 2 + yl
                base = 2 * yh * 64 + (4 * yl + x) * 8
                at = (x * 2 + yh) * 4 + yl
                first = jnp.broadcast_to(early[at : at + 1, :], (8, early.shape[1]))
                second = jnp.broadcast_to(early[at + 2 : at + 3, :], (8, early.shape[1]))
                for target, side in ((mine_ref, core), (theirs_ref, 1 - core)):
                    out = part_ref[pl.ds(pl.multiple_of(base + side * 64, 8), 8), :]
                    vector = jnp.where(side == 0, first, second)
                    target[to, 16:32, :] = jnp.concatenate([out, vector], axis=0).astype(bf16)


def mixer_sum_body(pieces, shared_ref, out_ref):
    rows = jnp.sum(pieces[...].astype(f32), axis=0)
    shared_ref[:16, :] = rows[:16].astype(bf16)
    shared_ref[16:, :] = rows[24:].astype(bf16)
    out_ref[...] = rows[16:24]


def project_sum_body(pieces, grad_ref, late_ref):
    late = jnp.zeros((8, late_ref.shape[1] // RING), f32)
    heads = grad_ref.shape[1] // 3 // RING
    for z in range(RING):
        part = pieces[z].astype(f32)
        for k in range(1, 16):
            part = part + pieces[k * RING + z].astype(f32)
        for j in range(3):
            grad_ref[:, (j * RING + z) * heads : (j * RING + z + 1) * heads] = part[:, j * heads : (j + 1) * heads]
        late = late + part[:, 3 * heads :]
    late_ref[...] = jnp.concatenate([late[k : k + 1] for k in range(RING)], axis=1)


def routers_body(
    core_ref, mine, theirs, width_ref, head_ref, qkv_ref, out_ref, up_ref, down_ref, attn_gain_ref, attn_shift_ref,
    ffn_gain_ref, ffn_shift_ref, head_out_ref, width_out_ref, prob_ref, full,
):
    core = core_ref[0]
    rows = width_ref.shape[0] // 32
    for j in range(16):
        x_yh, yl = j // 2, j % 2
        for source, side in ((mine, core), (theirs, 1 - core)):
            at = pl.multiple_of(((x_yh * 2 + side) * 2 + yl) * rows, rows)
            width_ref[pl.ds(at, rows), :] = source[j, :rows, :].astype(f32)
            head_ref[pl.ds(at, rows), :] = source[j, rows : 2 * rows, :].astype(f32)
            full[x_yh, pl.ds(side, 1), yl] = source[j, 2 * rows :, :].astype(f32)[None]

    def vector(at, late=0):
        return full[at // 4, at // 2 % 2, at % 2, late : late + 1, :]

    size = full.shape[-1]
    for k in range(3):
        qkv_ref[:, k * size : (k + 1) * size] = vector(k, 4)
    attn_gain_ref[...] = vector(3, 4)
    attn_shift_ref[...] = vector(4, 4)
    out_ref[...] = vector(8)
    down_ref[...] = vector(9)
    ffn_gain_ref[...] = vector(10)
    ffn_shift_ref[...] = vector(11)
    for k in range(RING):
        up_ref[:, k * size : (k + 1) * size] = vector(12 + k)
    prob_ref[...] = vector(16)[:, :128]
    head_out_ref[...] = jnp.concatenate([vector(k) for k in range(CHOICES)], axis=0)
    width_out_ref[...] = jnp.concatenate([vector(CHOICES + k) for k in range(CHOICES)], axis=0)


def result_body(ffn, r1, r2, r3, bias, middle, gate, result_ref):
    total = ffn[...]
    for part in (r1, r2, r3):
        total = total + part[...].astype(f32)
    result_ref[...] = (middle[...] + gate[...] * (total + bias[...])).astype(bf16)


def inputs_body(d_own, r1, r2, r3, tokens, d_middle, gain, d_inputs_ref):
    gradient = d_own[...]
    for part in (r1, r2, r3):
        gradient = gradient + part[...].astype(f32)
    unit, inv_std = normalize(tokens[...].astype(f32))
    scaled = gradient * gain[...]
    inner = (
        scaled
        - jnp.mean(scaled, axis=-1, keepdims=True)
        - unit * jnp.mean(scaled * unit, axis=-1, keepdims=True)
    )
    d_inputs_ref[...] = inner * inv_std + d_middle[...]


def local(
    tokens,
    out_grad,
    qkv_weight,
    qkv_bias,
    out_weight,
    out_bias,
    up_weight,
    up_bias,
    down_weight,
    down_bias,
    attn_gain,
    attn_shift,
    ffn_gain,
    ffn_shift,
    head_router_in,
    head_router_out,
    width_router_in,
    width_router_out,
    head_choice,
    width_choice,
    seq_ids,
):
    rows, width = tokens.shape
    half_rows = RING * rows
    own_heads = HEADS // RING
    head_width = own_heads * HEAD_DIM
    units = up_weight.shape[1] // RING
    router_width = head_router_in.shape[1]
    router_slice = router_width // RING
    all_rows = rows * 128
    core = lax.axis_index("c").astype(jnp.int32)
    place = lax.axis_index("z").astype(jnp.int32)
    one_sequence = (lax.axis_index("yl") == 1) & (seq_ids[0] % 2 == 0)
    core_scalar = core.reshape(1)
    scalars = jnp.stack([core, place, one_sequence.astype(jnp.int32)])
    flipped = [(a * 4 + b, b * 4 + a) for a in range(4) for b in range(4)]
    own_shape = shaped((rows, width), f32)
    part_shape = shaped((rows, width), bf16)
    half_shape = shaped((half_rows, width), bf16)
    sent_shape = shaped((rows + 8, width), bf16)

    def line(vector):
        return vector.reshape(1, -1)

    out_swapped = lax.ppermute(out_weight, ("x", "z"), flipped)
    down_swapped = lax.ppermute(down_weight, ("x", "z"), flipped)
    packed, _ = call(
        pack_body,
        [shaped((RING, 8, 3 * head_width + units + rows), bf16)],
        [qkv_weight, up_weight, line(head_choice), line(width_choice)],
        room=16,
    )
    ring_order = (place - jnp.arange(RING)) % RING
    order = (ring_order[:, None] * rows + jnp.arange(rows)[None, :]).reshape(half_rows)
    cosine, sine = rotary_tables(order + jnp.where(one_sequence, half_rows, 0))
    head_out = jnp.pad(head_router_out, ((0, 0), (0, 128 - CHOICES)))
    width_out = jnp.pad(width_router_out, ((0, 0), (CHOICES, 128 - 2 * CHOICES)))
    own_up_bias = lax.dynamic_index_in_dim(up_bias.reshape(RING, units), place, 0, keepdims=True)
    own_qkv_bias = lax.dynamic_index_in_dim(qkv_bias.reshape(3, RING, head_width), place, 1, keepdims=False)
    head_squash, head_prob, head_gate, head_done = call(
        head_body,
        [own_shape, shaped((rows, 128), f32), shaped((rows, 1), f32)],
        [tokens, line(attn_gain), line(attn_shift), head_router_in, head_out, line(head_choice)],
        waits=[cosine, width_out, own_up_bias, own_qkv_bias],
    )

    pieces = swap(packed, "z")
    choices = pieces[:, :, 3 * head_width + units :]
    token_blocks = ring_blocks(tokens)
    mixer_all, _ = call(
        mixer_body,
        [shaped((16, 32, width), bf16)],
        [pieces, out_swapped],
        waits=[head_done] + token_blocks[1:],
        room=16,
    )
    mixer_mine = swap(mixer_all, CHIPS)
    mixer_theirs = other_core(mixer_mine)
    rest_all, _ = call(
        count_body,
        [shaped((16, 72, width), bf16)],
        [choices, pieces, down_swapped],
        room=16,
        waits=[mixer_mine],
    )

    qkv_lanes = (slice(0, 8), slice(0, 64), slice(0, 3 * head_width))
    low1_half, query, kv_own, qkv_slice, _ = call(
        project_body,
        [
            half_shape,
            shaped((half_rows, head_width), bf16),
            shaped((half_rows, 2 * head_width), bf16),
            shaped((8, 2, 64, 3 * head_width), bf16),
        ],
        [core_scalar] + token_blocks
        + [
            line(attn_gain), line(attn_shift),
            mixer_mine.reshape(8, 64, -1), mixer_theirs.reshape(8, 64, -1),
            line(own_qkv_bias), cosine, sine,
        ],
        scalars=1,
        windows={7: qkv_lanes, 8: qkv_lanes},
    )
    qkv_slice = qkv_slice.reshape(width, 3 * head_width)
    kv_lower = lax.ppermute(kv_own, "yl", [(0, 1)])
    lines = shaped((own_heads * half_rows // QUERIES, 1, QUERIES), f32)
    turned_shape = shaped((half_rows // QUERIES, head_width, QUERIES), f32)
    own_top, own_total, own_out, own_done = call(
        attend_own_body,
        [lines, lines, turned_shape],
        [scalars, query, kv_own],
        [pltpu.VMEM((head_width, half_rows), bf16)],
        scalars=1,
    )
    head_slice, head_slice_done = call(
        head_slice_body,
        [shaped((half_rows, router_slice), f32)],
        [scalars, low1_half, head_router_in],
        scalars=1,
    )
    rest_all, _ = call(nothing, [], [], waits=[own_done], passes=[rest_all])
    rest_mine = swap(rest_all, CHIPS)
    grad_blocks = ring_blocks(out_grad)
    attended, log_total, _ = call(
        attend_body,
        [
            shaped((half_rows, head_width), bf16),
            shaped((own_heads * half_rows // QUERIES, 1, QUERIES), f32),
        ],
        [scalars, query, kv_lower, own_top, own_total, own_out, choices],
        [
            pltpu.VMEM((head_width, half_rows), bf16),
            pltpu.VMEM((half_rows // QUERIES, head_width, QUERIES), f32),
        ],
        scalars=1,
        waits=grad_blocks[1:] + [head_slice_done],
    )
    out_lanes = (slice(0, 16), slice(0, 32), slice(3 * head_width, 4 * head_width))
    out_slice, p0, p1, p2, p3, _ = call(
        out_body,
        [shaped((head_width, width), bf16), own_shape] + [part_shape] * 3,
        [scalars, attended, mixer_mine, mixer_theirs],
        [pltpu.VMEM((2, 2, 2, 4, 8, width), f32)],
        scalars=1,
        windows={2: out_lanes, 3: out_lanes},
    )
    attn_pre, middle, low2, rest_mine, _ = call(
        middle_body,
        [own_shape, own_shape, part_shape],
        [p0] + [to_sender(part, k) for k, part in ((1, p1), (2, p2), (3, p3))]
        + [tokens, line(out_bias), head_gate, line(ffn_gain), line(ffn_shift)],
        passes=[rest_mine],
    )
    rest_theirs = other_core(rest_mine)

    up_rows, down_rows = (
        (slice(0, 8), slice(0, 2), slice(*at), slice(0, size))
        for at, size in (((0, 32), width), ((32, 64), width))
    )
    count_rows = (slice(0, 16), slice(64, 72), slice(0, 128))
    rest_mine = rest_mine.reshape(8, 2, 72, width)
    rest_theirs = rest_theirs.reshape(8, 2, 72, width)
    (
        ffn_pre, f1, f2, f3, d_normed2, d1, d2, d3, width_dgate, low2_half, d_up, active_low, d_ffn_half,
        d_up_sum, width_prob, width_gate, width_squash, width_slice, forth_done,
    ) = call(
        feed_body,
        [own_shape] + [part_shape] * 3 + [own_shape] + [sent_shape] * 3
        + [shaped((1, rows), f32), half_shape, shaped((half_rows, units), bf16)]
        + [shaped((half_rows, units), bf16), half_shape, shaped((1, units), f32)]
        + [shaped((rows, 128), f32), shaped((rows, 1), f32), shaped((rows, router_width), f32)]
        + [shaped((half_rows, router_slice), f32)],
        [scalars] + ring_blocks(low2)
        + [rest_mine, rest_theirs, own_up_bias]
        + [width_router_in, width_out]
        + [rest_mine, rest_theirs]
        + grad_blocks + [choices],
        [pltpu.VMEM((8, 2, 2, 32, units), bf16), pltpu.VMEM((2, 2, 2, 4, 32, width), bf16)],
        scalars=1,
        room=48,
        windows={5: up_rows, 6: up_rows, 10: down_rows, 11: down_rows},
    )
    d_received = [to_sender(part, k) for k, part in ((1, d1), (2, d2), (3, d3))]
    feed_mine, feed_theirs, f1, f2, f3, _ = call(
        feed_weight_body,
        [shaped((16, 64, width), bf16)] * 2 + [part_shape] * 3,
        [core_scalar, low2_half, d_up, active_low, d_ffn_half, f1, f2, f3],
        scalars=1,
    )
    payload, d_middle, d_hidden_head, early, share, feed_theirs, payload_done = call(
        own_back_body,
        [sent_shape, own_shape, part_shape, shaped((32, width), f32), shaped((1, 128), f32)],
        [scalars, d_normed2] + d_received
        + [middle, width_router_in, out_grad, width_squash, head_squash, attn_pre]
        + [width_dgate, line(down_bias), width_prob, width_gate, head_prob, head_gate]
        + [line(head_choice), line(width_choice), rest_mine.reshape(16, 72, width), rest_theirs.reshape(16, 72, width)]
        + [width_out, head_out, line(ffn_gain), d_up_sum],
        scalars=1,
        windows={19: count_rows, 20: count_rows},
        passes=[feed_theirs],
    )
    feed_part, feed_done = call(pair_body, [shaped((16, 64, width), bf16)], [feed_mine, other_core(feed_theirs)], cost=0, near=[1], waits=[payload_done])
    feed_pieces = swap(feed_part, CHIPS)
    router_term1 = against(d_hidden_head, head_router_in)

    d_attn_blocks = ring_blocks(payload)
    mixed_mine, mixed_theirs, mixed_done = call(
        mixer_weight_body,
        [shaped((16, 32, width), bf16)] * 2,
        [scalars, low1_half, low2_half, width_slice, head_slice, width_out, head_out, attended]
        + d_attn_blocks
        + [early],
        [
            pltpu.VMEM((half_rows, router_slice), bf16),
            pltpu.VMEM((half_rows, router_slice), bf16),
            pltpu.VMEM((head_width, width), f32),
            pltpu.VMEM((rows, rows), f32),
        ],
        scalars=1,
        waits=[feed_done],
    )
    gradient_scratch = [pltpu.VMEM((half_rows, head_width), f32)] * 2
    d_lower, d_out, d_mean, d_query_lower, d_lower_done = call(
        attend_back_body,
        [
            shaped((half_rows, 2 * head_width), bf16),
            shaped((half_rows, head_width), bf16),
            lines,
            turned_shape,
        ],
        [scalars] + d_attn_blocks + [out_slice, query, kv_lower, choices, log_total, attended],
        [pltpu.VMEM((head_width, half_rows), bf16)] + gradient_scratch,
        scalars=1,
        cost=0,
        waits=[mixed_done],
    )
    back = lax.ppermute(d_lower, "yl", [(1, 0)])
    d_query, d_kv_own, d_query_done = call(
        attend_back_own_body,
        [shaped((half_rows, head_width), bf16), shaped((half_rows, 2 * head_width), f32)],
        [scalars, query, kv_own, log_total, d_out, d_mean, d_query_lower, cosine, sine],
        [
            pltpu.VMEM((head_width, half_rows), bf16),
            pltpu.VMEM((half_rows // QUERIES, head_width, QUERIES), f32),
        ]
        + gradient_scratch,
        scalars=1,
    )
    mixed_part, mixed_part_done = call(
        pair_body,
        [shaped((16, 32, width), bf16)],
        [mixed_mine, other_core(mixed_theirs)],
        cost=0,
        near=[1],
        waits=[d_query_done, feed_pieces],
    )
    mixer_pieces = swap(mixed_part, CHIPS)
    d_mixed, d_own, gain_shift, d_mixed_sum, *d_sent, _ = call(
        project_back_body,
        [
            shaped((half_rows, 3 * head_width), bf16),
            own_shape,
            shaped((2, width), f32),
            shaped((1, 3 * head_width), f32),
        ]
        + [part_shape] * 3,
        [back, d_kv_own, d_query, qkv_slice, cosine, sine] + token_blocks + [router_term1],
        waits=[mixed_part_done],
    )
    d_sent = [to_sender(part, k) for k, part in enumerate(d_sent, 1)]
    result, result_done = call(
        result_body,
        [part_shape],
        [ffn_pre] + [to_sender(part, k) for k, part in ((1, f1), (2, f2), (3, f3))]
        + [line(down_bias), middle, width_gate],
        room=16,
    )
    d_inputs, d_inputs_done = call(
        inputs_body,
        [own_shape],
        [d_own] + d_sent + [tokens, d_middle, line(attn_gain)],
        room=16,
    )

    feed_rows = block_sum(feed_pieces)
    down_grad = lax.ppermute(feed_rows[32:], ("x", "z"), flipped)
    mine, theirs, _ = call(
        project_weight_body,
        [shaped((8, 64, 3 * head_width + 256), bf16)] * 2,
        [scalars, low1_half, d_mixed, d_mixed_sum, gain_shift],
        scalars=1,
    )
    qkv_part, qkv_part_done = call(
        pair_body,
        [shaped((8, 64, 3 * head_width + 256), bf16)],
        [mine, other_core(theirs)],
        cost=0,
        near=[1],
        waits=[mixer_pieces],
    )
    qkv_part = swap(qkv_part.reshape(64, 8, -1), CHIPS + ("z",))
    qkv_grad, late, _ = call(
        project_sum_body,
        [shaped((8, 3 * width), f32), shaped((1, width), f32)],
        [qkv_part],
        near=[0],
    )

    shared, out_rows, _ = call(
        mixer_sum_body,
        [shaped((24, width), bf16), shaped((8, width), f32)],
        [mixer_pieces],
        near=[0],
    )
    out_grad_rows = lax.ppermute(out_rows, ("x", "z"), flipped)
    up_rows = feed_rows[:32].reshape(RING, 8, units).astype(bf16)
    from_ring = []
    for shift in range(RING):
        rows_of = lax.dynamic_index_in_dim(up_rows, (place + shift) % RING, 0, keepdims=False)
        block = jnp.concatenate([shared, rows_of], axis=0)
        if shift:
            block = lax.ppermute(block, "z", [(k, (k + shift) % RING) for k in range(RING)])
        from_ring.append(block)
    from_ring = jnp.take(jnp.stack(from_ring), ring_order, axis=0)
    early_sum = jnp.sum(from_ring[:, 16:24].astype(f32), axis=0).astype(bf16)
    up_grad = jnp.concatenate([from_ring[k, 24:] for k in range(RING)], axis=1).astype(f32)

    lanes = router_slice
    routers = jnp.concatenate(
        [
            jnp.concatenate([from_ring[k, :16, j * lanes : (j + 1) * lanes] for k in range(RING)], axis=1)
            for j in (0, 2, 1, 3)
        ]
        + [early_sum[:4], jnp.broadcast_to(late.astype(bf16), (4, width))],
        axis=0,
    )
    routers_mine = spread(routers, CHIPS, 16)
    routers_mine, _ = call(nothing, [], [], waits=[d_inputs_done, result_done], passes=[routers_mine])
    routers_theirs = other_core(routers_mine)
    vectors = [3 * width, width, RING * units, width, width, width, width, width]
    width_in_grad, head_in_grad, *vectors, head_out_grad, width_out_grad, prob_sums, _ = call(
        routers_body,
        [shaped((width, router_width), f32)] * 2
        + [shaped((1, size), f32) for size in vectors]
        + [shaped((CHOICES, router_width), f32)] * 2
        + [shaped((1, 128), f32)],
        [core_scalar, routers_mine, routers_theirs],
        [pltpu.VMEM((8, 2, 2, 8, width), f32)],
        scalars=1,
        near=[2],
    )
    balance = CHOICES * jnp.sum(share * prob_sums / all_rows)

    return (
        result,
        balance,
        d_inputs,
        qkv_grad,
        out_grad_rows,
        up_grad,
        down_grad,
        *[vector.reshape(-1) for vector in vectors],
        head_in_grad,
        head_out_grad.T,
        width_in_grad,
        width_out_grad.T,
    )


def solution(mesh):
    fine = Mesh(mesh.devices.reshape(4, 2, 2, 2, 4), AXES)
    whole = P(AXES, None)
    vector = P(AXES)
    in_specs = (
        whole, whole, whole, P(), whole, P(), whole, P(), whole, P(),
        P(), P(), P(), P(), P(), P(), P(), P(), vector, vector, vector,
    )
    out_specs = (whole, P(), whole, whole, whole, whole, whole) + (P(),) * 12
    return jax.shard_map(local, mesh=fine, in_specs=in_specs, out_specs=out_specs, check_vma=False)
```

```python
import jax
import jax.numpy as jnp
import numpy as np
from jax import lax
from jax.experimental import pallas as pl
from jax.experimental.pallas import tpu as pltpu
from jax.sharding import Mesh
from jax.sharding import PartitionSpec as P


AXES = ("x", "yh", "c", "yl", "z")
CHIPS = ("x", "yh", "yl")
RING = 4
HEADS = 16
HEAD_DIM = 64
CHOICES = 4
EPS = 1e-05
AUX_WEIGHT = 0.1
BLOCKED = -1e30
bf16 = jnp.bfloat16
f32 = jnp.float32
INTERPRET = False
QUERIES = 512
LONG = 10**10


def dot(former, latter):
    return jnp.dot(former, latter, preferred_element_type=f32)


def against(former, latter):
    return lax.dot_general(former, latter, (((1,), (1,)), ((), ())), preferred_element_type=f32)


def across(former, latter):
    return lax.dot_general(former, latter, (((0,), (0,)), ((), ())), preferred_element_type=f32)


def swap(value, axes):
    return lax.all_to_all(value, axes, split_axis=0, concat_axis=0, tiled=True)


def spread(value, axes, count):
    return swap(jnp.broadcast_to(value[None], (count,) + value.shape), axes)


def other_core(value):
    return lax.ppermute(value, "c", [(0, 1), (1, 0)])


def ring_blocks(value):
    return [value] + [
        lax.ppermute(value, "z", [(k, (k + shift) % RING) for k in range(RING)]) for shift in range(1, RING)
    ]


def to_sender(value, shift):
    return lax.ppermute(value, "z", [(k, (k - shift) % RING) for k in range(RING)])


def ring_product(former, latter, product, rows):
    sent = [
        to_sender(product(former[k * rows : (k + 1) * rows], latter).astype(bf16), k) for k in range(1, RING)
    ]
    total = product(former[:rows], latter)
    for part in sent:
        total = total + part.astype(f32)
    return total


def spread_chips(value):
    mine = spread(value, CHIPS, 16)
    return mine, other_core(mine)


def block_sum(pieces):
    return jnp.sum(pieces.astype(f32), axis=0)


def normalize(values):
    centred = values - jnp.mean(values, axis=-1, keepdims=True)
    inv_std = lax.rsqrt(jnp.mean(centred * centred, axis=-1, keepdims=True) + EPS)
    return (centred * inv_std, inv_std)


def rotary_tables(position):
    lane = jnp.arange(2 * HEAD_DIM)
    half = HEAD_DIM // 2
    freqs = 10000.0 ** (-2.0 * (lane % half).astype(f32) / HEAD_DIM)
    angle = position.astype(f32)[:, None] * freqs[None, :]
    return (jnp.cos(angle), jnp.sin(angle) * jnp.where(lane % HEAD_DIM < half, -1.0, 1.0)[None, :])


def call(body, outs, args, scratch=(), scalars=0, cost=LONG, waits=(), room=24, windows=None, passes=(), near=(), partly=None, into=()):
    outs = list(outs) + [shaped((8, 128), f32)]
    given, taken = len(args), len(args) + len(waits) + len(passes) + len(into)
    partly = partly or {}

    def large(value):
        return int(np.prod(value.shape)) * value.dtype.itemsize >= 65536

    windows = windows or {}

    def shape_in(k):
        if k not in windows:
            return args[k].shape
        return tuple(part.stop - part.start for part in windows[k])

    copied_in = [k for k in range(scalars, given) if large(args[k]) and k not in near]
    copied_out = [k for k in range(len(outs)) if large(outs[k])]
    copies = len(copied_in) + len(copied_out)

    def whole(*refs):
        ins, results = list(refs[:given]), list(refs[taken : taken + len(outs)])
        rest = refs[taken + len(outs) + len(passes) :]
        semaphores, buffers, own = rest[0], rest[1 : 1 + copies], rest[1 + copies :]
        moves = []
        for j, k in enumerate(copied_in):
            source = ins[k].at[windows[k]] if k in windows else ins[k]
            move = pltpu.make_async_copy(source, buffers[j], semaphores.at[j])
            move.start()
            moves.append(move)
            ins[k] = buffers[j]
        for move in moves:
            move.wait()
        targets = list(results)
        for j, k in enumerate(copied_out, len(copied_in)):
            results[k] = buffers[j]
        body(*ins, *results[:-1], *own)
        results[-1][...] = jnp.zeros((8, 128), f32)
        moves = []
        for j, k in enumerate(copied_out, len(copied_in)):
            target = targets[k].at[partly[k][1](refs[0])] if k in partly else targets[k]
            moves.append(pltpu.make_async_copy(buffers[j], target, semaphores.at[j]))
            moves[-1].start()
        for move in moves:
            move.wait()

    def spec(k, copied):
        return pl.BlockSpec(memory_space=pltpu.HBM if k in copied else pltpu.VMEM)

    spaces = [pl.BlockSpec(memory_space=pltpu.SMEM)] * scalars
    spaces += [spec(k, copied_in) for k in range(scalars, given)]
    spaces += [pl.BlockSpec(memory_space=pl.ANY)] * (len(waits) + len(passes) + len(into))
    buffers = [pltpu.VMEM(shape_in(k), args[k].dtype) for k in copied_in]
    buffers += [pltpu.VMEM(partly[k][0] if k in partly else outs[k].shape, outs[k].dtype) for k in copied_out]
    moved = sum(int(np.prod(value.shape)) * value.dtype.itemsize for value in list(args) + list(outs))
    shapes = list(outs) + [shaped(value.shape, value.dtype) for value in passes]
    if not INTERPRET:
        shapes = [
            pltpu.HBM(v.shape, v.dtype) if k in copied_out or k >= len(outs) else v for k, v in enumerate(shapes)
        ]
        args = [pltpu.with_memory_space_constraint(v, pltpu.HBM) if k in copied_in else v for k, v in enumerate(args)]
        passes = [pltpu.with_memory_space_constraint(v, pltpu.HBM) for v in passes]
        into = [pltpu.with_memory_space_constraint(v, pltpu.HBM) for v in into]
    results = pl.pallas_call(
        whole,
        out_shape=tuple(shapes),
        in_specs=spaces,
        out_specs=tuple(spec(k, copied_out) for k in range(len(outs)))
        + tuple(pl.BlockSpec(memory_space=pl.ANY) for _ in passes),
        scratch_shapes=[pltpu.SemaphoreType.DMA((max(copies, 1),))] + buffers + list(scratch),
        input_output_aliases={
            **{given + len(waits) + k: len(outs) + k for k in range(len(passes))},
            **{given + len(waits) + len(passes) + k: k for k in range(len(into))},
        },
        compiler_params=pltpu.CompilerParams(vmem_limit_bytes=room << 20),
        cost_estimate=pl.CostEstimate(flops=cost, bytes_accessed=moved if cost else 0, transcendentals=0),
        interpret=INTERPRET,
    )(*args, *waits, *passes, *into)
    last = len(outs) - 1
    return (*results[:last], *results[last + 1 :], results[last])


def shaped(shape, kind):
    return jax.ShapeDtypeStruct(shape, kind)


def turned(value, cosine, sine):
    lane = lax.broadcasted_iota(jnp.int32, value.shape, 1)
    width = value.shape[1]
    half = HEAD_DIM // 2
    flipped = jnp.where(
        lane % HEAD_DIM < half, pltpu.roll(value, width - half, 1), pltpu.roll(value, half, 1)
    )
    return value * cosine + flipped * sine


def turned_back(value, cosine, sine):
    lane = lax.broadcasted_iota(jnp.int32, value.shape, 1)
    width = value.shape[1]
    half = HEAD_DIM // 2
    moved = value * sine
    flipped = jnp.where(
        lane % HEAD_DIM < half, pltpu.roll(moved, width - half, 1), pltpu.roll(moved, half, 1)
    )
    return value * cosine + flipped


def project_body(core_ref, t0, t1, t2, t3, gain, shift, mine, theirs, bias, cosine, sine, low_ref, query_ref, kv_ref, weight_ref):
    core = core_ref[0]
    lanes = weight_ref.shape[-1]
    weight_ref[:, pl.ds(core, 1)] = mine[:, :, :lanes][:, None]
    weight_ref[:, pl.ds(1 - core, 1)] = theirs[:, :, :lanes][:, None]
    weight = weight_ref[...].reshape(-1, weight_ref.shape[-1])
    rows = t0.shape[0]
    heads = query_ref.shape[1]
    for k, block in enumerate((t0, t1, t2, t3)):
        at = slice(k * rows, (k + 1) * rows)
        unit, _ = normalize(block[...].astype(f32))
        low = (unit * gain[...] + shift[...]).astype(bf16)
        low_ref[at, :] = low
        mixed = dot(low, weight) + bias[...]
        for j in range(heads // 128):
            lanes = slice(128 * j, 128 * (j + 1))
            query_ref[at, lanes] = turned(mixed[:, lanes], cosine[at, :], sine[at, :]).astype(bf16)
            key = mixed[:, heads + 128 * j : heads + 128 * (j + 1)]
            kv_ref[at, lanes] = turned(key, cosine[at, :], sine[at, :]).astype(bf16)
        kv_ref[at, heads:] = mixed[:, 2 * heads :].astype(bf16)


def kept_row(choice_ref, which, place, k):
    chosen = choice_ref[(place + RING - k) % RING, which : which + 1, :].astype(f32)
    return jnp.where(chosen >= place.astype(f32), 1.0, 0.0)


def column(row):
    return jnp.broadcast_to(row, (row.shape[1], row.shape[1])).T[:, :1]


def order_of(shape, axis, place, first=0):
    at = lax.broadcasted_iota(jnp.int32, shape, axis) + first
    return ((place + RING - at // 128) % RING) * 128 + at % 128


def own_part(h, query):
    lane = lax.broadcasted_iota(jnp.int32, query.shape, 1)
    return jnp.where(lane // HEAD_DIM == h, query, jnp.zeros_like(query)) * jnp.asarray(HEAD_DIM ** (-0.5), bf16)


def masked(score, own, flag, place, q_block):
    if not own:
        return jnp.where(flag, score, BLOCKED)
    keys = order_of((score.shape[0], 1), 0, place)
    return jnp.where(keys <= order_of((1, score.shape[1]), 1, place, q_block * QUERIES), score, BLOCKED)


def loop(heads, queries, step):
    blocks = queries // QUERIES

    def one(at, carry):
        h, q_block = at // blocks, at % blocks
        here = pl.ds(pl.multiple_of(q_block * QUERIES, QUERIES), QUERIES)
        features = pl.ds(pl.multiple_of(h * HEAD_DIM, HEAD_DIM), HEAD_DIM)
        step(at, h, q_block, here, features)
        return carry

    lax.fori_loop(0, blocks * (heads // HEAD_DIM), one, 0)


def attend_own_body(scalars, query_ref, kv_ref, top_ref, total_ref, out_ref, value_turned):
    heads = query_ref.shape[1]
    value_turned[...] = kv_ref[:, heads:].T
    flag, place = scalars[2] == 1, scalars[1]

    def step(at, h, q_block, here, features):
        score = against(kv_ref[:, :heads], own_part(h, query_ref[here, :]))
        score = masked(score, True, flag, place, q_block)
        top = jnp.max(score, axis=0, keepdims=True)
        expo = jnp.exp(score - top)
        top_ref[at] = top
        total_ref[at] = jnp.sum(expo, axis=0, keepdims=True)
        out_ref[q_block, features, :] = dot(value_turned[features, :], expo.astype(bf16))

    loop(heads, query_ref.shape[0], step)


def attend_body(
    scalars, query_ref, kv_ref, own_top, own_total, own_out, choice_ref, out_ref, total_ref, value_turned, out_turned,
):
    heads = query_ref.shape[1]
    value_turned[...] = kv_ref[:, heads:].T
    flag, place = scalars[2] == 1, scalars[1]

    def step(at, h, q_block, here, features):
        score = against(kv_ref[:, :heads], own_part(h, query_ref[here, :]))
        score = masked(score, False, flag, place, q_block)
        top = jnp.maximum(jnp.max(score, axis=0, keepdims=True), own_top[at])
        expo = jnp.exp(score - top)
        factor = jnp.exp(own_top[at] - top)
        total = jnp.sum(expo, axis=0, keepdims=True) + factor * own_total[at]
        total_ref[at] = top + jnp.log(total)
        out = dot(value_turned[features, :], expo.astype(bf16)) + factor * own_out[q_block, features, :]
        out_turned[q_block, features, :] = out / total

    loop(heads, query_ref.shape[0], step)
    for k in range(query_ref.shape[0] // QUERIES):
        at = slice(k * QUERIES, (k + 1) * QUERIES)
        each = QUERIES // 128
        keep = jnp.concatenate([kept_row(choice_ref, 0, place, each * k + j) for j in range(each)], axis=1)
        out_ref[at, :] = (out_turned[k] * keep).T.astype(bf16)


def back_step(own, scalars, query_ref, kv_ref, total_ref, d_out, mean_ref, key_turned, d_query_turned, d_key, d_value):
    heads = query_ref.shape[1]
    flag, place = scalars[2] == 1, scalars[1]

    def step(at, h, q_block, here, features):
        query = own_part(h, query_ref[here, :])
        score = masked(against(kv_ref[:, :heads], query), own, flag, place, q_block)
        prob = jnp.exp(score - total_ref[at])
        gradient = d_out[here, :]
        lane = lax.broadcasted_iota(jnp.int32, gradient.shape, 1)
        gradient = jnp.where(lane // HEAD_DIM == h, gradient, jnp.zeros_like(gradient))
        d_value[...] += dot(prob.astype(bf16), gradient)
        d_score = (prob * (against(kv_ref[:, heads:], gradient) - mean_ref[at])).astype(bf16)
        d_key[...] += dot(d_score, query)
        d_query = dot(key_turned[features, :], d_score) * (HEAD_DIM ** (-0.5))
        if own:
            d_query += d_query_turned[q_block, features, :]
        d_query_turned[q_block, features, :] = d_query

    return step


def attend_back_body(
    scalars, g0, g1, g2, g3, out_slice, query_ref, kv_ref, choice_ref, total_ref, attended,
    send_ref, d_out, mean_ref, d_query_turned, key_turned, d_key, d_value,
):
    heads = query_ref.shape[1]
    rows = query_ref.shape[0] // RING
    place = scalars[1]
    blocks = query_ref.shape[0] // QUERIES
    key_turned[...] = kv_ref[:, :heads].T
    d_key[...] = jnp.zeros_like(d_key)
    d_value[...] = jnp.zeros_like(d_value)
    for k, block in enumerate((g0, g1, g2, g3)):
        at = slice(k * rows, (k + 1) * rows)
        part = against(block[:rows, :], out_slice[...])
        d_out[at, :] = (part * column(kept_row(choice_ref, 0, place, k))).astype(bf16)
    for k in range(blocks):
        at = slice(k * QUERIES, (k + 1) * QUERIES)
        product = (d_out[at, :].astype(f32) * attended[at, :].astype(f32)).T
        for h in range(heads // HEAD_DIM):
            part = product[h * HEAD_DIM : (h + 1) * HEAD_DIM]
            mean_ref[h * blocks + k] = jnp.sum(part, axis=0, keepdims=True)
    loop(
        heads,
        query_ref.shape[0],
        back_step(
            False, scalars, query_ref, kv_ref, total_ref, d_out, mean_ref, key_turned, d_query_turned, d_key, d_value
        ),
    )
    send_ref[:, :heads] = d_key[...].astype(bf16)
    send_ref[:, heads:] = d_value[...].astype(bf16)


def attend_back_own_body(
    scalars, query_ref, kv_ref, total_ref, d_out, mean_ref, lower, cosine, sine,
    d_query_ref, own_ref, key_turned, d_query_turned, d_key, d_value,
):
    heads = query_ref.shape[1]
    key_turned[...] = kv_ref[:, :heads].T
    d_query_turned[...] = lower[...]
    d_key[...] = jnp.zeros_like(d_key)
    d_value[...] = jnp.zeros_like(d_value)
    loop(
        heads,
        query_ref.shape[0],
        back_step(
            True, scalars, query_ref, kv_ref, total_ref, d_out, mean_ref, key_turned, d_query_turned, d_key, d_value
        ),
    )
    own_ref[:, :heads] = d_key[...]
    own_ref[:, heads:] = d_value[...]
    for k in range(query_ref.shape[0] // QUERIES):
        at = slice(k * QUERIES, (k + 1) * QUERIES)
        value = d_query_turned[k].T
        for j in range(heads // 128):
            lanes = slice(128 * j, 128 * (j + 1))
            d_query_ref[at, lanes] = turned_back(value[:, lanes], cosine[at, :], sine[at, :]).astype(bf16)


def head_slice_body(scalars, low, router_in, slice_ref):
    size = slice_ref.shape[1]
    lanes = pl.ds(pl.multiple_of(scalars[1] * size, size), size)
    slice_ref[...] = jnp.tanh(dot(low[...], router_in[:, lanes]))


def project_back_body(
    back_ref, own_ref, d_query_ref, weight, cosine, sine, t0, t1, t2, t3, term_ref,
    mixed_ref, total_ref, sums_ref, bias_ref, p1, p2, p3,
):
    heads = d_query_ref.shape[1]
    rows = t0.shape[0]
    gain_sum = jnp.zeros((1, t0.shape[1]), f32)
    shift_sum = jnp.zeros((1, t0.shape[1]), f32)
    bias_sum = jnp.zeros((1, 3 * heads), f32)
    for k, (block, part) in enumerate(((t1, p1), (t2, p2), (t3, p3), (t0, total_ref)), 1):
        k = k % RING
        at = slice(k * rows, (k + 1) * rows)
        mixed_ref[at, :heads] = d_query_ref[at, :]
        for j in range(heads // 128):
            lanes = slice(128 * j, 128 * (j + 1))
            value = own_ref[at, lanes] + back_ref[at, lanes].astype(f32)
            mixed_ref[at, heads + 128 * j : heads + 128 * (j + 1)] = turned_back(
                value, cosine[at, :], sine[at, :]
            ).astype(bf16)
        mixed_ref[at, 2 * heads :] = (own_ref[at, heads:] + back_ref[at, heads:].astype(f32)).astype(bf16)
        mixed = mixed_ref[at, :]
        bias_sum += jnp.sum(mixed.astype(f32), axis=0, keepdims=True)
        gradient = against(mixed, weight[...])
        if k == 0:
            gradient = gradient + term_ref[...]
        part[...] = gradient.astype(part.dtype)
        unit, _ = normalize(block[...].astype(f32))
        gain_sum += jnp.sum(gradient * unit, axis=0, keepdims=True)
        shift_sum += jnp.sum(gradient, axis=0, keepdims=True)
    sums_ref[0:1, :] = gain_sum
    sums_ref[1:2, :] = shift_sum
    bias_ref[...] = bias_sum


def project_weight_body(scalars, low_ref, mixed_ref, bias_ref, sums_ref, mine_ref, theirs_ref):
    core, place = scalars[0], scalars[1]
    size = bias_ref.shape[1] // 3
    row = lax.broadcasted_iota(jnp.int32, (8, size), 0)
    late = [jnp.where(row == place, bias_ref[:, size * k : size * (k + 1)], 0.0) for k in range(3)]
    for k in range(2):
        block = jnp.zeros((8, size), f32)
        for j in range(RING):
            block = jnp.where(row == j, sums_ref[k : k + 1, size * j : size * (j + 1)], block)
        late.append(block)
    late += [jnp.zeros((8, size), f32)] * 3
    lanes = mixed_ref.shape[1]
    for k in range(8):
        turned_low = low_ref[:, 128 * k : 128 * (k + 1)].T
        mine, theirs = halves(core, dot(turned_low, mixed_ref[...]))
        mine_ref[k, :, :lanes] = mine.astype(bf16)
        theirs_ref[k, :, :lanes] = theirs.astype(bf16)
        for j in range(2):
            at = slice(32 * j, 32 * (j + 1))
            if k >= 2:
                mine_ref[k, at, lanes:] = jnp.zeros((32, size), bf16)
                theirs_ref[k, at, lanes:] = jnp.zeros((32, size), bf16)
                continue
            mine, theirs = halves(core, jnp.concatenate([late[4 * k + j], late[4 * k + 2 + j]], axis=0))
            mine_ref[k, at, lanes:] = jnp.concatenate([mine] * RING, axis=0).astype(bf16)
            theirs_ref[k, at, lanes:] = jnp.concatenate([theirs] * RING, axis=0).astype(bf16)


def halves(core, part):
    half = part.shape[0] // 2
    first, second = part[:half], part[half:]
    return jnp.where(core == 0, first, second), jnp.where(core == 0, second, first)


def assemble(core, target, mine, theirs):
    target[:, pl.ds(core, 1)] = mine[...][:, None]
    target[:, pl.ds(1 - core, 1)] = theirs[...][:, None]
    return target[...].reshape(-1, target.shape[-1])


def pack_body(qkv, up, head_choice, width_choice, packed_ref):
    heads = qkv.shape[1] // 3 // RING
    units = up.shape[1] // RING
    row = lax.broadcasted_iota(jnp.int32, (8, head_choice.shape[1]), 0)
    choices = jnp.where(
        row == 0, head_choice[...].astype(f32), jnp.where(row == 1, width_choice[...].astype(f32), 0.0)
    ).astype(bf16)
    for z in range(RING):
        for j in range(3):
            packed_ref[z, :, j * heads : (j + 1) * heads] = qkv[:, (j * RING + z) * heads : (j * RING + z + 1) * heads]
        packed_ref[z, :, 3 * heads : 3 * heads + units] = up[:, z * units : (z + 1) * units]
        packed_ref[z, :, 3 * heads + units :] = choices


def head_body(tokens, gain, shift, router_in, router_out, choice, squash_ref, prob_ref, gate_ref):
    unit, _ = normalize(tokens[...].astype(f32))
    low = (unit * gain[...] + shift[...]).astype(bf16)
    squash = jnp.tanh(dot(low, router_in[...]))
    squash_ref[...] = squash
    logit = dot(squash.astype(bf16), router_out[...])
    lane = lax.broadcasted_iota(jnp.int32, logit.shape, 1)
    logit = jnp.where(lane < CHOICES, logit, BLOCKED)
    expo = jnp.exp(logit - jnp.max(logit, axis=-1, keepdims=True))
    prob = expo / jnp.sum(expo, axis=-1, keepdims=True)
    prob_ref[...] = prob
    gate_ref[...] = jnp.sum(
        jnp.where(lane.astype(f32) == column(choice[...].astype(f32)), prob, 0.0), axis=-1, keepdims=True
    )


def mixer_body(pieces, out_rows, mixer_ref):
    size = mixer_ref.shape[2] // RING
    for k in range(mixer_ref.shape[0]):
        for j in range(RING):
            at = slice(8 * j, 8 * (j + 1))
            mixer_ref[k, at, : 3 * size] = pieces[j, :, : 3 * size]
            mixer_ref[k, at, 3 * size :] = out_rows[:, j * size : (j + 1) * size]


def count_body(choice_ref, pieces, down, rest_ref):
    lane = lax.broadcasted_iota(jnp.int32, (1, rest_ref.shape[2]), 1)
    line = jnp.zeros((1, rest_ref.shape[2]), f32)
    for which in range(2):
        chosen = choice_ref[:, which, :].astype(f32)
        for option in range(CHOICES):
            count = jnp.sum(jnp.where(chosen == option, 1.0, 0.0), axis=1, keepdims=True)
            count = jnp.sum(count, axis=0, keepdims=True)
            pairs = jnp.floor(count * 0.5)
            at = which * CHOICES + option
            line = jnp.where(lane == at, pairs, line)
            line = jnp.where(lane == at + 2 * CHOICES, count - 2.0 * pairs, line)
    last = jnp.broadcast_to(line, (8, rest_ref.shape[2])).astype(bf16)
    heads = (pieces.shape[2] - rest_ref.shape[2] - choice_ref.shape[2]) // 3
    for k in range(rest_ref.shape[0]):
        for j in range(RING):
            rest_ref[k, 8 * j : 8 * (j + 1)] = pieces[j, :, 3 * heads : 3 * heads + rest_ref.shape[2]]
        rest_ref[k, 32:64] = down[...]
        rest_ref[k, 64:] = last


def out_body(scalars, attended, mine, theirs, slice_ref, p0, p1, p2, p3, full):
    core = scalars[0]
    size = mine.shape[-1]
    for x in range(4):
        for yh in range(2):
            for yl in range(2):
                at = (x * 2 + yh) * 2 + yl
                for k in range(4):
                    rows, lanes = slice(8 * k, 8 * (k + 1)), slice(size * k, size * (k + 1))
                    full[yh, pl.ds(core, 1), yl, x, :, lanes] = mine[at : at + 1, rows].astype(f32)
                    full[yh, pl.ds(1 - core, 1), yl, x, :, lanes] = theirs[at : at + 1, rows].astype(f32)
    weight = full[...].reshape(slice_ref.shape).astype(bf16)
    slice_ref[...] = weight
    rows = p0.shape[0]
    for k, part in ((1, p1), (2, p2), (3, p3), (0, p0)):
        part[...] = dot(attended[k * rows : (k + 1) * rows, :], weight).astype(part.dtype)


def middle_body(p0, r1, r2, r3, tokens, bias, gate, gain, shift, attn_pre_ref, middle_ref, low_ref):
    total = p0[...]
    for part in (r1, r2, r3):
        total = total + part[...].astype(f32)
    total = total + bias[...]
    attn_pre_ref[...] = total
    middle = tokens[...].astype(f32) + gate[...] * total
    middle_ref[...] = middle
    unit, _ = normalize(middle)
    low_ref[...] = (unit * gain[...] + shift[...]).astype(bf16)


def slice_of(value, place, size):
    part = value[:, :size]
    for k in range(1, RING):
        part = jnp.where(place == k, value[:, k * size : (k + 1) * size], part)
    return part


def feed_body(
    scalars, n0, n1, n2, n3, up_mine, up_theirs, up_bias, router_in, router_out, down_mine, down_theirs,
    g0, g1, g2, g3, choice_ref,
    f0, f1, f2, f3, d0, d1, d2, d3, dgate_ref, low_ref, d_up_ref, active_ref, d_ffn_ref, up_sum_ref,
    prob_ref, gate_ref, squash_ref, slice_ref, up_full, down_full,
):
    core, place = scalars[0], scalars[1]
    up = assemble(core, up_full, up_mine, up_theirs)
    for x in range(4):
        for yh in range(2):
            for yl in range(2):
                down_full[yh, pl.ds(core, 1), yl, x] = down_mine[2 * x + yh, yl : yl + 1]
                down_full[yh, pl.ds(1 - core, 1), yl, x] = down_theirs[2 * x + yh, yl : yl + 1]
    down = down_full[...].reshape(-1, down_full.shape[-1])
    rows = n0.shape[0]
    units = up_bias.shape[1]
    router_slice = slice_ref.shape[1]
    up_sum = jnp.zeros((1, units), f32)
    for blocks in (((1, n1, g1, f1, d1), (2, n2, g2, f2, d2)), ((3, n3, g3, f3, d3), (0, n0, g0, f0, d0))):
        low = jnp.concatenate([block[1][...] for block in blocks], axis=0)
        keep_row = [kept_row(choice_ref, 1, place, block[0]) for block in blocks]
        keep = jnp.concatenate([column(row) for row in keep_row], axis=0)
        chosen = jnp.concatenate(
            [column(choice_ref[(place + RING - block[0]) % RING, 1:2, :].astype(f32)) for block in blocks], axis=0
        )
        upward = dot(low, up) + up_bias[...]
        active = jnp.maximum(upward, 0.0) * keep
        active_low = (active * active).astype(bf16)
        squash = jnp.tanh(dot(low, router_in[...]))
        logit = dot(squash.astype(bf16), router_out[...])
        lane = lax.broadcasted_iota(jnp.int32, logit.shape, 1)
        logit = jnp.where(lane // CHOICES == 1, logit, BLOCKED)
        expo = jnp.exp(logit - jnp.max(logit, axis=-1, keepdims=True))
        prob = expo / jnp.sum(expo, axis=-1, keepdims=True)
        gate = jnp.sum(jnp.where((lane - CHOICES).astype(f32) == chosen, prob, 0.0), axis=-1, keepdims=True)
        part = slice_of(squash, place, router_slice)
        ffn_part = dot(active_low, down)
        grad_out = jnp.concatenate([block[2][...] for block in blocks], axis=0).astype(f32)
        dgate = jnp.sum(grad_out * ffn_part, axis=-1, keepdims=True)
        d_ffn = (gate * grad_out).astype(bf16)
        d_up = (against(d_ffn, down) * 2.0 * active).astype(bf16)
        up_sum += jnp.sum(d_up.astype(f32), axis=0, keepdims=True)
        d_normed = against(d_up, up)
        for j, (k, _, _, ffn, d_block) in enumerate(blocks):
            at, here = slice(k * rows, (k + 1) * rows), slice(j * rows, (j + 1) * rows)
            low_ref[at, :] = low[here]
            active_ref[at, :] = active_low[here]
            slice_ref[at, :] = part[here]
            d_ffn_ref[at, :] = d_ffn[here]
            d_up_ref[at, :] = d_up[here]
            ffn[...] = ffn_part[here].astype(ffn.dtype)
            d_block[:rows, :] = d_normed[here].astype(d_block.dtype)
            line = jnp.broadcast_to(dgate[here], (rows, rows)).T[:1]
            if k == 0:
                dgate_ref[...] = line
                squash_ref[...] = squash[here]
                prob_ref[...] = prob[here]
                gate_ref[...] = gate[here]
            else:
                upper = line.astype(bf16).astype(f32)
                row = lax.broadcasted_iota(jnp.int32, (8, rows), 0)
                lines = jnp.where(row == 0, upper, jnp.where(row == 1, line - upper, 0.0)).astype(bf16)
                d_block[rows:, :] = jnp.concatenate([lines] * (units // rows), axis=1)
    up_sum_ref[...] = up_sum


def feed_weight_body(
    core_ref, low_ref, d_up_ref, active_ref, d_ffn_ref, p1, p2, p3, mine_ref, theirs_ref, f1, f2, f3
):
    core = core_ref[0]
    for ffn, part in ((f1, p1), (f2, p2), (f3, p3)):
        ffn[...] = part[...]
    for k in range(8):
        turned_low = low_ref[:, 128 * k : 128 * (k + 1)].T
        mine, theirs = halves(core, dot(turned_low, d_up_ref[...]))
        for j in range(2):
            mine_ref[2 * k + j, :32, :] = mine[32 * j : 32 * (j + 1)].astype(bf16)
            theirs_ref[2 * k + j, :32, :] = theirs[32 * j : 32 * (j + 1)].astype(bf16)
    for yh in range(2):
        for yl in range(2):
            for target, side in ((mine_ref, core), (theirs_ref, 1 - core)):
                lanes = pl.ds(pl.multiple_of(((yh * 2 + side) * 2 + yl) * 128, 128), 128)
                part = dot(active_ref[:, lanes].T, d_ffn_ref[...]).astype(bf16)
                for x in range(4):
                    target[(x * 2 + yh) * 2 + yl, 32:, :] = part[32 * x : 32 * (x + 1)]


def pair_body(mine, theirs, sum_ref):
    sum_ref[...] = (mine[...].astype(f32) + theirs[...].astype(f32)).astype(bf16)


def nothing(*refs):
    pass


def own_back_body(
    scalars, d0, r1, r2, r3, middle_ref, router_in, grad_ref, squash_ref, head_squash_ref, attn_pre_ref,
    dgate_ref, down_bias, prob_ref, gate_ref, head_prob_ref, head_gate_ref, head_choice, width_choice,
    counts_mine, counts_theirs, width_out, head_out, gain, up_sum,
    payload_ref, d_middle_ref, d_hidden_ref, early_ref, share_ref,
):
    place = scalars[1]
    rows = grad_ref.shape[0]
    units = up_sum.shape[1]
    aux = AUX_WEIGHT * CHOICES / (128.0 * rows)
    grad_out = grad_ref[...].astype(f32)
    d_normed = d0[...]
    line = dgate_ref[...]
    for part in (r1, r2, r3):
        d_normed = d_normed + part[:rows, :].astype(f32)
        lines = part[rows:, :rows].astype(f32)
        line = line + lines[:1] + lines[1:2]
    dgate = column(line) + jnp.sum(grad_out * down_bias[...], axis=-1, keepdims=True)
    pairs = jnp.sum(counts_mine[...].astype(f32) + counts_theirs[...].astype(f32), axis=0)[:1]
    share = (2.0 * pairs + pltpu.roll(pairs, 128 - 2 * CHOICES, 1)) / (128.0 * rows)
    share_ref[...] = share
    at = lax.broadcasted_iota(jnp.int32, share.shape, 1)
    lane = lax.broadcasted_iota(jnp.int32, prob_ref.shape, 1).astype(f32)

    def d_logits(which, prob, choice, dgate):
        picked = jnp.where(lane - which * CHOICES == column(choice[...].astype(f32)), dgate, 0.0)
        d_prob = picked + aux * jnp.where(at // CHOICES == which, share, 0.0)
        return prob * (d_prob - jnp.sum(prob * d_prob, axis=-1, keepdims=True))

    d_width = d_logits(1, prob_ref[...], width_choice, dgate)
    squash = squash_ref[...]
    d_hidden = (against(d_width.astype(bf16), width_out[...]) * (1.0 - squash * squash)).astype(bf16)
    d_normed = d_normed + against(d_hidden, router_in[...])
    unit, inv_std = normalize(middle_ref[...])
    scaled = d_normed * gain[...]
    inner = (
        scaled
        - jnp.mean(scaled, axis=-1, keepdims=True)
        - unit * jnp.mean(scaled * unit, axis=-1, keepdims=True)
    )
    d_middle = inner * inv_std + grad_out
    d_middle_ref[...] = d_middle
    head_dgate = jnp.sum(d_middle * attn_pre_ref[...], axis=-1, keepdims=True)
    d_attn = (head_gate_ref[...] * d_middle).astype(bf16)
    payload_ref[:rows, :] = d_attn
    d_head = d_logits(0, head_prob_ref[...], head_choice, head_dgate)
    head_squash = head_squash_ref[...]
    d_hidden_ref[...] = (against(d_head.astype(bf16), head_out[...]) * (1.0 - head_squash * head_squash)).astype(bf16)
    d_logit = (d_head + d_width).T[:8].astype(bf16)
    payload_ref[rows:, :] = jnp.concatenate([d_logit] * (units // rows), axis=1)
    row = lax.broadcasted_iota(jnp.int32, (8, units), 0)
    d_ffn = (gate_ref[...] * grad_out).astype(bf16).astype(f32)
    vectors = (
        jnp.sum(d_attn.astype(f32), axis=0, keepdims=True),
        jnp.sum(d_ffn, axis=0, keepdims=True),
        jnp.sum(d_normed * unit, axis=0, keepdims=True),
        jnp.sum(d_normed, axis=0, keepdims=True),
    )
    first = dot(d_logit, head_squash.astype(bf16))
    second = dot(d_logit, squash.astype(bf16))
    block = jnp.where(row < CHOICES, first, second)
    early_ref[0:8, :] = block
    block = jnp.zeros((8, units), f32)
    for k, vector in enumerate(vectors):
        block = jnp.where(row == k, vector, block)
    for k in range(RING):
        block = jnp.where(row == RING + k, jnp.where(place == k, up_sum[...], 0.0), block)
    early_ref[8:16, :] = block
    probs = jnp.sum(head_prob_ref[...] + prob_ref[...], axis=0, keepdims=True)
    early_ref[16:24, :] = jnp.broadcast_to(jnp.concatenate([probs] * (units // 128), axis=1), (8, units))
    early_ref[24:32, :] = jnp.zeros((8, units), f32)


def mixer_weight_body(
    scalars, low1, low2, width_slice, head_slice, width_out, head_out, attended, g0, g1, g2, g3, early,
    mine_ref, theirs_ref, d_width, d_head, part_ref, logit_ref,
):
    core, place = scalars[0], scalars[1]
    rows = attended.shape[0] // RING
    size = width_slice.shape[1]
    here = pl.ds(pl.multiple_of(place * size, size), size)
    logit_ref[...] = jnp.zeros_like(logit_ref)
    for k, block in enumerate((g0, g1, g2, g3)):
        at = slice(k * rows, (k + 1) * rows)
        logit_ref[:8, :] = block[rows:, :rows].astype(f32)
        logit = logit_ref[...].T.astype(bf16)
        for target, weight, slices in ((d_width, width_out, width_slice), (d_head, head_out, head_slice)):
            squash = slices[at, :]
            target[at, :] = (against(logit, weight[here, :]) * (1.0 - squash * squash)).astype(bf16)
    for k in range(8):
        lanes = slice(128 * k, 128 * (k + 1))
        for first, former, latter in ((0, low2, d_width), (size, low1, d_head)):
            mine, theirs = halves(core, dot(former[:, lanes].T, latter[...]))
            for j in range(2):
                for half in range(2):
                    at = slice(32 * j + 16 * half, 32 * j + 16 * (half + 1))
                    to = slice(2 * size * half + first, 2 * size * half + first + size)
                    mine_ref[2 * k + j, 0:16, to] = mine[at].astype(bf16)
                    theirs_ref[2 * k + j, 0:16, to] = theirs[at].astype(bf16)
    turned_out = attended[...].T
    part = dot(turned_out[:, :rows], g0[:rows, :])
    for k, block in ((1, g1), (2, g2), (3, g3)):
        part += dot(turned_out[:, k * rows : (k + 1) * rows], block[:rows, :])
    part_ref[...] = part
    for x in range(4):
        for yh in range(2):
            for yl in range(2):
                to = (x * 2 + yh) * 2 + yl
                base = 2 * yh * 64 + (4 * yl + x) * 8
                at = (x * 2 + yh) * 4 + yl
                first = jnp.broadcast_to(early[at : at + 1, :], (8, early.shape[1]))
                second = jnp.broadcast_to(early[at + 2 : at + 3, :], (8, early.shape[1]))
                for target, side in ((mine_ref, core), (theirs_ref, 1 - core)):
                    out = part_ref[pl.ds(pl.multiple_of(base + side * 64, 8), 8), :]
                    vector = jnp.where(side == 0, first, second)
                    target[to, 16:32, :] = jnp.concatenate([out, vector], axis=0).astype(bf16)


def mixer_sum_body(pieces, shared_ref, out_ref):
    rows = jnp.sum(pieces[...].astype(f32), axis=0)
    shared_ref[:16, :] = rows[:16].astype(bf16)
    shared_ref[16:, :] = rows[24:].astype(bf16)
    out_ref[...] = rows[16:24]


def project_sum_body(pieces, grad_ref, late_ref):
    late = jnp.zeros((8, late_ref.shape[1] // RING), f32)
    heads = grad_ref.shape[1] // 3 // RING
    for z in range(RING):
        part = pieces[z].astype(f32)
        for k in range(1, 16):
            part = part + pieces[k * RING + z].astype(f32)
        for j in range(3):
            grad_ref[:, (j * RING + z) * heads : (j * RING + z + 1) * heads] = part[:, j * heads : (j + 1) * heads]
        late = late + part[:, 3 * heads :]
    late_ref[...] = jnp.concatenate([late[k : k + 1] for k in range(RING)], axis=1)


def unpack(source, width_ref, head_ref, early_ref):
    rows = source.shape[1] // 9 * 4
    for k in range(2):
        at = slice(k * rows, (k + 1) * rows)
        for j in range(8):
            width_ref[j, 0, at, :] = source[2 * j + k, :rows, :].astype(f32)
            head_ref[j, 0, at, :] = source[2 * j + k, rows : 2 * rows, :].astype(f32)
            early_ref[j, k] = source[2 * j + k, 2 * rows :, :].astype(f32)


def routers_own_body(core_ref, mine, width_ref, head_ref, early_ref):
    unpack(mine, width_ref, head_ref, early_ref)


def routers_body(
    core_ref, theirs, early_mine, width_ref, head_ref, qkv_ref, out_ref, up_ref, down_ref, attn_gain_ref, attn_shift_ref,
    ffn_gain_ref, ffn_shift_ref, head_out_ref, width_out_ref, prob_ref, early, full,
):
    core = core_ref[0]
    unpack(theirs, width_ref, head_ref, early)
    full[:, pl.ds(core, 1)] = early_mine[...][:, None]
    full[:, pl.ds(1 - core, 1)] = early[...][:, None]

    def vector(at, late=0):
        return full[at // 4, at // 2 % 2, at % 2, late : late + 1, :]

    size = full.shape[-1]
    for k in range(3):
        qkv_ref[:, k * size : (k + 1) * size] = vector(k, 4)
    attn_gain_ref[...] = vector(3, 4)
    attn_shift_ref[...] = vector(4, 4)
    out_ref[...] = vector(8)
    down_ref[...] = vector(9)
    ffn_gain_ref[...] = vector(10)
    ffn_shift_ref[...] = vector(11)
    for k in range(RING):
        up_ref[:, k * size : (k + 1) * size] = vector(12 + k)
    prob_ref[...] = vector(16)[:, :128]
    head_out_ref[...] = jnp.concatenate([vector(k) for k in range(CHOICES)], axis=0)
    width_out_ref[...] = jnp.concatenate([vector(CHOICES + k) for k in range(CHOICES)], axis=0)


def result_body(ffn, r1, r2, r3, bias, middle, gate, result_ref):
    total = ffn[...]
    for part in (r1, r2, r3):
        total = total + part[...].astype(f32)
    result_ref[...] = (middle[...] + gate[...] * (total + bias[...])).astype(bf16)


def inputs_body(d_own, r1, r2, r3, tokens, d_middle, gain, d_inputs_ref):
    gradient = d_own[...]
    for part in (r1, r2, r3):
        gradient = gradient + part[...].astype(f32)
    unit, inv_std = normalize(tokens[...].astype(f32))
    scaled = gradient * gain[...]
    inner = (
        scaled
        - jnp.mean(scaled, axis=-1, keepdims=True)
        - unit * jnp.mean(scaled * unit, axis=-1, keepdims=True)
    )
    d_inputs_ref[...] = inner * inv_std + d_middle[...]


def local(
    tokens,
    out_grad,
    qkv_weight,
    qkv_bias,
    out_weight,
    out_bias,
    up_weight,
    up_bias,
    down_weight,
    down_bias,
    attn_gain,
    attn_shift,
    ffn_gain,
    ffn_shift,
    head_router_in,
    head_router_out,
    width_router_in,
    width_router_out,
    head_choice,
    width_choice,
    seq_ids,
):
    rows, width = tokens.shape
    half_rows = RING * rows
    own_heads = HEADS // RING
    head_width = own_heads * HEAD_DIM
    units = up_weight.shape[1] // RING
    router_width = head_router_in.shape[1]
    router_slice = router_width // RING
    all_rows = rows * 128
    core = lax.axis_index("c").astype(jnp.int32)
    place = lax.axis_index("z").astype(jnp.int32)
    one_sequence = (lax.axis_index("yl") == 1) & (seq_ids[0] % 2 == 0)
    core_scalar = core.reshape(1)
    scalars = jnp.stack([core, place, one_sequence.astype(jnp.int32)])
    flipped = [(a * 4 + b, b * 4 + a) for a in range(4) for b in range(4)]
    own_shape = shaped((rows, width), f32)
    part_shape = shaped((rows, width), bf16)
    half_shape = shaped((half_rows, width), bf16)
    sent_shape = shaped((rows + 8, width), bf16)

    def line(vector):
        return vector.reshape(1, -1)

    out_swapped = lax.ppermute(out_weight, ("x", "z"), flipped)
    down_swapped = lax.ppermute(down_weight, ("x", "z"), flipped)
    packed, _ = call(
        pack_body,
        [shaped((RING, 8, 3 * head_width + units + rows), bf16)],
        [qkv_weight, up_weight, line(head_choice), line(width_choice)],
        room=16,
    )
    ring_order = (place - jnp.arange(RING)) % RING
    order = (ring_order[:, None] * rows + jnp.arange(rows)[None, :]).reshape(half_rows)
    cosine, sine = rotary_tables(order + jnp.where(one_sequence, half_rows, 0))
    head_out = jnp.pad(head_router_out, ((0, 0), (0, 128 - CHOICES)))
    width_out = jnp.pad(width_router_out, ((0, 0), (CHOICES, 128 - 2 * CHOICES)))
    own_up_bias = lax.dynamic_index_in_dim(up_bias.reshape(RING, units), place, 0, keepdims=True)
    own_qkv_bias = lax.dynamic_index_in_dim(qkv_bias.reshape(3, RING, head_width), place, 1, keepdims=False)
    head_squash, head_prob, head_gate, head_done = call(
        head_body,
        [own_shape, shaped((rows, 128), f32), shaped((rows, 1), f32)],
        [tokens, line(attn_gain), line(attn_shift), head_router_in, head_out, line(head_choice)],
        waits=[cosine, width_out, own_up_bias, own_qkv_bias],
    )

    pieces = swap(packed, "z")
    choices = pieces[:, :, 3 * head_width + units :]
    token_blocks = ring_blocks(tokens)
    mixer_all, _ = call(
        mixer_body,
        [shaped((16, 32, width), bf16)],
        [pieces, out_swapped],
        waits=[head_done],
        room=16,
    )
    mixer_mine = swap(mixer_all, CHIPS)
    mixer_theirs = other_core(mixer_mine)
    rest_all, _ = call(
        count_body,
        [shaped((16, 72, width), bf16)],
        [choices, pieces, down_swapped],
        room=16,
        waits=[mixer_mine] + token_blocks[1:],
    )

    low1_half, query, kv_own, qkv_slice, _ = call(
        project_body,
        [
            half_shape,
            shaped((half_rows, head_width), bf16),
            shaped((half_rows, 2 * head_width), bf16),
            shaped((8, 2, 64, 3 * head_width), bf16),
        ],
        [core_scalar] + token_blocks
        + [
            line(attn_gain), line(attn_shift),
            mixer_mine.reshape(8, 64, -1), mixer_theirs.reshape(8, 64, -1),
            line(own_qkv_bias), cosine, sine,
        ],
        scalars=1,
        near=[7, 8],
    )
    qkv_slice = qkv_slice.reshape(width, 3 * head_width)
    kv_lower = lax.ppermute(kv_own, "yl", [(0, 1)])
    lines = shaped((own_heads * half_rows // QUERIES, 1, QUERIES), f32)
    turned_shape = shaped((half_rows // QUERIES, head_width, QUERIES), f32)
    own_top, own_total, own_out, own_done = call(
        attend_own_body,
        [lines, lines, turned_shape],
        [scalars, query, kv_own],
        [pltpu.VMEM((head_width, half_rows), bf16)],
        scalars=1,
    )
    head_slice, head_slice_done = call(
        head_slice_body,
        [shaped((half_rows, router_slice), f32)],
        [scalars, low1_half, head_router_in],
        scalars=1,
    )
    rest_all, _ = call(nothing, [], [], waits=[own_done], passes=[rest_all])
    rest_mine = swap(rest_all, CHIPS)
    grad_blocks = ring_blocks(out_grad)
    attended, log_total, _ = call(
        attend_body,
        [
            shaped((half_rows, head_width), bf16),
            shaped((own_heads * half_rows // QUERIES, 1, QUERIES), f32),
        ],
        [scalars, query, kv_lower, own_top, own_total, own_out, choices],
        [
            pltpu.VMEM((head_width, half_rows), bf16),
            pltpu.VMEM((half_rows // QUERIES, head_width, QUERIES), f32),
        ],
        scalars=1,
        waits=grad_blocks[1:] + [head_slice_done],
    )
    out_lanes = (slice(0, 16), slice(0, 32), slice(3 * head_width, 4 * head_width))
    out_slice, p0, p1, p2, p3, _ = call(
        out_body,
        [shaped((head_width, width), bf16), own_shape] + [part_shape] * 3,
        [scalars, attended, mixer_mine, mixer_theirs],
        [pltpu.VMEM((2, 2, 2, 4, 8, width), f32)],
        scalars=1,
        windows={2: out_lanes, 3: out_lanes},
    )
    attn_pre, middle, low2, rest_mine, _ = call(
        middle_body,
        [own_shape, own_shape, part_shape],
        [p0] + [to_sender(part, k) for k, part in ((1, p1), (2, p2), (3, p3))]
        + [tokens, line(out_bias), head_gate, line(ffn_gain), line(ffn_shift)],
        passes=[rest_mine],
    )
    rest_theirs = other_core(rest_mine)

    up_rows, down_rows = (
        (slice(0, 8), slice(0, 2), slice(*at), slice(0, size))
        for at, size in (((0, 32), width), ((32, 64), width))
    )
    count_rows = (slice(0, 16), slice(64, 72), slice(0, 128))
    rest_mine = rest_mine.reshape(8, 2, 72, width)
    rest_theirs = rest_theirs.reshape(8, 2, 72, width)
    (
        ffn_pre, f1, f2, f3, d_normed2, d1, d2, d3, width_dgate, low2_half, d_up, active_low, d_ffn_half,
        d_up_sum, width_prob, width_gate, width_squash, width_slice, forth_done,
    ) = call(
        feed_body,
        [own_shape] + [part_shape] * 3 + [own_shape] + [sent_shape] * 3
        + [shaped((1, rows), f32), half_shape, shaped((half_rows, units), bf16)]
        + [shaped((half_rows, units), bf16), half_shape, shaped((1, units), f32)]
        + [shaped((rows, 128), f32), shaped((rows, 1), f32), shaped((rows, router_width), f32)]
        + [shaped((half_rows, router_slice), f32)],
        [scalars] + ring_blocks(low2)
        + [rest_mine, rest_theirs, own_up_bias]
        + [width_router_in, width_out]
        + [rest_mine, rest_theirs]
        + grad_blocks + [choices],
        [pltpu.VMEM((8, 2, 2, 32, units), bf16), pltpu.VMEM((2, 2, 2, 4, 32, width), bf16)],
        scalars=1,
        room=48,
        windows={5: up_rows, 6: up_rows, 10: down_rows, 11: down_rows},
    )
    d_received = [to_sender(part, k) for k, part in ((1, d1), (2, d2), (3, d3))]
    feed_mine, feed_theirs, f1, f2, f3, _ = call(
        feed_weight_body,
        [shaped((16, 64, width), bf16)] * 2 + [part_shape] * 3,
        [core_scalar, low2_half, d_up, active_low, d_ffn_half, f1, f2, f3],
        scalars=1,
    )
    payload, d_middle, d_hidden_head, early, share, feed_theirs, payload_done = call(
        own_back_body,
        [sent_shape, own_shape, part_shape, shaped((32, width), f32), shaped((1, 128), f32)],
        [scalars, d_normed2] + d_received
        + [middle, width_router_in, out_grad, width_squash, head_squash, attn_pre]
        + [width_dgate, line(down_bias), width_prob, width_gate, head_prob, head_gate]
        + [line(head_choice), line(width_choice), rest_mine.reshape(16, 72, width), rest_theirs.reshape(16, 72, width)]
        + [width_out, head_out, line(ffn_gain), d_up_sum],
        scalars=1,
        windows={19: count_rows, 20: count_rows},
        passes=[feed_theirs],
    )
    feed_part, feed_done = call(pair_body, [shaped((16, 64, width), bf16)], [feed_mine, other_core(feed_theirs)], cost=0, near=[1], waits=[payload_done])
    feed_pieces = swap(feed_part, CHIPS)
    router_term1 = against(d_hidden_head, head_router_in)

    d_attn_blocks = ring_blocks(payload)
    mixed_mine, mixed_theirs, mixed_done = call(
        mixer_weight_body,
        [shaped((16, 32, width), bf16)] * 2,
        [scalars, low1_half, low2_half, width_slice, head_slice, width_out, head_out, attended]
        + d_attn_blocks
        + [early],
        [
            pltpu.VMEM((half_rows, router_slice), bf16),
            pltpu.VMEM((half_rows, router_slice), bf16),
            pltpu.VMEM((head_width, width), f32),
            pltpu.VMEM((rows, rows), f32),
        ],
        scalars=1,
        waits=[feed_done],
    )
    gradient_scratch = [pltpu.VMEM((half_rows, head_width), f32)] * 2
    d_lower, d_out, d_mean, d_query_lower, d_lower_done = call(
        attend_back_body,
        [
            shaped((half_rows, 2 * head_width), bf16),
            shaped((half_rows, head_width), bf16),
            lines,
            turned_shape,
        ],
        [scalars] + d_attn_blocks + [out_slice, query, kv_lower, choices, log_total, attended],
        [pltpu.VMEM((head_width, half_rows), bf16)] + gradient_scratch,
        scalars=1,
        cost=0,
        waits=[mixed_done],
    )
    back = lax.ppermute(d_lower, "yl", [(1, 0)])
    d_query, d_kv_own, d_query_done = call(
        attend_back_own_body,
        [shaped((half_rows, head_width), bf16), shaped((half_rows, 2 * head_width), f32)],
        [scalars, query, kv_own, log_total, d_out, d_mean, d_query_lower, cosine, sine],
        [
            pltpu.VMEM((head_width, half_rows), bf16),
            pltpu.VMEM((half_rows // QUERIES, head_width, QUERIES), f32),
        ]
        + gradient_scratch,
        scalars=1,
    )
    mixed_part, mixed_part_done = call(
        pair_body,
        [shaped((16, 32, width), bf16)],
        [mixed_mine, other_core(mixed_theirs)],
        cost=0,
        near=[1],
        waits=[d_query_done, feed_pieces],
    )
    mixer_pieces = swap(mixed_part, CHIPS)
    d_mixed, d_own, gain_shift, d_mixed_sum, *d_sent, _ = call(
        project_back_body,
        [
            shaped((half_rows, 3 * head_width), bf16),
            own_shape,
            shaped((2, width), f32),
            shaped((1, 3 * head_width), f32),
        ]
        + [part_shape] * 3,
        [back, d_kv_own, d_query, qkv_slice, cosine, sine] + token_blocks + [router_term1],
        waits=[mixed_part_done],
    )
    d_sent = [to_sender(part, k) for k, part in enumerate(d_sent, 1)]
    result, result_done = call(
        result_body,
        [part_shape],
        [ffn_pre] + [to_sender(part, k) for k, part in ((1, f1), (2, f2), (3, f3))]
        + [line(down_bias), middle, width_gate],
        room=16,
    )
    d_inputs, d_inputs_done = call(
        inputs_body,
        [own_shape],
        [d_own] + d_sent + [tokens, d_middle, line(attn_gain)],
        room=16,
    )

    feed_rows = block_sum(feed_pieces)
    down_grad = lax.ppermute(feed_rows[32:], ("x", "z"), flipped)
    mine, theirs, _ = call(
        project_weight_body,
        [shaped((8, 64, 3 * head_width + 256), bf16)] * 2,
        [scalars, low1_half, d_mixed, d_mixed_sum, gain_shift],
        scalars=1,
    )
    qkv_part, qkv_part_done = call(
        pair_body,
        [shaped((8, 64, 3 * head_width + 256), bf16)],
        [mine, other_core(theirs)],
        cost=0,
        near=[1],
        waits=[mixer_pieces],
    )
    qkv_part = swap(qkv_part.reshape(64, 8, -1), CHIPS + ("z",))
    qkv_grad, late, _ = call(
        project_sum_body,
        [shaped((8, 3 * width), f32), shaped((1, width), f32)],
        [qkv_part],
        near=[0],
    )

    shared, out_rows, _ = call(
        mixer_sum_body,
        [shaped((24, width), bf16), shaped((8, width), f32)],
        [mixer_pieces],
        near=[0],
    )
    out_grad_rows = lax.ppermute(out_rows, ("x", "z"), flipped)
    up_rows = feed_rows[:32].reshape(RING, 8, units).astype(bf16)
    from_ring = []
    for shift in range(RING):
        rows_of = lax.dynamic_index_in_dim(up_rows, (place + shift) % RING, 0, keepdims=False)
        block = jnp.concatenate([shared, rows_of], axis=0)
        if shift:
            block = lax.ppermute(block, "z", [(k, (k + shift) % RING) for k in range(RING)])
        from_ring.append(block)
    from_ring = jnp.take(jnp.stack(from_ring), ring_order, axis=0)
    early_sum = jnp.sum(from_ring[:, 16:24].astype(f32), axis=0).astype(bf16)
    up_grad = jnp.concatenate([from_ring[k, 24:] for k in range(RING)], axis=1).astype(f32)

    lanes = router_slice
    routers = jnp.concatenate(
        [
            jnp.concatenate([from_ring[k, :16, j * lanes : (j + 1) * lanes] for k in range(RING)], axis=1)
            for j in (0, 2, 1, 3)
        ]
        + [early_sum[:4], jnp.broadcast_to(late.astype(bf16), (4, width))],
        axis=0,
    )
    routers_mine = spread(routers, CHIPS, 16)
    routers_mine, _ = call(nothing, [], [], waits=[d_inputs_done, result_done], passes=[routers_mine])
    routers_theirs = other_core(routers_mine)
    half_part = (8, 1, 64, router_width)

    def own_half(scalars):
        return (slice(None), pl.ds(scalars[0], 1))

    def other_half(scalars):
        return (slice(None), pl.ds(1 - scalars[0], 1))

    whole_shape = shaped((8, 2, 64, router_width), f32)
    width_in_grad, head_in_grad, early_mine, _ = call(
        routers_own_body,
        [whole_shape, whole_shape, shaped((8, 2, 8, width), f32)],
        [core_scalar, routers_mine],
        scalars=1,
        partly={0: (half_part, own_half), 1: (half_part, own_half)},
    )
    vectors = [3 * width, width, RING * units, width, width, width, width, width]
    width_in_grad, head_in_grad, *vectors, head_out_grad, width_out_grad, prob_sums, _ = call(
        routers_body,
        [whole_shape, whole_shape]
        + [shaped((1, size), f32) for size in vectors]
        + [shaped((CHOICES, router_width), f32)] * 2
        + [shaped((1, 128), f32)],
        [core_scalar, routers_theirs, early_mine],
        [pltpu.VMEM((8, 2, 8, width), f32), pltpu.VMEM((8, 2, 2, 8, width), f32)],
        scalars=1,
        near=[1],
        partly={0: (half_part, other_half), 1: (half_part, other_half)},
        into=[width_in_grad, head_in_grad],
    )
    width_in_grad = width_in_grad.reshape(width, router_width)
    head_in_grad = head_in_grad.reshape(width, router_width)
    balance = CHOICES * jnp.sum(share * prob_sums / all_rows)

    return (
        result,
        balance,
        d_inputs,
        qkv_grad,
        out_grad_rows,
        up_grad,
        down_grad,
        *[vector.reshape(-1) for vector in vectors],
        head_in_grad,
        head_out_grad.T,
        width_in_grad,
        width_out_grad.T,
    )


def solution(mesh):
    fine = Mesh(mesh.devices.reshape(4, 2, 2, 2, 4), AXES)
    whole = P(AXES, None)
    vector = P(AXES)
    in_specs = (
        whole, whole, whole, P(), whole, P(), whole, P(), whole, P(),
        P(), P(), P(), P(), P(), P(), P(), P(), vector, vector, vector,
    )
    out_specs = (whole, P(), whole, whole, whole, whole, whole) + (P(),) * 12
    return jax.shard_map(local, mesh=fine, in_specs=in_specs, out_specs=out_specs, check_vma=False)
```

```python
import jax
import jax.numpy as jnp
import numpy as np
from jax import lax
from jax.experimental import pallas as pl
from jax.experimental.pallas import tpu as pltpu
from jax.sharding import Mesh
from jax.sharding import PartitionSpec as P


AXES = ("x", "yh", "c", "yl", "z")
CHIPS = ("x", "yh", "yl")
RING = 4
HEADS = 16
HEAD_DIM = 64
CHOICES = 4
EPS = 1e-05
AUX_WEIGHT = 0.1
BLOCKED = -1e30
bf16 = jnp.bfloat16
f32 = jnp.float32
INTERPRET = False
QUERIES = 512
LONG = 10**10


def dot(former, latter):
    return jnp.dot(former, latter, preferred_element_type=f32)


def against(former, latter):
    return lax.dot_general(former, latter, (((1,), (1,)), ((), ())), preferred_element_type=f32)


def across(former, latter):
    return lax.dot_general(former, latter, (((0,), (0,)), ((), ())), preferred_element_type=f32)


def swap(value, axes):
    return lax.all_to_all(value, axes, split_axis=0, concat_axis=0, tiled=True)


def spread(value, axes, count):
    return swap(jnp.broadcast_to(value[None], (count,) + value.shape), axes)


def other_core(value):
    return lax.ppermute(value, "c", [(0, 1), (1, 0)])


def ring_blocks(value):
    return [value] + [
        lax.ppermute(value, "z", [(k, (k + shift) % RING) for k in range(RING)]) for shift in range(1, RING)
    ]


def to_sender(value, shift):
    return lax.ppermute(value, "z", [(k, (k - shift) % RING) for k in range(RING)])


def ring_product(former, latter, product, rows):
    sent = [
        to_sender(product(former[k * rows : (k + 1) * rows], latter).astype(bf16), k) for k in range(1, RING)
    ]
    total = product(former[:rows], latter)
    for part in sent:
        total = total + part.astype(f32)
    return total


def spread_chips(value):
    mine = spread(value, CHIPS, 16)
    return mine, other_core(mine)


def block_sum(pieces):
    return jnp.sum(pieces.astype(f32), axis=0)


def normalize(values):
    centred = values - jnp.mean(values, axis=-1, keepdims=True)
    inv_std = lax.rsqrt(jnp.mean(centred * centred, axis=-1, keepdims=True) + EPS)
    return (centred * inv_std, inv_std)


def rotary_tables(position):
    lane = jnp.arange(2 * HEAD_DIM)
    half = HEAD_DIM // 2
    freqs = 10000.0 ** (-2.0 * (lane % half).astype(f32) / HEAD_DIM)
    angle = position.astype(f32)[:, None] * freqs[None, :]
    return (jnp.cos(angle), jnp.sin(angle) * jnp.where(lane % HEAD_DIM < half, -1.0, 1.0)[None, :])


def call(body, outs, args, scratch=(), scalars=0, cost=LONG, waits=(), room=24, windows=None, passes=(), near=(), partly=None, into=(), near_outs=(), far=()):
    outs = list(outs) + [shaped((8, 128), f32)]
    given, taken = len(args), len(args) + len(waits) + len(passes) + len(into)
    partly = partly or {}

    def large(value):
        return int(np.prod(value.shape)) * value.dtype.itemsize >= 65536

    windows = windows or {}

    def shape_in(k):
        if k not in windows:
            return args[k].shape
        return tuple(part.stop - part.start for part in windows[k])

    copied_in = [k for k in range(scalars, given) if (large(args[k]) or k in far) and k not in near]
    copied_out = [k for k in range(len(outs)) if large(outs[k]) and k not in near_outs]
    copies = len(copied_in) + len(copied_out)

    def whole(*refs):
        ins, results = list(refs[:given]), list(refs[taken : taken + len(outs)])
        rest = refs[taken + len(outs) + len(passes) :]
        semaphores, buffers, own = rest[0], rest[1 : 1 + copies], rest[1 + copies :]
        moves = []
        for j, k in enumerate(copied_in):
            source = ins[k].at[windows[k]] if k in windows else ins[k]
            move = pltpu.make_async_copy(source, buffers[j], semaphores.at[j])
            move.start()
            moves.append(move)
            ins[k] = buffers[j]
        for move in moves:
            move.wait()
        targets = list(results)
        for j, k in enumerate(copied_out, len(copied_in)):
            results[k] = buffers[j]
        body(*ins, *results[:-1], *own)
        results[-1][...] = jnp.zeros((8, 128), f32)
        moves = []
        for j, k in enumerate(copied_out, len(copied_in)):
            target = targets[k].at[partly[k][1](refs[0])] if k in partly else targets[k]
            moves.append(pltpu.make_async_copy(buffers[j], target, semaphores.at[j]))
            moves[-1].start()
        for move in moves:
            move.wait()

    def spec(k, copied):
        return pl.BlockSpec(memory_space=pltpu.HBM if k in copied else pltpu.VMEM)

    spaces = [pl.BlockSpec(memory_space=pltpu.SMEM)] * scalars
    spaces += [spec(k, copied_in) for k in range(scalars, given)]
    spaces += [pl.BlockSpec(memory_space=pl.ANY)] * (len(waits) + len(passes) + len(into))
    buffers = [pltpu.VMEM(shape_in(k), args[k].dtype) for k in copied_in]
    buffers += [pltpu.VMEM(partly[k][0] if k in partly else outs[k].shape, outs[k].dtype) for k in copied_out]
    moved = sum(int(np.prod(value.shape)) * value.dtype.itemsize for value in list(args) + list(outs))
    shapes = list(outs) + [shaped(value.shape, value.dtype) for value in passes]
    if not INTERPRET:
        shapes = [
            pltpu.HBM(v.shape, v.dtype) if k in copied_out or k >= len(outs) else v for k, v in enumerate(shapes)
        ]
        args = [pltpu.with_memory_space_constraint(v, pltpu.HBM) if k in copied_in else v for k, v in enumerate(args)]
        passes = [pltpu.with_memory_space_constraint(v, pltpu.HBM) for v in passes]
        into = [pltpu.with_memory_space_constraint(v, pltpu.HBM) for v in into]
    results = pl.pallas_call(
        whole,
        out_shape=tuple(shapes),
        in_specs=spaces,
        out_specs=tuple(spec(k, copied_out) for k in range(len(outs)))
        + tuple(pl.BlockSpec(memory_space=pl.ANY) for _ in passes),
        scratch_shapes=[pltpu.SemaphoreType.DMA((max(copies, 1),))] + buffers + list(scratch),
        input_output_aliases={
            **{given + len(waits) + k: len(outs) + k for k in range(len(passes))},
            **{given + len(waits) + len(passes) + k: k for k in range(len(into))},
        },
        compiler_params=pltpu.CompilerParams(vmem_limit_bytes=room << 20),
        cost_estimate=pl.CostEstimate(flops=cost, bytes_accessed=moved if cost else 0, transcendentals=0),
        interpret=INTERPRET,
    )(*args, *waits, *passes, *into)
    last = len(outs) - 1
    return (*results[:last], *results[last + 1 :], results[last])


def shaped(shape, kind):
    return jax.ShapeDtypeStruct(shape, kind)


def turned(value, cosine, sine):
    lane = lax.broadcasted_iota(jnp.int32, value.shape, 1)
    width = value.shape[1]
    half = HEAD_DIM // 2
    flipped = jnp.where(
        lane % HEAD_DIM < half, pltpu.roll(value, width - half, 1), pltpu.roll(value, half, 1)
    )
    return value * cosine + flipped * sine


def turned_back(value, cosine, sine):
    lane = lax.broadcasted_iota(jnp.int32, value.shape, 1)
    width = value.shape[1]
    half = HEAD_DIM // 2
    moved = value * sine
    flipped = jnp.where(
        lane % HEAD_DIM < half, pltpu.roll(moved, width - half, 1), pltpu.roll(moved, half, 1)
    )
    return value * cosine + flipped


def project_body(core_ref, t0, t1, t2, t3, gain, shift, mine, theirs, bias, cosine, sine, low_ref, query_ref, kv_ref, weight_ref):
    core = core_ref[0]
    lanes = weight_ref.shape[-1]
    weight_ref[:, pl.ds(core, 1)] = mine[:, :, :lanes][:, None]
    weight_ref[:, pl.ds(1 - core, 1)] = theirs[:, :, :lanes][:, None]
    weight = weight_ref[...].reshape(-1, weight_ref.shape[-1])
    rows = t0.shape[0]
    heads = query_ref.shape[1]
    for k, block in enumerate((t0, t1, t2, t3)):
        at = slice(k * rows, (k + 1) * rows)
        unit, _ = normalize(block[...].astype(f32))
        low = (unit * gain[...] + shift[...]).astype(bf16)
        low_ref[at, :] = low
        mixed = dot(low, weight) + bias[...]
        for j in range(heads // 128):
            lanes = slice(128 * j, 128 * (j + 1))
            query_ref[at, lanes] = turned(mixed[:, lanes], cosine[at, :], sine[at, :]).astype(bf16)
            key = mixed[:, heads + 128 * j : heads + 128 * (j + 1)]
            kv_ref[at, lanes] = turned(key, cosine[at, :], sine[at, :]).astype(bf16)
        kv_ref[at, heads:] = mixed[:, 2 * heads :].astype(bf16)


def kept_row(choice_ref, which, place, k):
    chosen = choice_ref[(place + RING - k) % RING, which : which + 1, :].astype(f32)
    return jnp.where(chosen >= place.astype(f32), 1.0, 0.0)


def column(row):
    return jnp.broadcast_to(row, (row.shape[1], row.shape[1])).T[:, :1]


def order_of(shape, axis, place, first=0):
    at = lax.broadcasted_iota(jnp.int32, shape, axis) + first
    return ((place + RING - at // 128) % RING) * 128 + at % 128


def own_part(h, query):
    lane = lax.broadcasted_iota(jnp.int32, query.shape, 1)
    return jnp.where(lane // HEAD_DIM == h, query, jnp.zeros_like(query)) * jnp.asarray(HEAD_DIM ** (-0.5), bf16)


def masked(score, own, flag, place, q_block):
    if not own:
        return jnp.where(flag, score, BLOCKED)
    keys = order_of((score.shape[0], 1), 0, place)
    return jnp.where(keys <= order_of((1, score.shape[1]), 1, place, q_block * QUERIES), score, BLOCKED)


def loop(heads, queries, step):
    blocks = queries // QUERIES

    def one(at, carry):
        h, q_block = at // blocks, at % blocks
        here = pl.ds(pl.multiple_of(q_block * QUERIES, QUERIES), QUERIES)
        features = pl.ds(pl.multiple_of(h * HEAD_DIM, HEAD_DIM), HEAD_DIM)
        step(at, h, q_block, here, features)
        return carry

    lax.fori_loop(0, blocks * (heads // HEAD_DIM), one, 0)


def attend_own_body(scalars, query_ref, kv_ref, top_ref, total_ref, out_ref, value_turned):
    heads = query_ref.shape[1]
    value_turned[...] = kv_ref[:, heads:].T
    flag, place = scalars[2] == 1, scalars[1]

    def step(at, h, q_block, here, features):
        score = against(kv_ref[:, :heads], own_part(h, query_ref[here, :]))
        score = masked(score, True, flag, place, q_block)
        top = jnp.max(score, axis=0, keepdims=True)
        expo = jnp.exp(score - top)
        top_ref[at] = top
        total_ref[at] = jnp.sum(expo, axis=0, keepdims=True)
        out_ref[q_block, features, :] = dot(value_turned[features, :], expo.astype(bf16))

    loop(heads, query_ref.shape[0], step)


def attend_body(
    scalars, query_ref, kv_ref, own_top, own_total, own_out, choice_ref, out_ref, total_ref, value_turned, out_turned,
):
    heads = query_ref.shape[1]
    value_turned[...] = kv_ref[:, heads:].T
    flag, place = scalars[2] == 1, scalars[1]

    def step(at, h, q_block, here, features):
        score = against(kv_ref[:, :heads], own_part(h, query_ref[here, :]))
        score = masked(score, False, flag, place, q_block)
        top = jnp.maximum(jnp.max(score, axis=0, keepdims=True), own_top[at])
        expo = jnp.exp(score - top)
        factor = jnp.exp(own_top[at] - top)
        total = jnp.sum(expo, axis=0, keepdims=True) + factor * own_total[at]
        total_ref[at] = top + jnp.log(total)
        out = dot(value_turned[features, :], expo.astype(bf16)) + factor * own_out[q_block, features, :]
        out_turned[q_block, features, :] = out / total

    loop(heads, query_ref.shape[0], step)
    for k in range(query_ref.shape[0] // QUERIES):
        at = slice(k * QUERIES, (k + 1) * QUERIES)
        each = QUERIES // 128
        keep = jnp.concatenate([kept_row(choice_ref, 0, place, each * k + j) for j in range(each)], axis=1)
        out_ref[at, :] = (out_turned[k] * keep).T.astype(bf16)


def back_step(own, scalars, query_ref, kv_ref, total_ref, d_out, mean_ref, key_turned, d_query_turned, d_key, d_value):
    heads = query_ref.shape[1]
    flag, place = scalars[2] == 1, scalars[1]

    def step(at, h, q_block, here, features):
        query = own_part(h, query_ref[here, :])
        score = masked(against(kv_ref[:, :heads], query), own, flag, place, q_block)
        prob = jnp.exp(score - total_ref[at])
        gradient = d_out[here, :]
        lane = lax.broadcasted_iota(jnp.int32, gradient.shape, 1)
        gradient = jnp.where(lane // HEAD_DIM == h, gradient, jnp.zeros_like(gradient))
        d_value[...] += dot(prob.astype(bf16), gradient)
        d_score = (prob * (against(kv_ref[:, heads:], gradient) - mean_ref[at])).astype(bf16)
        d_key[...] += dot(d_score, query)
        d_query = dot(key_turned[features, :], d_score) * (HEAD_DIM ** (-0.5))
        if own:
            d_query += d_query_turned[q_block, features, :]
        d_query_turned[q_block, features, :] = d_query

    return step


def attend_back_body(
    scalars, g0, g1, g2, g3, out_slice, query_ref, kv_ref, choice_ref, total_ref, attended,
    send_ref, d_out, mean_ref, d_query_turned, key_turned, d_key, d_value,
):
    heads = query_ref.shape[1]
    rows = query_ref.shape[0] // RING
    place = scalars[1]
    blocks = query_ref.shape[0] // QUERIES
    key_turned[...] = kv_ref[:, :heads].T
    d_key[...] = jnp.zeros_like(d_key)
    d_value[...] = jnp.zeros_like(d_value)
    for k, block in enumerate((g0, g1, g2, g3)):
        at = slice(k * rows, (k + 1) * rows)
        part = against(block[:rows, :], out_slice[...])
        d_out[at, :] = (part * column(kept_row(choice_ref, 0, place, k))).astype(bf16)
    for k in range(blocks):
        at = slice(k * QUERIES, (k + 1) * QUERIES)
        product = (d_out[at, :].astype(f32) * attended[at, :].astype(f32)).T
        for h in range(heads // HEAD_DIM):
            part = product[h * HEAD_DIM : (h + 1) * HEAD_DIM]
            mean_ref[h * blocks + k] = jnp.sum(part, axis=0, keepdims=True)
    loop(
        heads,
        query_ref.shape[0],
        back_step(
            False, scalars, query_ref, kv_ref, total_ref, d_out, mean_ref, key_turned, d_query_turned, d_key, d_value
        ),
    )
    send_ref[:, :heads] = d_key[...].astype(bf16)
    send_ref[:, heads:] = d_value[...].astype(bf16)


def attend_back_own_body(
    scalars, query_ref, kv_ref, total_ref, d_out, mean_ref, lower, cosine, sine,
    d_query_ref, own_ref, key_turned, d_query_turned, d_key, d_value,
):
    heads = query_ref.shape[1]
    key_turned[...] = kv_ref[:, :heads].T
    d_query_turned[...] = lower[...]
    d_key[...] = jnp.zeros_like(d_key)
    d_value[...] = jnp.zeros_like(d_value)
    loop(
        heads,
        query_ref.shape[0],
        back_step(
            True, scalars, query_ref, kv_ref, total_ref, d_out, mean_ref, key_turned, d_query_turned, d_key, d_value
        ),
    )
    own_ref[:, :heads] = d_key[...]
    own_ref[:, heads:] = d_value[...]
    for k in range(query_ref.shape[0] // QUERIES):
        at = slice(k * QUERIES, (k + 1) * QUERIES)
        value = d_query_turned[k].T
        for j in range(heads // 128):
            lanes = slice(128 * j, 128 * (j + 1))
            d_query_ref[at, lanes] = turned_back(value[:, lanes], cosine[at, :], sine[at, :]).astype(bf16)


def head_slice_body(scalars, low, router_in, slice_ref):
    size = slice_ref.shape[1]
    lanes = pl.ds(pl.multiple_of(scalars[1] * size, size), size)
    slice_ref[...] = jnp.tanh(dot(low[...], router_in[:, lanes]))


def project_back_body(
    back_ref, own_ref, d_query_ref, weight, cosine, sine, t0, t1, t2, t3, term_ref,
    mixed_ref, total_ref, sums_ref, bias_ref, p1, p2, p3,
):
    heads = d_query_ref.shape[1]
    rows = t0.shape[0]
    gain_sum = jnp.zeros((1, t0.shape[1]), f32)
    shift_sum = jnp.zeros((1, t0.shape[1]), f32)
    bias_sum = jnp.zeros((1, 3 * heads), f32)
    for k, (block, part) in enumerate(((t1, p1), (t2, p2), (t3, p3), (t0, total_ref)), 1):
        k = k % RING
        at = slice(k * rows, (k + 1) * rows)
        mixed_ref[at, :heads] = d_query_ref[at, :]
        for j in range(heads // 128):
            lanes = slice(128 * j, 128 * (j + 1))
            value = own_ref[at, lanes] + back_ref[at, lanes].astype(f32)
            mixed_ref[at, heads + 128 * j : heads + 128 * (j + 1)] = turned_back(
                value, cosine[at, :], sine[at, :]
            ).astype(bf16)
        mixed_ref[at, 2 * heads :] = (own_ref[at, heads:] + back_ref[at, heads:].astype(f32)).astype(bf16)
        mixed = mixed_ref[at, :]
        bias_sum += jnp.sum(mixed.astype(f32), axis=0, keepdims=True)
        gradient = against(mixed, weight[...])
        if k == 0:
            gradient = gradient + term_ref[...]
        part[...] = gradient.astype(part.dtype)
        unit, _ = normalize(block[...].astype(f32))
        gain_sum += jnp.sum(gradient * unit, axis=0, keepdims=True)
        shift_sum += jnp.sum(gradient, axis=0, keepdims=True)
    sums_ref[0:1, :] = gain_sum
    sums_ref[1:2, :] = shift_sum
    bias_ref[...] = bias_sum


def project_weight_body(scalars, low_ref, mixed_ref, bias_ref, sums_ref, mine_ref, theirs_ref):
    core, place = scalars[0], scalars[1]
    size = bias_ref.shape[1] // 3
    row = lax.broadcasted_iota(jnp.int32, (8, size), 0)
    late = [jnp.where(row == place, bias_ref[:, size * k : size * (k + 1)], 0.0) for k in range(3)]
    for k in range(2):
        block = jnp.zeros((8, size), f32)
        for j in range(RING):
            block = jnp.where(row == j, sums_ref[k : k + 1, size * j : size * (j + 1)], block)
        late.append(block)
    late += [jnp.zeros((8, size), f32)] * 3
    lanes = mixed_ref.shape[1]
    for k in range(8):
        turned_low = low_ref[:, 128 * k : 128 * (k + 1)].T
        mine, theirs = halves(core, dot(turned_low, mixed_ref[...]))
        mine_ref[k, :, :lanes] = mine.astype(bf16)
        theirs_ref[k, :, :lanes] = theirs.astype(bf16)
        for j in range(2):
            at = slice(32 * j, 32 * (j + 1))
            if k >= 2:
                mine_ref[k, at, lanes:] = jnp.zeros((32, size), bf16)
                theirs_ref[k, at, lanes:] = jnp.zeros((32, size), bf16)
                continue
            mine, theirs = halves(core, jnp.concatenate([late[4 * k + j], late[4 * k + 2 + j]], axis=0))
            mine_ref[k, at, lanes:] = jnp.concatenate([mine] * RING, axis=0).astype(bf16)
            theirs_ref[k, at, lanes:] = jnp.concatenate([theirs] * RING, axis=0).astype(bf16)


def halves(core, part):
    half = part.shape[0] // 2
    first, second = part[:half], part[half:]
    return jnp.where(core == 0, first, second), jnp.where(core == 0, second, first)


def assemble(core, target, mine, theirs):
    target[:, pl.ds(core, 1)] = mine[...][:, None]
    target[:, pl.ds(1 - core, 1)] = theirs[...][:, None]
    return target[...].reshape(-1, target.shape[-1])


def pack_body(qkv, up, head_choice, width_choice, packed_ref):
    heads = qkv.shape[1] // 3 // RING
    units = up.shape[1] // RING
    row = lax.broadcasted_iota(jnp.int32, (8, head_choice.shape[1]), 0)
    choices = jnp.where(
        row == 0, head_choice[...].astype(f32), jnp.where(row == 1, width_choice[...].astype(f32), 0.0)
    ).astype(bf16)
    for z in range(RING):
        for j in range(3):
            packed_ref[z, :, j * heads : (j + 1) * heads] = qkv[:, (j * RING + z) * heads : (j * RING + z + 1) * heads]
        packed_ref[z, :, 3 * heads : 3 * heads + units] = up[:, z * units : (z + 1) * units]
        packed_ref[z, :, 3 * heads + units :] = choices


def head_body(tokens, gain, shift, router_in, router_out, choice, squash_ref, prob_ref, gate_ref):
    unit, _ = normalize(tokens[...].astype(f32))
    low = (unit * gain[...] + shift[...]).astype(bf16)
    squash = jnp.tanh(dot(low, router_in[...]))
    squash_ref[...] = squash
    logit = dot(squash.astype(bf16), router_out[...])
    lane = lax.broadcasted_iota(jnp.int32, logit.shape, 1)
    logit = jnp.where(lane < CHOICES, logit, BLOCKED)
    expo = jnp.exp(logit - jnp.max(logit, axis=-1, keepdims=True))
    prob = expo / jnp.sum(expo, axis=-1, keepdims=True)
    prob_ref[...] = prob
    gate_ref[...] = jnp.sum(
        jnp.where(lane.astype(f32) == column(choice[...].astype(f32)), prob, 0.0), axis=-1, keepdims=True
    )


def mixer_body(pieces, out_rows, mixer_ref):
    size = mixer_ref.shape[2] // RING
    for k in range(mixer_ref.shape[0]):
        for j in range(RING):
            at = slice(8 * j, 8 * (j + 1))
            mixer_ref[k, at, : 3 * size] = pieces[j, :, : 3 * size]
            mixer_ref[k, at, 3 * size :] = out_rows[:, j * size : (j + 1) * size]


def count_body(choice_ref, pieces, down, rest_ref):
    lane = lax.broadcasted_iota(jnp.int32, (1, rest_ref.shape[2]), 1)
    line = jnp.zeros((1, rest_ref.shape[2]), f32)
    for which in range(2):
        chosen = choice_ref[:, which, :].astype(f32)
        for option in range(CHOICES):
            count = jnp.sum(jnp.where(chosen == option, 1.0, 0.0), axis=1, keepdims=True)
            count = jnp.sum(count, axis=0, keepdims=True)
            pairs = jnp.floor(count * 0.5)
            at = which * CHOICES + option
            line = jnp.where(lane == at, pairs, line)
            line = jnp.where(lane == at + 2 * CHOICES, count - 2.0 * pairs, line)
    last = jnp.broadcast_to(line, (8, rest_ref.shape[2])).astype(bf16)
    heads = (pieces.shape[2] - rest_ref.shape[2] - choice_ref.shape[2]) // 3
    for k in range(rest_ref.shape[0]):
        for j in range(RING):
            rest_ref[k, 8 * j : 8 * (j + 1)] = pieces[j, :, 3 * heads : 3 * heads + rest_ref.shape[2]]
        rest_ref[k, 32:64] = down[...]
        rest_ref[k, 64:] = last


def out_body(scalars, attended, mine, theirs, slice_ref, p0, p1, p2, p3, full):
    core = scalars[0]
    size = mine.shape[-1]
    for x in range(4):
        for yh in range(2):
            for yl in range(2):
                at = (x * 2 + yh) * 2 + yl
                for k in range(4):
                    rows, lanes = slice(8 * k, 8 * (k + 1)), slice(size * k, size * (k + 1))
                    full[yh, pl.ds(core, 1), yl, x, :, lanes] = mine[at : at + 1, rows].astype(f32)
                    full[yh, pl.ds(1 - core, 1), yl, x, :, lanes] = theirs[at : at + 1, rows].astype(f32)
    weight = full[...].reshape(slice_ref.shape).astype(bf16)
    slice_ref[...] = weight
    rows = p0.shape[0]
    for k, part in ((1, p1), (2, p2), (3, p3), (0, p0)):
        part[...] = dot(attended[k * rows : (k + 1) * rows, :], weight).astype(part.dtype)


def middle_body(p0, r1, r2, r3, tokens, bias, gate, gain, shift, attn_pre_ref, middle_ref, low_ref):
    total = p0[...]
    for part in (r1, r2, r3):
        total = total + part[...].astype(f32)
    total = total + bias[...]
    attn_pre_ref[...] = total
    middle = tokens[...].astype(f32) + gate[...] * total
    middle_ref[...] = middle
    unit, _ = normalize(middle)
    low_ref[...] = (unit * gain[...] + shift[...]).astype(bf16)


def slice_of(value, place, size):
    part = value[:, :size]
    for k in range(1, RING):
        part = jnp.where(place == k, value[:, k * size : (k + 1) * size], part)
    return part


def feed_body(
    scalars, n0, n1, n2, n3, up_mine, up_theirs, up_bias, router_in, router_out, down_mine, down_theirs,
    g0, g1, g2, g3, choice_ref,
    f0, f1, f2, f3, d0, d1, d2, d3, dgate_ref, low_ref, d_up_ref, active_ref, d_ffn_ref, up_sum_ref,
    prob_ref, gate_ref, squash_ref, slice_ref, up_full, down_full,
):
    core, place = scalars[0], scalars[1]
    up = assemble(core, up_full, up_mine, up_theirs)
    for x in range(4):
        for yh in range(2):
            for yl in range(2):
                down_full[yh, pl.ds(core, 1), yl, x] = down_mine[2 * x + yh, yl : yl + 1]
                down_full[yh, pl.ds(1 - core, 1), yl, x] = down_theirs[2 * x + yh, yl : yl + 1]
    down = down_full[...].reshape(-1, down_full.shape[-1])
    rows = n0.shape[0]
    units = up_bias.shape[1]
    router_slice = slice_ref.shape[1]
    up_sum = jnp.zeros((1, units), f32)
    for blocks in (((1, n1, g1, f1, d1), (2, n2, g2, f2, d2)), ((3, n3, g3, f3, d3), (0, n0, g0, f0, d0))):
        low = jnp.concatenate([block[1][...] for block in blocks], axis=0)
        keep_row = [kept_row(choice_ref, 1, place, block[0]) for block in blocks]
        keep = jnp.concatenate([column(row) for row in keep_row], axis=0)
        chosen = jnp.concatenate(
            [column(choice_ref[(place + RING - block[0]) % RING, 1:2, :].astype(f32)) for block in blocks], axis=0
        )
        upward = dot(low, up) + up_bias[...]
        active = jnp.maximum(upward, 0.0) * keep
        active_low = (active * active).astype(bf16)
        squash = jnp.tanh(dot(low, router_in[...]))
        logit = dot(squash.astype(bf16), router_out[...])
        lane = lax.broadcasted_iota(jnp.int32, logit.shape, 1)
        logit = jnp.where(lane // CHOICES == 1, logit, BLOCKED)
        expo = jnp.exp(logit - jnp.max(logit, axis=-1, keepdims=True))
        prob = expo / jnp.sum(expo, axis=-1, keepdims=True)
        gate = jnp.sum(jnp.where((lane - CHOICES).astype(f32) == chosen, prob, 0.0), axis=-1, keepdims=True)
        part = slice_of(squash, place, router_slice)
        ffn_part = dot(active_low, down)
        grad_out = jnp.concatenate([block[2][...] for block in blocks], axis=0).astype(f32)
        dgate = jnp.sum(grad_out * ffn_part, axis=-1, keepdims=True)
        d_ffn = (gate * grad_out).astype(bf16)
        d_up = (against(d_ffn, down) * 2.0 * active).astype(bf16)
        up_sum += jnp.sum(d_up.astype(f32), axis=0, keepdims=True)
        d_normed = against(d_up, up)
        for j, (k, _, _, ffn, d_block) in enumerate(blocks):
            at, here = slice(k * rows, (k + 1) * rows), slice(j * rows, (j + 1) * rows)
            low_ref[at, :] = low[here]
            active_ref[at, :] = active_low[here]
            slice_ref[at, :] = part[here]
            d_ffn_ref[at, :] = d_ffn[here]
            d_up_ref[at, :] = d_up[here]
            ffn[...] = ffn_part[here].astype(ffn.dtype)
            d_block[:rows, :] = d_normed[here].astype(d_block.dtype)
            line = jnp.broadcast_to(dgate[here], (rows, rows)).T[:1]
            if k == 0:
                dgate_ref[...] = line
                squash_ref[...] = squash[here]
                prob_ref[...] = prob[here]
                gate_ref[...] = gate[here]
            else:
                upper = line.astype(bf16).astype(f32)
                row = lax.broadcasted_iota(jnp.int32, (8, rows), 0)
                lines = jnp.where(row == 0, upper, jnp.where(row == 1, line - upper, 0.0)).astype(bf16)
                d_block[rows:, :] = jnp.concatenate([lines] * (units // rows), axis=1)
    up_sum_ref[...] = up_sum


def feed_weight_body(
    core_ref, low_ref, d_up_ref, active_ref, d_ffn_ref, p1, p2, p3, mine_ref, theirs_ref, f1, f2, f3
):
    core = core_ref[0]
    for ffn, part in ((f1, p1), (f2, p2), (f3, p3)):
        ffn[...] = part[...]
    for k in range(8):
        turned_low = low_ref[:, 128 * k : 128 * (k + 1)].T
        mine, theirs = halves(core, dot(turned_low, d_up_ref[...]))
        for j in range(2):
            mine_ref[2 * k + j, :32, :] = mine[32 * j : 32 * (j + 1)].astype(bf16)
            theirs_ref[2 * k + j, :32, :] = theirs[32 * j : 32 * (j + 1)].astype(bf16)
    for yh in range(2):
        for yl in range(2):
            for target, side in ((mine_ref, core), (theirs_ref, 1 - core)):
                lanes = pl.ds(pl.multiple_of(((yh * 2 + side) * 2 + yl) * 128, 128), 128)
                part = dot(active_ref[:, lanes].T, d_ffn_ref[...]).astype(bf16)
                for x in range(4):
                    target[(x * 2 + yh) * 2 + yl, 32:, :] = part[32 * x : 32 * (x + 1)]


def pair_body(mine, theirs, sum_ref):
    sum_ref[...] = (mine[...].astype(f32) + theirs[...].astype(f32)).astype(bf16)


def nothing(*refs):
    pass


def own_back_body(
    scalars, d0, r1, r2, r3, middle_ref, router_in, grad_ref, squash_ref, head_squash_ref, attn_pre_ref,
    dgate_ref, down_bias, prob_ref, gate_ref, head_prob_ref, head_gate_ref, head_choice, width_choice,
    counts_mine, counts_theirs, width_out, head_out, gain, up_sum,
    payload_ref, d_middle_ref, d_hidden_ref, early_ref, share_ref,
):
    place = scalars[1]
    rows = grad_ref.shape[0]
    units = up_sum.shape[1]
    aux = AUX_WEIGHT * CHOICES / (128.0 * rows)
    grad_out = grad_ref[...].astype(f32)
    d_normed = d0[...]
    line = dgate_ref[...]
    for part in (r1, r2, r3):
        d_normed = d_normed + part[:rows, :].astype(f32)
        lines = part[rows:, :rows].astype(f32)
        line = line + lines[:1] + lines[1:2]
    dgate = column(line) + jnp.sum(grad_out * down_bias[...], axis=-1, keepdims=True)
    pairs = jnp.sum(counts_mine[...].astype(f32) + counts_theirs[...].astype(f32), axis=0)[:1]
    share = (2.0 * pairs + pltpu.roll(pairs, 128 - 2 * CHOICES, 1)) / (128.0 * rows)
    share_ref[...] = share
    at = lax.broadcasted_iota(jnp.int32, share.shape, 1)
    lane = lax.broadcasted_iota(jnp.int32, prob_ref.shape, 1).astype(f32)

    def d_logits(which, prob, choice, dgate):
        picked = jnp.where(lane - which * CHOICES == column(choice[...].astype(f32)), dgate, 0.0)
        d_prob = picked + aux * jnp.where(at // CHOICES == which, share, 0.0)
        return prob * (d_prob - jnp.sum(prob * d_prob, axis=-1, keepdims=True))

    d_width = d_logits(1, prob_ref[...], width_choice, dgate)
    squash = squash_ref[...]
    d_hidden = (against(d_width.astype(bf16), width_out[...]) * (1.0 - squash * squash)).astype(bf16)
    d_normed = d_normed + against(d_hidden, router_in[...])
    unit, inv_std = normalize(middle_ref[...])
    scaled = d_normed * gain[...]
    inner = (
        scaled
        - jnp.mean(scaled, axis=-1, keepdims=True)
        - unit * jnp.mean(scaled * unit, axis=-1, keepdims=True)
    )
    d_middle = inner * inv_std + grad_out
    d_middle_ref[...] = d_middle
    head_dgate = jnp.sum(d_middle * attn_pre_ref[...], axis=-1, keepdims=True)
    d_attn = (head_gate_ref[...] * d_middle).astype(bf16)
    payload_ref[:rows, :] = d_attn
    d_head = d_logits(0, head_prob_ref[...], head_choice, head_dgate)
    head_squash = head_squash_ref[...]
    d_hidden_ref[...] = (against(d_head.astype(bf16), head_out[...]) * (1.0 - head_squash * head_squash)).astype(bf16)
    d_logit = (d_head + d_width).T[:8].astype(bf16)
    payload_ref[rows:, :] = jnp.concatenate([d_logit] * (units // rows), axis=1)
    row = lax.broadcasted_iota(jnp.int32, (8, units), 0)
    d_ffn = (gate_ref[...] * grad_out).astype(bf16).astype(f32)
    vectors = (
        jnp.sum(d_attn.astype(f32), axis=0, keepdims=True),
        jnp.sum(d_ffn, axis=0, keepdims=True),
        jnp.sum(d_normed * unit, axis=0, keepdims=True),
        jnp.sum(d_normed, axis=0, keepdims=True),
    )
    first = dot(d_logit, head_squash.astype(bf16))
    second = dot(d_logit, squash.astype(bf16))
    block = jnp.where(row < CHOICES, first, second)
    early_ref[0:8, :] = block
    block = jnp.zeros((8, units), f32)
    for k, vector in enumerate(vectors):
        block = jnp.where(row == k, vector, block)
    for k in range(RING):
        block = jnp.where(row == RING + k, jnp.where(place == k, up_sum[...], 0.0), block)
    early_ref[8:16, :] = block
    probs = jnp.sum(head_prob_ref[...] + prob_ref[...], axis=0, keepdims=True)
    early_ref[16:24, :] = jnp.broadcast_to(jnp.concatenate([probs] * (units // 128), axis=1), (8, units))
    early_ref[24:32, :] = jnp.zeros((8, units), f32)


def mixer_weight_body(
    scalars, low1, low2, width_slice, head_slice, width_out, head_out, attended, g0, g1, g2, g3, early,
    mine_ref, theirs_ref, d_width, d_head, part_ref, logit_ref,
):
    core, place = scalars[0], scalars[1]
    rows = attended.shape[0] // RING
    size = width_slice.shape[1]
    here = pl.ds(pl.multiple_of(place * size, size), size)
    logit_ref[...] = jnp.zeros_like(logit_ref)
    for k, block in enumerate((g0, g1, g2, g3)):
        at = slice(k * rows, (k + 1) * rows)
        logit_ref[:8, :] = block[rows:, :rows].astype(f32)
        logit = logit_ref[...].T.astype(bf16)
        for target, weight, slices in ((d_width, width_out, width_slice), (d_head, head_out, head_slice)):
            squash = slices[at, :]
            target[at, :] = (against(logit, weight[here, :]) * (1.0 - squash * squash)).astype(bf16)
    for k in range(8):
        lanes = slice(128 * k, 128 * (k + 1))
        for first, former, latter in ((0, low2, d_width), (size, low1, d_head)):
            mine, theirs = halves(core, dot(former[:, lanes].T, latter[...]))
            for j in range(2):
                for half in range(2):
                    at = slice(32 * j + 16 * half, 32 * j + 16 * (half + 1))
                    to = slice(2 * size * half + first, 2 * size * half + first + size)
                    mine_ref[2 * k + j, 0:16, to] = mine[at].astype(bf16)
                    theirs_ref[2 * k + j, 0:16, to] = theirs[at].astype(bf16)
    turned_out = attended[...].T
    part = dot(turned_out[:, :rows], g0[:rows, :])
    for k, block in ((1, g1), (2, g2), (3, g3)):
        part += dot(turned_out[:, k * rows : (k + 1) * rows], block[:rows, :])
    part_ref[...] = part
    for x in range(4):
        for yh in range(2):
            for yl in range(2):
                to = (x * 2 + yh) * 2 + yl
                base = 2 * yh * 64 + (4 * yl + x) * 8
                at = (x * 2 + yh) * 4 + yl
                first = jnp.broadcast_to(early[at : at + 1, :], (8, early.shape[1]))
                second = jnp.broadcast_to(early[at + 2 : at + 3, :], (8, early.shape[1]))
                for target, side in ((mine_ref, core), (theirs_ref, 1 - core)):
                    out = part_ref[pl.ds(pl.multiple_of(base + side * 64, 8), 8), :]
                    vector = jnp.where(side == 0, first, second)
                    target[to, 16:32, :] = jnp.concatenate([out, vector], axis=0).astype(bf16)


def mixer_sum_body(pieces, shared_ref, out_ref):
    rows = jnp.sum(pieces[...].astype(f32), axis=0)
    shared_ref[:16, :] = rows[:16].astype(bf16)
    shared_ref[16:, :] = rows[24:].astype(bf16)
    out_ref[...] = rows[16:24]


def project_sum_body(pieces, grad_ref, late_ref):
    late = jnp.zeros((8, late_ref.shape[1] // RING), f32)
    heads = grad_ref.shape[1] // 3 // RING
    for z in range(RING):
        part = pieces[z].astype(f32)
        for k in range(1, 16):
            part = part + pieces[k * RING + z].astype(f32)
        for j in range(3):
            grad_ref[:, (j * RING + z) * heads : (j * RING + z + 1) * heads] = part[:, j * heads : (j + 1) * heads]
        late = late + part[:, 3 * heads :]
    late_ref[...] = jnp.concatenate([late[k : k + 1] for k in range(RING)], axis=1)


def unpack(source, width_ref, head_ref, early_ref):
    rows = source.shape[1] // 9 * 4
    for k in range(2):
        at = slice(k * rows, (k + 1) * rows)
        for j in range(8):
            width_ref[j, 0, at, :] = source[2 * j + k, :rows, :].astype(f32)
            head_ref[j, 0, at, :] = source[2 * j + k, rows : 2 * rows, :].astype(f32)
            early_ref[j, k] = source[2 * j + k, 2 * rows :, :].astype(f32)


def routers_own_body(core_ref, mine, width_ref, head_ref, early_ref):
    unpack(mine, width_ref, head_ref, early_ref)


def routers_body(
    core_ref, theirs, early_mine, width_ref, head_ref, qkv_ref, out_ref, up_ref, down_ref, attn_gain_ref, attn_shift_ref,
    ffn_gain_ref, ffn_shift_ref, head_out_ref, width_out_ref, prob_ref, early, full,
):
    core = core_ref[0]
    unpack(theirs, width_ref, head_ref, early)
    full[:, pl.ds(core, 1)] = early_mine[...][:, None]
    full[:, pl.ds(1 - core, 1)] = early[...][:, None]

    def vector(at, late=0):
        return full[at // 4, at // 2 % 2, at % 2, late : late + 1, :]

    size = full.shape[-1]
    for k in range(3):
        qkv_ref[:, k * size : (k + 1) * size] = vector(k, 4)
    attn_gain_ref[...] = vector(3, 4)
    attn_shift_ref[...] = vector(4, 4)
    out_ref[...] = vector(8)
    down_ref[...] = vector(9)
    ffn_gain_ref[...] = vector(10)
    ffn_shift_ref[...] = vector(11)
    for k in range(RING):
        up_ref[:, k * size : (k + 1) * size] = vector(12 + k)
    prob_ref[...] = vector(16)[:, :128]
    head_out_ref[...] = jnp.concatenate([vector(k) for k in range(CHOICES)], axis=0)
    width_out_ref[...] = jnp.concatenate([vector(CHOICES + k) for k in range(CHOICES)], axis=0)


def result_body(ffn, r1, r2, r3, bias, middle, gate, result_ref):
    total = ffn[...]
    for part in (r1, r2, r3):
        total = total + part[...].astype(f32)
    result_ref[...] = (middle[...] + gate[...] * (total + bias[...])).astype(bf16)


def inputs_body(d_own, r1, r2, r3, tokens, d_middle, gain, d_inputs_ref):
    gradient = d_own[...]
    for part in (r1, r2, r3):
        gradient = gradient + part[...].astype(f32)
    unit, inv_std = normalize(tokens[...].astype(f32))
    scaled = gradient * gain[...]
    inner = (
        scaled
        - jnp.mean(scaled, axis=-1, keepdims=True)
        - unit * jnp.mean(scaled * unit, axis=-1, keepdims=True)
    )
    d_inputs_ref[...] = inner * inv_std + d_middle[...]


def local(
    tokens,
    out_grad,
    qkv_weight,
    qkv_bias,
    out_weight,
    out_bias,
    up_weight,
    up_bias,
    down_weight,
    down_bias,
    attn_gain,
    attn_shift,
    ffn_gain,
    ffn_shift,
    head_router_in,
    head_router_out,
    width_router_in,
    width_router_out,
    head_choice,
    width_choice,
    seq_ids,
):
    rows, width = tokens.shape
    half_rows = RING * rows
    own_heads = HEADS // RING
    head_width = own_heads * HEAD_DIM
    units = up_weight.shape[1] // RING
    router_width = head_router_in.shape[1]
    router_slice = router_width // RING
    all_rows = rows * 128
    core = lax.axis_index("c").astype(jnp.int32)
    place = lax.axis_index("z").astype(jnp.int32)
    one_sequence = (lax.axis_index("yl") == 1) & (seq_ids[0] % 2 == 0)
    core_scalar = core.reshape(1)
    scalars = jnp.stack([core, place, one_sequence.astype(jnp.int32)])
    flipped = [(a * 4 + b, b * 4 + a) for a in range(4) for b in range(4)]
    own_shape = shaped((rows, width), f32)
    part_shape = shaped((rows, width), bf16)
    half_shape = shaped((half_rows, width), bf16)
    sent_shape = shaped((rows + 8, width), bf16)

    def line(vector):
        return vector.reshape(1, -1)

    out_swapped = lax.ppermute(out_weight, ("x", "z"), flipped)
    down_swapped = lax.ppermute(down_weight, ("x", "z"), flipped)
    packed, _ = call(
        pack_body,
        [shaped((RING, 8, 3 * head_width + units + rows), bf16)],
        [qkv_weight, up_weight, line(head_choice), line(width_choice)],
        far=[0, 2, 3],
        room=16,
    )
    ring_order = (place - jnp.arange(RING)) % RING
    order = (ring_order[:, None] * rows + jnp.arange(rows)[None, :]).reshape(half_rows)
    cosine, sine = rotary_tables(order + jnp.where(one_sequence, half_rows, 0))
    head_out = jnp.pad(head_router_out, ((0, 0), (0, 128 - CHOICES)))
    width_out = jnp.pad(width_router_out, ((0, 0), (CHOICES, 128 - 2 * CHOICES)))
    own_up_bias = lax.dynamic_index_in_dim(up_bias.reshape(RING, units), place, 0, keepdims=True)
    own_qkv_bias = lax.dynamic_index_in_dim(qkv_bias.reshape(3, RING, head_width), place, 1, keepdims=False)
    head_squash, head_prob, head_gate, head_done = call(
        head_body,
        [own_shape, shaped((rows, 128), f32), shaped((rows, 1), f32)],
        [tokens, line(attn_gain), line(attn_shift), head_router_in, head_out, line(head_choice)],
        waits=[cosine, width_out, own_up_bias, own_qkv_bias],
    )

    pieces = swap(packed, "z")
    choices = pieces[:, :, 3 * head_width + units :]
    token_blocks = ring_blocks(tokens)
    mixer_all, _ = call(
        mixer_body,
        [shaped((16, 32, width), bf16)],
        [pieces, out_swapped],
        waits=[head_done],
        near_outs=[0],
        room=16,
    )
    mixer_mine = swap(mixer_all, CHIPS)
    mixer_theirs = other_core(mixer_mine)
    rest_all, _ = call(
        count_body,
        [shaped((16, 72, width), bf16)],
        [choices, pieces, down_swapped],
        room=16,
        waits=[mixer_mine] + token_blocks[1:],
    )

    low1_half, query, kv_own, qkv_slice, _ = call(
        project_body,
        [
            half_shape,
            shaped((half_rows, head_width), bf16),
            shaped((half_rows, 2 * head_width), bf16),
            shaped((8, 2, 64, 3 * head_width), bf16),
        ],
        [core_scalar] + token_blocks
        + [
            line(attn_gain), line(attn_shift),
            mixer_mine.reshape(8, 64, -1), mixer_theirs.reshape(8, 64, -1),
            line(own_qkv_bias), cosine, sine,
        ],
        scalars=1,
        near=[7, 8],
    )
    qkv_slice = qkv_slice.reshape(width, 3 * head_width)
    kv_lower = lax.ppermute(kv_own, "yl", [(0, 1)])
    lines = shaped((own_heads * half_rows // QUERIES, 1, QUERIES), f32)
    turned_shape = shaped((half_rows // QUERIES, head_width, QUERIES), f32)
    own_top, own_total, own_out, own_done = call(
        attend_own_body,
        [lines, lines, turned_shape],
        [scalars, query, kv_own],
        [pltpu.VMEM((head_width, half_rows), bf16)],
        scalars=1,
    )
    head_slice, head_slice_done = call(
        head_slice_body,
        [shaped((half_rows, router_slice), f32)],
        [scalars, low1_half, head_router_in],
        scalars=1,
    )
    rest_all, _ = call(nothing, [], [], waits=[own_done], passes=[rest_all])
    rest_mine = swap(rest_all, CHIPS)
    grad_blocks = ring_blocks(out_grad)
    attended, log_total, _ = call(
        attend_body,
        [
            shaped((half_rows, head_width), bf16),
            shaped((own_heads * half_rows // QUERIES, 1, QUERIES), f32),
        ],
        [scalars, query, kv_lower, own_top, own_total, own_out, choices],
        [
            pltpu.VMEM((head_width, half_rows), bf16),
            pltpu.VMEM((half_rows // QUERIES, head_width, QUERIES), f32),
        ],
        scalars=1,
        near=[2],
        waits=grad_blocks[1:] + [head_slice_done],
    )
    out_lanes = (slice(0, 16), slice(0, 32), slice(3 * head_width, 4 * head_width))
    out_slice, p0, p1, p2, p3, _ = call(
        out_body,
        [shaped((head_width, width), bf16), own_shape] + [part_shape] * 3,
        [scalars, attended, mixer_mine, mixer_theirs],
        [pltpu.VMEM((2, 2, 2, 4, 8, width), f32)],
        scalars=1,
        windows={2: out_lanes, 3: out_lanes},
    )
    attn_pre, middle, low2, rest_mine, _ = call(
        middle_body,
        [own_shape, own_shape, part_shape],
        [p0] + [to_sender(part, k) for k, part in ((1, p1), (2, p2), (3, p3))]
        + [tokens, line(out_bias), head_gate, line(ffn_gain), line(ffn_shift)],
        passes=[rest_mine],
    )
    rest_theirs = other_core(rest_mine)

    up_rows, down_rows = (
        (slice(0, 8), slice(0, 2), slice(*at), slice(0, size))
        for at, size in (((0, 32), width), ((32, 64), width))
    )
    count_rows = (slice(0, 16), slice(64, 72), slice(0, 128))
    rest_mine = rest_mine.reshape(8, 2, 72, width)
    rest_theirs = rest_theirs.reshape(8, 2, 72, width)
    (
        ffn_pre, f1, f2, f3, d_normed2, d1, d2, d3, width_dgate, low2_half, d_up, active_low, d_ffn_half,
        d_up_sum, width_prob, width_gate, width_squash, width_slice, forth_done,
    ) = call(
        feed_body,
        [own_shape] + [part_shape] * 3 + [own_shape] + [sent_shape] * 3
        + [shaped((1, rows), f32), half_shape, shaped((half_rows, units), bf16)]
        + [shaped((half_rows, units), bf16), half_shape, shaped((1, units), f32)]
        + [shaped((rows, 128), f32), shaped((rows, 1), f32), shaped((rows, router_width), f32)]
        + [shaped((half_rows, router_slice), f32)],
        [scalars] + ring_blocks(low2)
        + [rest_mine, rest_theirs, own_up_bias]
        + [width_router_in, width_out]
        + [rest_mine, rest_theirs]
        + grad_blocks + [choices],
        [pltpu.VMEM((8, 2, 2, 32, units), bf16), pltpu.VMEM((2, 2, 2, 4, 32, width), bf16)],
        scalars=1,
        room=48,
        windows={5: up_rows, 6: up_rows, 10: down_rows, 11: down_rows},
    )
    d_received = [to_sender(part, k) for k, part in ((1, d1), (2, d2), (3, d3))]
    feed_mine, feed_theirs, f1, f2, f3, _ = call(
        feed_weight_body,
        [shaped((16, 64, width), bf16)] * 2 + [part_shape] * 3,
        [core_scalar, low2_half, d_up, active_low, d_ffn_half, f1, f2, f3],
        scalars=1,
    )
    payload, d_middle, d_hidden_head, early, share, feed_theirs, payload_done = call(
        own_back_body,
        [sent_shape, own_shape, part_shape, shaped((32, width), f32), shaped((1, 128), f32)],
        [scalars, d_normed2] + d_received
        + [middle, width_router_in, out_grad, width_squash, head_squash, attn_pre]
        + [width_dgate, line(down_bias), width_prob, width_gate, head_prob, head_gate]
        + [line(head_choice), line(width_choice), rest_mine.reshape(16, 72, width), rest_theirs.reshape(16, 72, width)]
        + [width_out, head_out, line(ffn_gain), d_up_sum],
        scalars=1,
        windows={19: count_rows, 20: count_rows},
        passes=[feed_theirs],
    )
    feed_part, feed_done = call(pair_body, [shaped((16, 64, width), bf16)], [feed_mine, other_core(feed_theirs)], cost=0, near=[1], near_outs=[0], waits=[payload_done])
    feed_pieces = swap(feed_part, CHIPS)
    router_term1 = against(d_hidden_head, head_router_in)

    d_attn_blocks = ring_blocks(payload)
    mixed_mine, mixed_theirs, mixed_done = call(
        mixer_weight_body,
        [shaped((16, 32, width), bf16)] * 2,
        [scalars, low1_half, low2_half, width_slice, head_slice, width_out, head_out, attended]
        + d_attn_blocks
        + [early],
        [
            pltpu.VMEM((half_rows, router_slice), bf16),
            pltpu.VMEM((half_rows, router_slice), bf16),
            pltpu.VMEM((head_width, width), f32),
            pltpu.VMEM((rows, rows), f32),
        ],
        scalars=1,
        waits=[feed_done],
    )
    gradient_scratch = [pltpu.VMEM((half_rows, head_width), f32)] * 2
    d_lower, d_out, d_mean, d_query_lower, d_lower_done = call(
        attend_back_body,
        [
            shaped((half_rows, 2 * head_width), bf16),
            shaped((half_rows, head_width), bf16),
            lines,
            turned_shape,
        ],
        [scalars] + d_attn_blocks + [out_slice, query, kv_lower, choices, log_total, attended],
        [pltpu.VMEM((head_width, half_rows), bf16)] + gradient_scratch,
        scalars=1,
        cost=0,
        waits=[mixed_done],
    )
    back = lax.ppermute(d_lower, "yl", [(1, 0)])
    d_query, d_kv_own, d_query_done = call(
        attend_back_own_body,
        [shaped((half_rows, head_width), bf16), shaped((half_rows, 2 * head_width), f32)],
        [scalars, query, kv_own, log_total, d_out, d_mean, d_query_lower, cosine, sine],
        [
            pltpu.VMEM((head_width, half_rows), bf16),
            pltpu.VMEM((half_rows // QUERIES, head_width, QUERIES), f32),
        ]
        + gradient_scratch,
        scalars=1,
    )
    mixed_part, mixed_part_done = call(
        pair_body,
        [shaped((16, 32, width), bf16)],
        [mixed_mine, other_core(mixed_theirs)],
        cost=0,
        near=[1],
        near_outs=[0],
        waits=[d_query_done, feed_pieces],
    )
    mixer_pieces = swap(mixed_part, CHIPS)
    d_mixed, d_own, gain_shift, d_mixed_sum, *d_sent, _ = call(
        project_back_body,
        [
            shaped((half_rows, 3 * head_width), bf16),
            own_shape,
            shaped((2, width), f32),
            shaped((1, 3 * head_width), f32),
        ]
        + [part_shape] * 3,
        [back, d_kv_own, d_query, qkv_slice, cosine, sine] + token_blocks + [router_term1],
        waits=[mixed_part_done],
    )
    d_sent = [to_sender(part, k) for k, part in enumerate(d_sent, 1)]
    result, result_done = call(
        result_body,
        [part_shape],
        [ffn_pre] + [to_sender(part, k) for k, part in ((1, f1), (2, f2), (3, f3))]
        + [line(down_bias), middle, width_gate],
        room=16,
    )
    d_inputs, d_inputs_done = call(
        inputs_body,
        [own_shape],
        [d_own] + d_sent + [tokens, d_middle, line(attn_gain)],
        room=16,
    )

    feed_rows = block_sum(feed_pieces)
    down_grad = lax.ppermute(feed_rows[32:], ("x", "z"), flipped)
    mine, theirs, _ = call(
        project_weight_body,
        [shaped((8, 64, 3 * head_width + 256), bf16)] * 2,
        [scalars, low1_half, d_mixed, d_mixed_sum, gain_shift],
        scalars=1,
    )
    qkv_part, qkv_part_done = call(
        pair_body,
        [shaped((8, 64, 3 * head_width + 256), bf16)],
        [mine, other_core(theirs)],
        cost=0,
        near=[1],
        near_outs=[0],
        waits=[mixer_pieces],
    )
    qkv_part = swap(qkv_part.reshape(64, 8, -1), CHIPS + ("z",))
    qkv_grad, late, _ = call(
        project_sum_body,
        [shaped((8, 3 * width), f32), shaped((1, width), f32)],
        [qkv_part],
        near=[0],
    )

    shared, out_rows, _ = call(
        mixer_sum_body,
        [shaped((24, width), bf16), shaped((8, width), f32)],
        [mixer_pieces],
        near=[0],
    )
    out_grad_rows = lax.ppermute(out_rows, ("x", "z"), flipped)
    up_rows = feed_rows[:32].reshape(RING, 8, units).astype(bf16)
    from_ring = []
    for shift in range(RING):
        rows_of = lax.dynamic_index_in_dim(up_rows, (place + shift) % RING, 0, keepdims=False)
        block = jnp.concatenate([shared, rows_of], axis=0)
        if shift:
            block = lax.ppermute(block, "z", [(k, (k + shift) % RING) for k in range(RING)])
        from_ring.append(block)
    from_ring = jnp.take(jnp.stack(from_ring), ring_order, axis=0)
    early_sum = jnp.sum(from_ring[:, 16:24].astype(f32), axis=0).astype(bf16)
    up_grad = jnp.concatenate([from_ring[k, 24:] for k in range(RING)], axis=1).astype(f32)

    lanes = router_slice
    routers = jnp.concatenate(
        [
            jnp.concatenate([from_ring[k, :16, j * lanes : (j + 1) * lanes] for k in range(RING)], axis=1)
            for j in (0, 2, 1, 3)
        ]
        + [early_sum[:4], jnp.broadcast_to(late.astype(bf16), (4, width))],
        axis=0,
    )
    routers_mine = spread(routers, CHIPS, 16)
    routers_theirs = other_core(routers_mine)
    half_part = (8, 1, 64, router_width)

    def own_half(scalars):
        return (slice(None), pl.ds(scalars[0], 1))

    def other_half(scalars):
        return (slice(None), pl.ds(1 - scalars[0], 1))

    whole_shape = shaped((8, 2, 64, router_width), f32)
    width_in_grad, head_in_grad, early_mine, _ = call(
        routers_own_body,
        [whole_shape, whole_shape, shaped((8, 2, 8, width), f32)],
        [core_scalar, routers_mine],
        scalars=1,
        near=[1],
        waits=[d_inputs_done, result_done],
        partly={0: (half_part, own_half), 1: (half_part, own_half)},
    )
    vectors = [3 * width, width, RING * units, width, width, width, width, width]
    width_in_grad, head_in_grad, *vectors, head_out_grad, width_out_grad, prob_sums, _ = call(
        routers_body,
        [whole_shape, whole_shape]
        + [shaped((1, size), f32) for size in vectors]
        + [shaped((CHOICES, router_width), f32)] * 2
        + [shaped((1, 128), f32)],
        [core_scalar, routers_theirs, early_mine],
        [pltpu.VMEM((8, 2, 8, width), f32), pltpu.VMEM((8, 2, 2, 8, width), f32)],
        scalars=1,
        near=[1],
        partly={0: (half_part, other_half), 1: (half_part, other_half)},
        into=[width_in_grad, head_in_grad],
    )
    width_in_grad = width_in_grad.reshape(width, router_width)
    head_in_grad = head_in_grad.reshape(width, router_width)
    balance = CHOICES * jnp.sum(share * prob_sums / all_rows)

    return (
        result,
        balance,
        d_inputs,
        qkv_grad,
        out_grad_rows,
        up_grad,
        down_grad,
        *[vector.reshape(-1) for vector in vectors],
        head_in_grad,
        head_out_grad.T,
        width_in_grad,
        width_out_grad.T,
    )


def solution(mesh):
    fine = Mesh(mesh.devices.reshape(4, 2, 2, 2, 4), AXES)
    whole = P(AXES, None)
    vector = P(AXES)
    in_specs = (
        whole, whole, whole, P(), whole, P(), whole, P(), whole, P(),
        P(), P(), P(), P(), P(), P(), P(), P(), vector, vector, vector,
    )
    out_specs = (whole, P(), whole, whole, whole, whole, whole) + (P(),) * 12
    return jax.shard_map(local, mesh=fine, in_specs=in_specs, out_specs=out_specs, check_vma=False)
```

```python
import jax
import jax.numpy as jnp
import numpy as np
from jax import lax
from jax.experimental import pallas as pl
from jax.experimental.pallas import tpu as pltpu
from jax.sharding import Mesh
from jax.sharding import PartitionSpec as P


AXES = ("x", "yh", "c", "yl", "z")
CHIPS = ("x", "yh", "yl")
RING = 4
HEADS = 16
HEAD_DIM = 64
CHOICES = 4
EPS = 1e-05
AUX_WEIGHT = 0.1
BLOCKED = -1e30
bf16 = jnp.bfloat16
f32 = jnp.float32
INTERPRET = False
QUERIES = 512
LONG = 10**10


def dot(former, latter):
    return jnp.dot(former, latter, preferred_element_type=f32)


def against(former, latter):
    return lax.dot_general(former, latter, (((1,), (1,)), ((), ())), preferred_element_type=f32)


def across(former, latter):
    return lax.dot_general(former, latter, (((0,), (0,)), ((), ())), preferred_element_type=f32)


def swap(value, axes):
    return lax.all_to_all(value, axes, split_axis=0, concat_axis=0, tiled=True)


def spread(value, axes, count):
    return swap(jnp.broadcast_to(value[None], (count,) + value.shape), axes)


def other_core(value):
    return lax.ppermute(value, "c", [(0, 1), (1, 0)])


def ring_blocks(value):
    return [value] + [
        lax.ppermute(value, "z", [(k, (k + shift) % RING) for k in range(RING)]) for shift in range(1, RING)
    ]


def to_sender(value, shift):
    return lax.ppermute(value, "z", [(k, (k - shift) % RING) for k in range(RING)])


def ring_product(former, latter, product, rows):
    sent = [
        to_sender(product(former[k * rows : (k + 1) * rows], latter).astype(bf16), k) for k in range(1, RING)
    ]
    total = product(former[:rows], latter)
    for part in sent:
        total = total + part.astype(f32)
    return total


def spread_chips(value):
    mine = spread(value, CHIPS, 16)
    return mine, other_core(mine)


def block_sum(pieces):
    return jnp.sum(pieces.astype(f32), axis=0)


def normalize(values):
    centred = values - jnp.mean(values, axis=-1, keepdims=True)
    inv_std = lax.rsqrt(jnp.mean(centred * centred, axis=-1, keepdims=True) + EPS)
    return (centred * inv_std, inv_std)


def rotary_tables(position):
    lane = jnp.arange(2 * HEAD_DIM)
    half = HEAD_DIM // 2
    freqs = 10000.0 ** (-2.0 * (lane % half).astype(f32) / HEAD_DIM)
    angle = position.astype(f32)[:, None] * freqs[None, :]
    return (jnp.cos(angle), jnp.sin(angle) * jnp.where(lane % HEAD_DIM < half, -1.0, 1.0)[None, :])


def call(body, outs, args, scratch=(), scalars=0, cost=LONG, waits=(), room=24, windows=None, passes=(), near=(), partly=None, into=(), near_outs=(), far=()):
    outs = list(outs) + [shaped((8, 128), f32)]
    given, taken = len(args), len(args) + len(waits) + len(passes) + len(into)
    partly = partly or {}

    def large(value):
        return int(np.prod(value.shape)) * value.dtype.itemsize >= 65536

    windows = windows or {}

    def shape_in(k):
        if k not in windows:
            return args[k].shape
        return tuple(part.stop - part.start for part in windows[k])

    copied_in = [k for k in range(scalars, given) if (large(args[k]) or k in far) and k not in near]
    copied_out = [k for k in range(len(outs)) if large(outs[k]) and k not in near_outs]
    copies = len(copied_in) + len(copied_out)

    def whole(*refs):
        ins, results = list(refs[:given]), list(refs[taken : taken + len(outs)])
        rest = refs[taken + len(outs) + len(passes) :]
        semaphores, buffers, own = rest[0], rest[1 : 1 + copies], rest[1 + copies :]
        moves = []
        for j, k in enumerate(copied_in):
            source = ins[k].at[windows[k]] if k in windows else ins[k]
            move = pltpu.make_async_copy(source, buffers[j], semaphores.at[j])
            move.start()
            moves.append(move)
            ins[k] = buffers[j]
        for move in moves:
            move.wait()
        targets = list(results)
        for j, k in enumerate(copied_out, len(copied_in)):
            results[k] = buffers[j]
        body(*ins, *results[:-1], *own)
        results[-1][...] = jnp.zeros((8, 128), f32)
        moves = []
        for j, k in enumerate(copied_out, len(copied_in)):
            target = targets[k].at[partly[k][1](refs[0])] if k in partly else targets[k]
            moves.append(pltpu.make_async_copy(buffers[j], target, semaphores.at[j]))
            moves[-1].start()
        for move in moves:
            move.wait()

    def spec(k, copied):
        return pl.BlockSpec(memory_space=pltpu.HBM if k in copied else pltpu.VMEM)

    spaces = [pl.BlockSpec(memory_space=pltpu.SMEM)] * scalars
    spaces += [spec(k, copied_in) for k in range(scalars, given)]
    spaces += [pl.BlockSpec(memory_space=pl.ANY)] * (len(waits) + len(passes) + len(into))
    buffers = [pltpu.VMEM(shape_in(k), args[k].dtype) for k in copied_in]
    buffers += [pltpu.VMEM(partly[k][0] if k in partly else outs[k].shape, outs[k].dtype) for k in copied_out]
    moved = sum(int(np.prod(value.shape)) * value.dtype.itemsize for value in list(args) + list(outs))
    shapes = list(outs) + [shaped(value.shape, value.dtype) for value in passes]
    if not INTERPRET:
        shapes = [
            pltpu.HBM(v.shape, v.dtype) if k in copied_out or k >= len(outs) else v for k, v in enumerate(shapes)
        ]
        args = [pltpu.with_memory_space_constraint(v, pltpu.HBM) if k in copied_in else v for k, v in enumerate(args)]
        passes = [pltpu.with_memory_space_constraint(v, pltpu.HBM) for v in passes]
        into = [pltpu.with_memory_space_constraint(v, pltpu.HBM) for v in into]
    results = pl.pallas_call(
        whole,
        out_shape=tuple(shapes),
        in_specs=spaces,
        out_specs=tuple(spec(k, copied_out) for k in range(len(outs)))
        + tuple(pl.BlockSpec(memory_space=pl.ANY) for _ in passes),
        scratch_shapes=[pltpu.SemaphoreType.DMA((max(copies, 1),))] + buffers + list(scratch),
        input_output_aliases={
            **{given + len(waits) + k: len(outs) + k for k in range(len(passes))},
            **{given + len(waits) + len(passes) + k: k for k in range(len(into))},
        },
        compiler_params=pltpu.CompilerParams(vmem_limit_bytes=room << 20),
        cost_estimate=pl.CostEstimate(flops=cost, bytes_accessed=moved if cost else 0, transcendentals=0),
        interpret=INTERPRET,
    )(*args, *waits, *passes, *into)
    last = len(outs) - 1
    return (*results[:last], *results[last + 1 :], results[last])


def shaped(shape, kind):
    return jax.ShapeDtypeStruct(shape, kind)


def turned(value, cosine, sine):
    lane = lax.broadcasted_iota(jnp.int32, value.shape, 1)
    width = value.shape[1]
    half = HEAD_DIM // 2
    flipped = jnp.where(
        lane % HEAD_DIM < half, pltpu.roll(value, width - half, 1), pltpu.roll(value, half, 1)
    )
    return value * cosine + flipped * sine


def turned_back(value, cosine, sine):
    lane = lax.broadcasted_iota(jnp.int32, value.shape, 1)
    width = value.shape[1]
    half = HEAD_DIM // 2
    moved = value * sine
    flipped = jnp.where(
        lane % HEAD_DIM < half, pltpu.roll(moved, width - half, 1), pltpu.roll(moved, half, 1)
    )
    return value * cosine + flipped


def project_body(core_ref, t0, t1, t2, t3, gain, shift, mine, theirs, bias, cosine, sine, low_ref, query_ref, kv_ref, weight_ref):
    core = core_ref[0]
    lanes = weight_ref.shape[-1]
    weight_ref[:, pl.ds(core, 1)] = mine[:, :, :lanes][:, None]
    weight_ref[:, pl.ds(1 - core, 1)] = theirs[:, :, :lanes][:, None]
    weight = weight_ref[...].reshape(-1, weight_ref.shape[-1])
    rows = t0.shape[0]
    heads = query_ref.shape[1]
    for k, block in enumerate((t0, t1, t2, t3)):
        at = slice(k * rows, (k + 1) * rows)
        unit, _ = normalize(block[...].astype(f32))
        low = (unit * gain[...] + shift[...]).astype(bf16)
        low_ref[at, :] = low
    mixed = dot(low_ref[...], weight) + bias[...]
    for j in range(heads // 128):
        lanes = slice(128 * j, 128 * (j + 1))
        query_ref[:, lanes] = turned(mixed[:, lanes], cosine[...], sine[...]).astype(bf16)
        key = mixed[:, heads + 128 * j : heads + 128 * (j + 1)]
        kv_ref[:, lanes] = turned(key, cosine[...], sine[...]).astype(bf16)
    kv_ref[:, heads:] = mixed[:, 2 * heads :].astype(bf16)


def kept_row(choice_ref, which, place, k):
    chosen = choice_ref[(place + RING - k) % RING, which : which + 1, :].astype(f32)
    return jnp.where(chosen >= place.astype(f32), 1.0, 0.0)


def column(row):
    return jnp.broadcast_to(row, (row.shape[1], row.shape[1])).T[:, :1]


def order_of(shape, axis, place, first=0):
    at = lax.broadcasted_iota(jnp.int32, shape, axis) + first
    return ((place + RING - at // 128) % RING) * 128 + at % 128


def own_part(h, query):
    lane = lax.broadcasted_iota(jnp.int32, query.shape, 1)
    return jnp.where(lane // HEAD_DIM == h, query, jnp.zeros_like(query)) * jnp.asarray(HEAD_DIM ** (-0.5), bf16)


def masked(score, own, flag, place, q_block):
    if not own:
        return jnp.where(flag, score, BLOCKED)
    keys = order_of((score.shape[0], 1), 0, place)
    return jnp.where(keys <= order_of((1, score.shape[1]), 1, place, q_block * QUERIES), score, BLOCKED)


def loop(heads, queries, step):
    blocks = queries // QUERIES

    def one(at, carry):
        h, q_block = at // blocks, at % blocks
        here = pl.ds(pl.multiple_of(q_block * QUERIES, QUERIES), QUERIES)
        features = pl.ds(pl.multiple_of(h * HEAD_DIM, HEAD_DIM), HEAD_DIM)
        step(at, h, q_block, here, features)
        return carry

    lax.fori_loop(0, blocks * (heads // HEAD_DIM), one, 0)


def attend_own_body(scalars, query_ref, kv_ref, top_ref, total_ref, out_ref, value_turned):
    heads = query_ref.shape[1]
    value_turned[...] = kv_ref[:, heads:].T
    flag, place = scalars[2] == 1, scalars[1]

    def step(at, h, q_block, here, features):
        score = against(kv_ref[:, :heads], own_part(h, query_ref[here, :]))
        score = masked(score, True, flag, place, q_block)
        top = jnp.max(score, axis=0, keepdims=True)
        expo = jnp.exp(score - top)
        top_ref[at] = top
        total_ref[at] = jnp.sum(expo, axis=0, keepdims=True)
        out_ref[q_block, features, :] = dot(value_turned[features, :], expo.astype(bf16))

    loop(heads, query_ref.shape[0], step)


def attend_body(
    scalars, query_ref, kv_ref, own_top, own_total, own_out, choice_ref, out_ref, total_ref, value_turned, out_turned,
):
    heads = query_ref.shape[1]
    value_turned[...] = kv_ref[:, heads:].T
    flag, place = scalars[2] == 1, scalars[1]

    def step(at, h, q_block, here, features):
        score = against(kv_ref[:, :heads], own_part(h, query_ref[here, :]))
        score = masked(score, False, flag, place, q_block)
        top = jnp.maximum(jnp.max(score, axis=0, keepdims=True), own_top[at])
        expo = jnp.exp(score - top)
        factor = jnp.exp(own_top[at] - top)
        total = jnp.sum(expo, axis=0, keepdims=True) + factor * own_total[at]
        total_ref[at] = top + jnp.log(total)
        out = dot(value_turned[features, :], expo.astype(bf16)) + factor * own_out[q_block, features, :]
        out_turned[q_block, features, :] = out / total

    loop(heads, query_ref.shape[0], step)
    for k in range(query_ref.shape[0] // QUERIES):
        at = slice(k * QUERIES, (k + 1) * QUERIES)
        each = QUERIES // 128
        keep = jnp.concatenate([kept_row(choice_ref, 0, place, each * k + j) for j in range(each)], axis=1)
        out_ref[at, :] = (out_turned[k] * keep).T.astype(bf16)


def back_step(own, scalars, query_ref, kv_ref, total_ref, d_out, mean_ref, key_turned, d_query_turned, d_key, d_value):
    heads = query_ref.shape[1]
    flag, place = scalars[2] == 1, scalars[1]

    def step(at, h, q_block, here, features):
        query = own_part(h, query_ref[here, :])
        score = masked(against(kv_ref[:, :heads], query), own, flag, place, q_block)
        prob = jnp.exp(score - total_ref[at])
        gradient = d_out[here, :]
        lane = lax.broadcasted_iota(jnp.int32, gradient.shape, 1)
        gradient = jnp.where(lane // HEAD_DIM == h, gradient, jnp.zeros_like(gradient))
        d_value[...] += dot(prob.astype(bf16), gradient)
        d_score = (prob * (against(kv_ref[:, heads:], gradient) - mean_ref[at])).astype(bf16)
        d_key[...] += dot(d_score, query)
        d_query = dot(key_turned[features, :], d_score) * (HEAD_DIM ** (-0.5))
        if own:
            d_query += d_query_turned[q_block, features, :]
        d_query_turned[q_block, features, :] = d_query

    return step


def attend_back_body(
    scalars, g0, g1, g2, g3, out_slice, query_ref, kv_ref, choice_ref, total_ref, attended,
    send_ref, d_out, mean_ref, d_query_turned, key_turned, d_key, d_value,
):
    heads = query_ref.shape[1]
    rows = query_ref.shape[0] // RING
    place = scalars[1]
    blocks = query_ref.shape[0] // QUERIES
    key_turned[...] = kv_ref[:, :heads].T
    d_key[...] = jnp.zeros_like(d_key)
    d_value[...] = jnp.zeros_like(d_value)
    for k, block in enumerate((g0, g1, g2, g3)):
        at = slice(k * rows, (k + 1) * rows)
        part = against(block[:rows, :], out_slice[...])
        d_out[at, :] = (part * column(kept_row(choice_ref, 0, place, k))).astype(bf16)
    for k in range(blocks):
        at = slice(k * QUERIES, (k + 1) * QUERIES)
        product = (d_out[at, :].astype(f32) * attended[at, :].astype(f32)).T
        for h in range(heads // HEAD_DIM):
            part = product[h * HEAD_DIM : (h + 1) * HEAD_DIM]
            mean_ref[h * blocks + k] = jnp.sum(part, axis=0, keepdims=True)
    loop(
        heads,
        query_ref.shape[0],
        back_step(
            False, scalars, query_ref, kv_ref, total_ref, d_out, mean_ref, key_turned, d_query_turned, d_key, d_value
        ),
    )
    send_ref[:, :heads] = d_key[...].astype(bf16)
    send_ref[:, heads:] = d_value[...].astype(bf16)


def attend_back_own_body(
    scalars, query_ref, kv_ref, total_ref, d_out, mean_ref, lower, cosine, sine,
    d_query_ref, own_ref, key_turned, d_query_turned, d_key, d_value,
):
    heads = query_ref.shape[1]
    key_turned[...] = kv_ref[:, :heads].T
    d_query_turned[...] = lower[...]
    d_key[...] = jnp.zeros_like(d_key)
    d_value[...] = jnp.zeros_like(d_value)
    loop(
        heads,
        query_ref.shape[0],
        back_step(
            True, scalars, query_ref, kv_ref, total_ref, d_out, mean_ref, key_turned, d_query_turned, d_key, d_value
        ),
    )
    own_ref[:, :heads] = d_key[...]
    own_ref[:, heads:] = d_value[...]
    for k in range(query_ref.shape[0] // QUERIES):
        at = slice(k * QUERIES, (k + 1) * QUERIES)
        value = d_query_turned[k].T
        for j in range(heads // 128):
            lanes = slice(128 * j, 128 * (j + 1))
            d_query_ref[at, lanes] = turned_back(value[:, lanes], cosine[at, :], sine[at, :]).astype(bf16)


def head_slice_body(scalars, low, router_in, slice_ref):
    size = slice_ref.shape[1]
    lanes = pl.ds(pl.multiple_of(scalars[1] * size, size), size)
    slice_ref[...] = jnp.tanh(dot(low[...], router_in[:, lanes]))


def project_back_body(
    back_ref, own_ref, d_query_ref, weight, cosine, sine, t0, t1, t2, t3, term_ref,
    mixed_ref, total_ref, sums_ref, bias_ref, p1, p2, p3,
):
    heads = d_query_ref.shape[1]
    rows = t0.shape[0]
    gain_sum = jnp.zeros((1, t0.shape[1]), f32)
    shift_sum = jnp.zeros((1, t0.shape[1]), f32)
    mixed_ref[:, :heads] = d_query_ref[...]
    for j in range(heads // 128):
        lanes = slice(128 * j, 128 * (j + 1))
        value = own_ref[:, lanes] + back_ref[:, lanes].astype(f32)
        mixed_ref[:, heads + 128 * j : heads + 128 * (j + 1)] = turned_back(value, cosine[...], sine[...]).astype(bf16)
    mixed_ref[:, 2 * heads :] = (own_ref[:, heads:] + back_ref[:, heads:].astype(f32)).astype(bf16)
    mixed = mixed_ref[...]
    bias_sum = jnp.sum(mixed.astype(f32), axis=0, keepdims=True)
    product = against(mixed, weight[...])
    for k, (block, part) in enumerate(((t0, total_ref), (t1, p1), (t2, p2), (t3, p3))):
        gradient = product[k * rows : (k + 1) * rows]
        if k == 0:
            gradient = gradient + term_ref[...]
        part[...] = gradient.astype(part.dtype)
        unit, _ = normalize(block[...].astype(f32))
        gain_sum += jnp.sum(gradient * unit, axis=0, keepdims=True)
        shift_sum += jnp.sum(gradient, axis=0, keepdims=True)
    sums_ref[0:1, :] = gain_sum
    sums_ref[1:2, :] = shift_sum
    bias_ref[...] = bias_sum


def project_weight_body(scalars, low_ref, mixed_ref, bias_ref, sums_ref, mine_ref, theirs_ref):
    core, place = scalars[0], scalars[1]
    size = bias_ref.shape[1] // 3
    row = lax.broadcasted_iota(jnp.int32, (8, size), 0)
    late = [jnp.where(row == place, bias_ref[:, size * k : size * (k + 1)], 0.0) for k in range(3)]
    for k in range(2):
        block = jnp.zeros((8, size), f32)
        for j in range(RING):
            block = jnp.where(row == j, sums_ref[k : k + 1, size * j : size * (j + 1)], block)
        late.append(block)
    late += [jnp.zeros((8, size), f32)] * 3
    lanes = mixed_ref.shape[1]
    for k in range(8):
        turned_low = low_ref[:, 128 * k : 128 * (k + 1)].T
        mine, theirs = halves(core, dot(turned_low, mixed_ref[...]))
        mine_ref[k, :, :lanes] = mine.astype(bf16)
        theirs_ref[k, :, :lanes] = theirs.astype(bf16)
        for j in range(2):
            at = slice(32 * j, 32 * (j + 1))
            if k >= 2:
                mine_ref[k, at, lanes:] = jnp.zeros((32, size), bf16)
                theirs_ref[k, at, lanes:] = jnp.zeros((32, size), bf16)
                continue
            mine, theirs = halves(core, jnp.concatenate([late[4 * k + j], late[4 * k + 2 + j]], axis=0))
            mine_ref[k, at, lanes:] = jnp.concatenate([mine] * RING, axis=0).astype(bf16)
            theirs_ref[k, at, lanes:] = jnp.concatenate([theirs] * RING, axis=0).astype(bf16)


def halves(core, part):
    half = part.shape[0] // 2
    first, second = part[:half], part[half:]
    return jnp.where(core == 0, first, second), jnp.where(core == 0, second, first)


def assemble(core, target, mine, theirs):
    target[:, pl.ds(core, 1)] = mine[...][:, None]
    target[:, pl.ds(1 - core, 1)] = theirs[...][:, None]
    return target[...].reshape(-1, target.shape[-1])


def pack_body(qkv, up, head_choice, width_choice, packed_ref):
    heads = qkv.shape[1] // 3 // RING
    units = up.shape[1] // RING
    row = lax.broadcasted_iota(jnp.int32, (8, head_choice.shape[1]), 0)
    choices = jnp.where(
        row == 0, head_choice[...].astype(f32), jnp.where(row == 1, width_choice[...].astype(f32), 0.0)
    ).astype(bf16)
    for z in range(RING):
        for j in range(3):
            packed_ref[z, :, j * heads : (j + 1) * heads] = qkv[:, (j * RING + z) * heads : (j * RING + z + 1) * heads]
        packed_ref[z, :, 3 * heads : 3 * heads + units] = up[:, z * units : (z + 1) * units]
        packed_ref[z, :, 3 * heads + units :] = choices


def head_body(tokens, gain, shift, router_in, router_out, choice, squash_ref, prob_ref, gate_ref):
    unit, _ = normalize(tokens[...].astype(f32))
    low = (unit * gain[...] + shift[...]).astype(bf16)
    squash = jnp.tanh(dot(low, router_in[...]))
    squash_ref[...] = squash
    logit = dot(squash.astype(bf16), router_out[...])
    lane = lax.broadcasted_iota(jnp.int32, logit.shape, 1)
    logit = jnp.where(lane < CHOICES, logit, BLOCKED)
    expo = jnp.exp(logit - jnp.max(logit, axis=-1, keepdims=True))
    prob = expo / jnp.sum(expo, axis=-1, keepdims=True)
    prob_ref[...] = prob
    gate_ref[...] = jnp.sum(
        jnp.where(lane.astype(f32) == column(choice[...].astype(f32)), prob, 0.0), axis=-1, keepdims=True
    )


def mixer_body(pieces, out_rows, mixer_ref):
    size = mixer_ref.shape[2] // RING
    for k in range(mixer_ref.shape[0]):
        for j in range(RING):
            at = slice(8 * j, 8 * (j + 1))
            mixer_ref[k, at, : 3 * size] = pieces[j, :, : 3 * size]
            mixer_ref[k, at, 3 * size :] = out_rows[:, j * size : (j + 1) * size]


def count_body(choice_ref, pieces, down, rest_ref):
    lane = lax.broadcasted_iota(jnp.int32, (1, rest_ref.shape[2]), 1)
    line = jnp.zeros((1, rest_ref.shape[2]), f32)
    for which in range(2):
        chosen = choice_ref[:, which, :].astype(f32)
        for option in range(CHOICES):
            count = jnp.sum(jnp.where(chosen == option, 1.0, 0.0), axis=1, keepdims=True)
            count = jnp.sum(count, axis=0, keepdims=True)
            pairs = jnp.floor(count * 0.5)
            at = which * CHOICES + option
            line = jnp.where(lane == at, pairs, line)
            line = jnp.where(lane == at + 2 * CHOICES, count - 2.0 * pairs, line)
    last = jnp.broadcast_to(line, (8, rest_ref.shape[2])).astype(bf16)
    heads = (pieces.shape[2] - rest_ref.shape[2] - choice_ref.shape[2]) // 3
    for k in range(rest_ref.shape[0]):
        for j in range(RING):
            rest_ref[k, 8 * j : 8 * (j + 1)] = pieces[j, :, 3 * heads : 3 * heads + rest_ref.shape[2]]
        rest_ref[k, 32:64] = down[...]
        rest_ref[k, 64:] = last


def out_body(scalars, attended, mine, theirs, slice_ref, p0, p1, p2, p3, full):
    core = scalars[0]
    size = mine.shape[-1]
    for x in range(4):
        for yh in range(2):
            for yl in range(2):
                at = (x * 2 + yh) * 2 + yl
                for k in range(4):
                    rows, lanes = slice(8 * k, 8 * (k + 1)), slice(size * k, size * (k + 1))
                    full[yh, pl.ds(core, 1), yl, x, :, lanes] = mine[at : at + 1, rows].astype(f32)
                    full[yh, pl.ds(1 - core, 1), yl, x, :, lanes] = theirs[at : at + 1, rows].astype(f32)
    weight = full[...].reshape(slice_ref.shape).astype(bf16)
    slice_ref[...] = weight
    rows = p0.shape[0]
    product = dot(attended[...], weight)
    for k, part in enumerate((p0, p1, p2, p3)):
        part[...] = product[k * rows : (k + 1) * rows].astype(part.dtype)


def middle_body(p0, r1, r2, r3, tokens, bias, gate, gain, shift, attn_pre_ref, middle_ref, low_ref):
    total = p0[...]
    for part in (r1, r2, r3):
        total = total + part[...].astype(f32)
    total = total + bias[...]
    attn_pre_ref[...] = total
    middle = tokens[...].astype(f32) + gate[...] * total
    middle_ref[...] = middle
    unit, _ = normalize(middle)
    low_ref[...] = (unit * gain[...] + shift[...]).astype(bf16)


def slice_of(value, place, size):
    part = value[:, :size]
    for k in range(1, RING):
        part = jnp.where(place == k, value[:, k * size : (k + 1) * size], part)
    return part


def feed_body(
    scalars, n0, n1, n2, n3, up_mine, up_theirs, up_bias, router_in, router_out, down_mine, down_theirs,
    g0, g1, g2, g3, choice_ref,
    f0, f1, f2, f3, d0, d1, d2, d3, dgate_ref, low_ref, d_up_ref, active_ref, d_ffn_ref, up_sum_ref,
    prob_ref, gate_ref, squash_ref, slice_ref, up_full, down_full,
):
    core, place = scalars[0], scalars[1]
    up = assemble(core, up_full, up_mine, up_theirs)
    for x in range(4):
        for yh in range(2):
            for yl in range(2):
                down_full[yh, pl.ds(core, 1), yl, x] = down_mine[2 * x + yh, yl : yl + 1]
                down_full[yh, pl.ds(1 - core, 1), yl, x] = down_theirs[2 * x + yh, yl : yl + 1]
    down = down_full[...].reshape(-1, down_full.shape[-1])
    rows = n0.shape[0]
    units = up_bias.shape[1]
    router_slice = slice_ref.shape[1]
    up_sum = jnp.zeros((1, units), f32)
    for blocks in (((0, n0, g0, f0, d0), (1, n1, g1, f1, d1), (2, n2, g2, f2, d2), (3, n3, g3, f3, d3)),):
        low = jnp.concatenate([block[1][...] for block in blocks], axis=0)
        keep_row = [kept_row(choice_ref, 1, place, block[0]) for block in blocks]
        keep = jnp.concatenate([column(row) for row in keep_row], axis=0)
        chosen = jnp.concatenate(
            [column(choice_ref[(place + RING - block[0]) % RING, 1:2, :].astype(f32)) for block in blocks], axis=0
        )
        upward = dot(low, up) + up_bias[...]
        active = jnp.maximum(upward, 0.0) * keep
        active_low = (active * active).astype(bf16)
        squash = jnp.tanh(dot(low, router_in[...]))
        logit = dot(squash.astype(bf16), router_out[...])
        lane = lax.broadcasted_iota(jnp.int32, logit.shape, 1)
        logit = jnp.where(lane // CHOICES == 1, logit, BLOCKED)
        expo = jnp.exp(logit - jnp.max(logit, axis=-1, keepdims=True))
        prob = expo / jnp.sum(expo, axis=-1, keepdims=True)
        gate = jnp.sum(jnp.where((lane - CHOICES).astype(f32) == chosen, prob, 0.0), axis=-1, keepdims=True)
        part = slice_of(squash, place, router_slice)
        ffn_part = dot(active_low, down)
        grad_out = jnp.concatenate([block[2][...] for block in blocks], axis=0).astype(f32)
        dgate = jnp.sum(grad_out * ffn_part, axis=-1, keepdims=True)
        d_ffn = (gate * grad_out).astype(bf16)
        d_up = (against(d_ffn, down) * 2.0 * active).astype(bf16)
        up_sum += jnp.sum(d_up.astype(f32), axis=0, keepdims=True)
        d_normed = against(d_up, up)
        for j, (k, _, _, ffn, d_block) in enumerate(blocks):
            at, here = slice(k * rows, (k + 1) * rows), slice(j * rows, (j + 1) * rows)
            low_ref[at, :] = low[here]
            active_ref[at, :] = active_low[here]
            slice_ref[at, :] = part[here]
            d_ffn_ref[at, :] = d_ffn[here]
            d_up_ref[at, :] = d_up[here]
            ffn[...] = ffn_part[here].astype(ffn.dtype)
            d_block[:rows, :] = d_normed[here].astype(d_block.dtype)
            line = jnp.broadcast_to(dgate[here], (rows, rows)).T[:1]
            if k == 0:
                dgate_ref[...] = line
                squash_ref[...] = squash[here]
                prob_ref[...] = prob[here]
                gate_ref[...] = gate[here]
            else:
                upper = line.astype(bf16).astype(f32)
                row = lax.broadcasted_iota(jnp.int32, (8, rows), 0)
                lines = jnp.where(row == 0, upper, jnp.where(row == 1, line - upper, 0.0)).astype(bf16)
                d_block[rows:, :] = jnp.concatenate([lines] * (units // rows), axis=1)
    up_sum_ref[...] = up_sum


def feed_weight_body(
    core_ref, low_ref, d_up_ref, active_ref, d_ffn_ref, p1, p2, p3, mine_ref, theirs_ref, f1, f2, f3
):
    core = core_ref[0]
    for ffn, part in ((f1, p1), (f2, p2), (f3, p3)):
        ffn[...] = part[...]
    for k in range(8):
        turned_low = low_ref[:, 128 * k : 128 * (k + 1)].T
        mine, theirs = halves(core, dot(turned_low, d_up_ref[...]))
        for j in range(2):
            mine_ref[2 * k + j, :32, :] = mine[32 * j : 32 * (j + 1)].astype(bf16)
            theirs_ref[2 * k + j, :32, :] = theirs[32 * j : 32 * (j + 1)].astype(bf16)
    for yh in range(2):
        for yl in range(2):
            for target, side in ((mine_ref, core), (theirs_ref, 1 - core)):
                lanes = pl.ds(pl.multiple_of(((yh * 2 + side) * 2 + yl) * 128, 128), 128)
                part = dot(active_ref[:, lanes].T, d_ffn_ref[...]).astype(bf16)
                for x in range(4):
                    target[(x * 2 + yh) * 2 + yl, 32:, :] = part[32 * x : 32 * (x + 1)]


def pair_body(mine, theirs, sum_ref):
    sum_ref[...] = (mine[...].astype(f32) + theirs[...].astype(f32)).astype(bf16)


def nothing(*refs):
    pass


def own_back_body(
    scalars, d0, r1, r2, r3, middle_ref, router_in, grad_ref, squash_ref, head_squash_ref, attn_pre_ref,
    dgate_ref, down_bias, prob_ref, gate_ref, head_prob_ref, head_gate_ref, head_choice, width_choice,
    counts_mine, counts_theirs, width_out, head_out, gain, up_sum,
    payload_ref, d_middle_ref, d_hidden_ref, early_ref, share_ref,
):
    place = scalars[1]
    rows = grad_ref.shape[0]
    units = up_sum.shape[1]
    aux = AUX_WEIGHT * CHOICES / (128.0 * rows)
    grad_out = grad_ref[...].astype(f32)
    d_normed = d0[...]
    line = dgate_ref[...]
    for part in (r1, r2, r3):
        d_normed = d_normed + part[:rows, :].astype(f32)
        lines = part[rows:, :rows].astype(f32)
        line = line + lines[:1] + lines[1:2]
    dgate = column(line) + jnp.sum(grad_out * down_bias[...], axis=-1, keepdims=True)
    pairs = jnp.sum(counts_mine[...].astype(f32) + counts_theirs[...].astype(f32), axis=0)[:1]
    share = (2.0 * pairs + pltpu.roll(pairs, 128 - 2 * CHOICES, 1)) / (128.0 * rows)
    share_ref[...] = share
    at = lax.broadcasted_iota(jnp.int32, share.shape, 1)
    lane = lax.broadcasted_iota(jnp.int32, prob_ref.shape, 1).astype(f32)

    def d_logits(which, prob, choice, dgate):
        picked = jnp.where(lane - which * CHOICES == column(choice[...].astype(f32)), dgate, 0.0)
        d_prob = picked + aux * jnp.where(at // CHOICES == which, share, 0.0)
        return prob * (d_prob - jnp.sum(prob * d_prob, axis=-1, keepdims=True))

    d_width = d_logits(1, prob_ref[...], width_choice, dgate)
    squash = squash_ref[...]
    d_hidden = (against(d_width.astype(bf16), width_out[...]) * (1.0 - squash * squash)).astype(bf16)
    d_normed = d_normed + against(d_hidden, router_in[...])
    unit, inv_std = normalize(middle_ref[...])
    scaled = d_normed * gain[...]
    inner = (
        scaled
        - jnp.mean(scaled, axis=-1, keepdims=True)
        - unit * jnp.mean(scaled * unit, axis=-1, keepdims=True)
    )
    d_middle = inner * inv_std + grad_out
    d_middle_ref[...] = d_middle
    head_dgate = jnp.sum(d_middle * attn_pre_ref[...], axis=-1, keepdims=True)
    d_attn = (head_gate_ref[...] * d_middle).astype(bf16)
    payload_ref[:rows, :] = d_attn
    d_head = d_logits(0, head_prob_ref[...], head_choice, head_dgate)
    head_squash = head_squash_ref[...]
    d_hidden_ref[...] = (against(d_head.astype(bf16), head_out[...]) * (1.0 - head_squash * head_squash)).astype(bf16)
    d_logit = (d_head + d_width).T[:8].astype(bf16)
    payload_ref[rows:, :] = jnp.concatenate([d_logit] * (units // rows), axis=1)
    row = lax.broadcasted_iota(jnp.int32, (8, units), 0)
    d_ffn = (gate_ref[...] * grad_out).astype(bf16).astype(f32)
    vectors = (
        jnp.sum(d_attn.astype(f32), axis=0, keepdims=True),
        jnp.sum(d_ffn, axis=0, keepdims=True),
        jnp.sum(d_normed * unit, axis=0, keepdims=True),
        jnp.sum(d_normed, axis=0, keepdims=True),
    )
    first = dot(d_logit, head_squash.astype(bf16))
    second = dot(d_logit, squash.astype(bf16))
    block = jnp.where(row < CHOICES, first, second)
    early_ref[0:8, :] = block
    block = jnp.zeros((8, units), f32)
    for k, vector in enumerate(vectors):
        block = jnp.where(row == k, vector, block)
    for k in range(RING):
        block = jnp.where(row == RING + k, jnp.where(place == k, up_sum[...], 0.0), block)
    early_ref[8:16, :] = block
    probs = jnp.sum(head_prob_ref[...] + prob_ref[...], axis=0, keepdims=True)
    early_ref[16:24, :] = jnp.broadcast_to(jnp.concatenate([probs] * (units // 128), axis=1), (8, units))
    early_ref[24:32, :] = jnp.zeros((8, units), f32)


def mixer_weight_body(
    scalars, low1, low2, width_slice, head_slice, width_out, head_out, attended, g0, g1, g2, g3, early,
    mine_ref, theirs_ref, d_width, d_head, part_ref, logit_ref,
):
    core, place = scalars[0], scalars[1]
    rows = attended.shape[0] // RING
    size = width_slice.shape[1]
    here = pl.ds(pl.multiple_of(place * size, size), size)
    logit_ref[...] = jnp.zeros_like(logit_ref)
    for k, block in enumerate((g0, g1, g2, g3)):
        at = slice(k * rows, (k + 1) * rows)
        logit_ref[:8, :] = block[rows:, :rows].astype(f32)
        logit = logit_ref[...].T.astype(bf16)
        for target, weight, slices in ((d_width, width_out, width_slice), (d_head, head_out, head_slice)):
            squash = slices[at, :]
            target[at, :] = (against(logit, weight[here, :]) * (1.0 - squash * squash)).astype(bf16)
    for k in range(8):
        lanes = slice(128 * k, 128 * (k + 1))
        for first, former, latter in ((0, low2, d_width), (size, low1, d_head)):
            mine, theirs = halves(core, dot(former[:, lanes].T, latter[...]))
            for j in range(2):
                for half in range(2):
                    at = slice(32 * j + 16 * half, 32 * j + 16 * (half + 1))
                    to = slice(2 * size * half + first, 2 * size * half + first + size)
                    mine_ref[2 * k + j, 0:16, to] = mine[at].astype(bf16)
                    theirs_ref[2 * k + j, 0:16, to] = theirs[at].astype(bf16)
    turned_out = attended[...].T
    part = dot(turned_out[:, :rows], g0[:rows, :])
    for k, block in ((1, g1), (2, g2), (3, g3)):
        part += dot(turned_out[:, k * rows : (k + 1) * rows], block[:rows, :])
    part_ref[...] = part
    for x in range(4):
        for yh in range(2):
            for yl in range(2):
                to = (x * 2 + yh) * 2 + yl
                base = 2 * yh * 64 + (4 * yl + x) * 8
                at = (x * 2 + yh) * 4 + yl
                first = jnp.broadcast_to(early[at : at + 1, :], (8, early.shape[1]))
                second = jnp.broadcast_to(early[at + 2 : at + 3, :], (8, early.shape[1]))
                for target, side in ((mine_ref, core), (theirs_ref, 1 - core)):
                    out = part_ref[pl.ds(pl.multiple_of(base + side * 64, 8), 8), :]
                    vector = jnp.where(side == 0, first, second)
                    target[to, 16:32, :] = jnp.concatenate([out, vector], axis=0).astype(bf16)


def mixer_sum_body(pieces, shared_ref, out_ref):
    rows = jnp.sum(pieces[...].astype(f32), axis=0)
    shared_ref[:16, :] = rows[:16].astype(bf16)
    shared_ref[16:, :] = rows[24:].astype(bf16)
    out_ref[...] = rows[16:24]


def project_sum_body(pieces, grad_ref, late_ref):
    late = jnp.zeros((8, late_ref.shape[1] // RING), f32)
    heads = grad_ref.shape[1] // 3 // RING
    for z in range(RING):
        part = pieces[z].astype(f32)
        for k in range(1, 16):
            part = part + pieces[k * RING + z].astype(f32)
        for j in range(3):
            grad_ref[:, (j * RING + z) * heads : (j * RING + z + 1) * heads] = part[:, j * heads : (j + 1) * heads]
        late = late + part[:, 3 * heads :]
    late_ref[...] = jnp.concatenate([late[k : k + 1] for k in range(RING)], axis=1)


def unpack(source, width_ref, head_ref, early_ref):
    rows = source.shape[1] // 9 * 4
    for k in range(2):
        at = slice(k * rows, (k + 1) * rows)
        for j in range(8):
            width_ref[j, 0, at, :] = source[2 * j + k, :rows, :].astype(f32)
            head_ref[j, 0, at, :] = source[2 * j + k, rows : 2 * rows, :].astype(f32)
            early_ref[j, k] = source[2 * j + k, 2 * rows :, :].astype(f32)


def routers_own_body(core_ref, mine, width_ref, head_ref, early_ref):
    unpack(mine, width_ref, head_ref, early_ref)


def routers_body(
    core_ref, theirs, early_mine, width_ref, head_ref, qkv_ref, out_ref, up_ref, down_ref, attn_gain_ref, attn_shift_ref,
    ffn_gain_ref, ffn_shift_ref, head_out_ref, width_out_ref, prob_ref, early, full,
):
    core = core_ref[0]
    unpack(theirs, width_ref, head_ref, early)
    full[:, pl.ds(core, 1)] = early_mine[...][:, None]
    full[:, pl.ds(1 - core, 1)] = early[...][:, None]

    def vector(at, late=0):
        return full[at // 4, at // 2 % 2, at % 2, late : late + 1, :]

    size = full.shape[-1]
    for k in range(3):
        qkv_ref[:, k * size : (k + 1) * size] = vector(k, 4)
    attn_gain_ref[...] = vector(3, 4)
    attn_shift_ref[...] = vector(4, 4)
    out_ref[...] = vector(8)
    down_ref[...] = vector(9)
    ffn_gain_ref[...] = vector(10)
    ffn_shift_ref[...] = vector(11)
    for k in range(RING):
        up_ref[:, k * size : (k + 1) * size] = vector(12 + k)
    prob_ref[...] = vector(16)[:, :128]
    head_out_ref[...] = jnp.concatenate([vector(k) for k in range(CHOICES)], axis=0)
    width_out_ref[...] = jnp.concatenate([vector(CHOICES + k) for k in range(CHOICES)], axis=0)


def result_body(ffn, r1, r2, r3, bias, middle, gate, result_ref):
    total = ffn[...]
    for part in (r1, r2, r3):
        total = total + part[...].astype(f32)
    result_ref[...] = (middle[...] + gate[...] * (total + bias[...])).astype(bf16)


def inputs_body(d_own, r1, r2, r3, tokens, d_middle, gain, d_inputs_ref):
    gradient = d_own[...]
    for part in (r1, r2, r3):
        gradient = gradient + part[...].astype(f32)
    unit, inv_std = normalize(tokens[...].astype(f32))
    scaled = gradient * gain[...]
    inner = (
        scaled
        - jnp.mean(scaled, axis=-1, keepdims=True)
        - unit * jnp.mean(scaled * unit, axis=-1, keepdims=True)
    )
    d_inputs_ref[...] = inner * inv_std + d_middle[...]


def local(
    tokens,
    out_grad,
    qkv_weight,
    qkv_bias,
    out_weight,
    out_bias,
    up_weight,
    up_bias,
    down_weight,
    down_bias,
    attn_gain,
    attn_shift,
    ffn_gain,
    ffn_shift,
    head_router_in,
    head_router_out,
    width_router_in,
    width_router_out,
    head_choice,
    width_choice,
    seq_ids,
):
    rows, width = tokens.shape
    half_rows = RING * rows
    own_heads = HEADS // RING
    head_width = own_heads * HEAD_DIM
    units = up_weight.shape[1] // RING
    router_width = head_router_in.shape[1]
    router_slice = router_width // RING
    all_rows = rows * 128
    core = lax.axis_index("c").astype(jnp.int32)
    place = lax.axis_index("z").astype(jnp.int32)
    one_sequence = (lax.axis_index("yl") == 1) & (seq_ids[0] % 2 == 0)
    core_scalar = core.reshape(1)
    scalars = jnp.stack([core, place, one_sequence.astype(jnp.int32)])
    flipped = [(a * 4 + b, b * 4 + a) for a in range(4) for b in range(4)]
    own_shape = shaped((rows, width), f32)
    part_shape = shaped((rows, width), bf16)
    half_shape = shaped((half_rows, width), bf16)
    sent_shape = shaped((rows + 8, width), bf16)

    def line(vector):
        return vector.reshape(1, -1)

    out_swapped = lax.ppermute(out_weight, ("x", "z"), flipped)
    down_swapped = lax.ppermute(down_weight, ("x", "z"), flipped)
    packed, _ = call(
        pack_body,
        [shaped((RING, 8, 3 * head_width + units + rows), bf16)],
        [qkv_weight, up_weight, line(head_choice), line(width_choice)],
        far=[0, 2, 3],
        room=16,
    )
    ring_order = (place - jnp.arange(RING)) % RING
    order = (ring_order[:, None] * rows + jnp.arange(rows)[None, :]).reshape(half_rows)
    cosine, sine = rotary_tables(order + jnp.where(one_sequence, half_rows, 0))
    head_out = jnp.pad(head_router_out, ((0, 0), (0, 128 - CHOICES)))
    width_out = jnp.pad(width_router_out, ((0, 0), (CHOICES, 128 - 2 * CHOICES)))
    own_up_bias = lax.dynamic_index_in_dim(up_bias.reshape(RING, units), place, 0, keepdims=True)
    own_qkv_bias = lax.dynamic_index_in_dim(qkv_bias.reshape(3, RING, head_width), place, 1, keepdims=False)
    head_squash, head_prob, head_gate, head_done = call(
        head_body,
        [own_shape, shaped((rows, 128), f32), shaped((rows, 1), f32)],
        [tokens, line(attn_gain), line(attn_shift), head_router_in, head_out, line(head_choice)],
        waits=[cosine, width_out, own_up_bias, own_qkv_bias],
    )

    pieces = swap(packed, "z")
    choices = pieces[:, :, 3 * head_width + units :]
    token_blocks = ring_blocks(tokens)
    mixer_all, _ = call(
        mixer_body,
        [shaped((16, 32, width), bf16)],
        [pieces, out_swapped],
        waits=[head_done],
        near_outs=[0],
        room=16,
    )
    mixer_mine = swap(mixer_all, CHIPS)
    mixer_theirs = other_core(mixer_mine)
    rest_all, _ = call(
        count_body,
        [shaped((16, 72, width), bf16)],
        [choices, pieces, down_swapped],
        room=16,
        waits=[mixer_mine] + token_blocks[1:],
    )

    low1_half, query, kv_own, qkv_slice, _ = call(
        project_body,
        [
            half_shape,
            shaped((half_rows, head_width), bf16),
            shaped((half_rows, 2 * head_width), bf16),
            shaped((8, 2, 64, 3 * head_width), bf16),
        ],
        [core_scalar] + token_blocks
        + [
            line(attn_gain), line(attn_shift),
            mixer_mine.reshape(8, 64, -1), mixer_theirs.reshape(8, 64, -1),
            line(own_qkv_bias), cosine, sine,
        ],
        scalars=1,
        near=[7, 8],
    )
    qkv_slice = qkv_slice.reshape(width, 3 * head_width)
    kv_lower = lax.ppermute(kv_own, "yl", [(0, 1)])
    lines = shaped((own_heads * half_rows // QUERIES, 1, QUERIES), f32)
    turned_shape = shaped((half_rows // QUERIES, head_width, QUERIES), f32)
    own_top, own_total, own_out, own_done = call(
        attend_own_body,
        [lines, lines, turned_shape],
        [scalars, query, kv_own],
        [pltpu.VMEM((head_width, half_rows), bf16)],
        scalars=1,
    )
    head_slice, head_slice_done = call(
        head_slice_body,
        [shaped((half_rows, router_slice), f32)],
        [scalars, low1_half, head_router_in],
        scalars=1,
    )
    rest_all, _ = call(nothing, [], [], waits=[own_done], passes=[rest_all])
    rest_mine = swap(rest_all, CHIPS)
    grad_blocks = ring_blocks(out_grad)
    attended, log_total, _ = call(
        attend_body,
        [
            shaped((half_rows, head_width), bf16),
            shaped((own_heads * half_rows // QUERIES, 1, QUERIES), f32),
        ],
        [scalars, query, kv_lower, own_top, own_total, own_out, choices],
        [
            pltpu.VMEM((head_width, half_rows), bf16),
            pltpu.VMEM((half_rows // QUERIES, head_width, QUERIES), f32),
        ],
        scalars=1,
        near=[2],
        waits=grad_blocks[1:],
    )
    out_lanes = (slice(0, 16), slice(0, 32), slice(3 * head_width, 4 * head_width))
    out_slice, p0, p1, p2, p3, _ = call(
        out_body,
        [shaped((head_width, width), bf16), own_shape] + [part_shape] * 3,
        [scalars, attended, mixer_mine, mixer_theirs],
        [pltpu.VMEM((2, 2, 2, 4, 8, width), f32)],
        scalars=1,
        windows={2: out_lanes, 3: out_lanes},
    )
    attn_pre, middle, low2, rest_mine, _ = call(
        middle_body,
        [own_shape, own_shape, part_shape],
        [p0] + [to_sender(part, k) for k, part in ((1, p1), (2, p2), (3, p3))]
        + [tokens, line(out_bias), head_gate, line(ffn_gain), line(ffn_shift)],
        passes=[rest_mine],
    )
    rest_theirs = other_core(rest_mine)

    up_rows, down_rows = (
        (slice(0, 8), slice(0, 2), slice(*at), slice(0, size))
        for at, size in (((0, 32), width), ((32, 64), width))
    )
    count_rows = (slice(0, 16), slice(64, 72), slice(0, 128))
    rest_mine = rest_mine.reshape(8, 2, 72, width)
    rest_theirs = rest_theirs.reshape(8, 2, 72, width)
    (
        ffn_pre, f1, f2, f3, d_normed2, d1, d2, d3, width_dgate, low2_half, d_up, active_low, d_ffn_half,
        d_up_sum, width_prob, width_gate, width_squash, width_slice, forth_done,
    ) = call(
        feed_body,
        [own_shape] + [part_shape] * 3 + [own_shape] + [sent_shape] * 3
        + [shaped((1, rows), f32), half_shape, shaped((half_rows, units), bf16)]
        + [shaped((half_rows, units), bf16), half_shape, shaped((1, units), f32)]
        + [shaped((rows, 128), f32), shaped((rows, 1), f32), shaped((rows, router_width), f32)]
        + [shaped((half_rows, router_slice), f32)],
        [scalars] + ring_blocks(low2)
        + [rest_mine, rest_theirs, own_up_bias]
        + [width_router_in, width_out]
        + [rest_mine, rest_theirs]
        + grad_blocks + [choices],
        [pltpu.VMEM((8, 2, 2, 32, units), bf16), pltpu.VMEM((2, 2, 2, 4, 32, width), bf16)],
        scalars=1,
        room=48,
        windows={5: up_rows, 6: up_rows, 10: down_rows, 11: down_rows},
        near=[8, 12, 13, 14, 15],
        waits=[head_slice_done],
    )
    d_received = [to_sender(part, k) for k, part in ((1, d1), (2, d2), (3, d3))]
    feed_mine, feed_theirs, f1, f2, f3, _ = call(
        feed_weight_body,
        [shaped((16, 64, width), bf16)] * 2 + [part_shape] * 3,
        [core_scalar, low2_half, d_up, active_low, d_ffn_half, f1, f2, f3],
        scalars=1,
    )
    payload, d_middle, d_hidden_head, early, share, feed_theirs, payload_done = call(
        own_back_body,
        [sent_shape, own_shape, part_shape, shaped((32, width), f32), shaped((1, 128), f32)],
        [scalars, d_normed2] + d_received
        + [middle, width_router_in, out_grad, width_squash, head_squash, attn_pre]
        + [width_dgate, line(down_bias), width_prob, width_gate, head_prob, head_gate]
        + [line(head_choice), line(width_choice), rest_mine.reshape(16, 72, width), rest_theirs.reshape(16, 72, width)]
        + [width_out, head_out, line(ffn_gain), d_up_sum],
        scalars=1,
        windows={19: count_rows, 20: count_rows},
        near=[6],
        passes=[feed_theirs],
    )
    feed_part, feed_done = call(pair_body, [shaped((16, 64, width), bf16)], [feed_mine, other_core(feed_theirs)], cost=0, near=[1], near_outs=[0], waits=[payload_done])
    feed_pieces = swap(feed_part, CHIPS)
    router_term1 = against(d_hidden_head, head_router_in)

    d_attn_blocks = ring_blocks(payload)
    mixed_mine, mixed_theirs, mixed_done = call(
        mixer_weight_body,
        [shaped((16, 32, width), bf16)] * 2,
        [scalars, low1_half, low2_half, width_slice, head_slice, width_out, head_out, attended]
        + d_attn_blocks
        + [early],
        [
            pltpu.VMEM((half_rows, router_slice), bf16),
            pltpu.VMEM((half_rows, router_slice), bf16),
            pltpu.VMEM((head_width, width), f32),
            pltpu.VMEM((rows, rows), f32),
        ],
        scalars=1,
        waits=[feed_done],
    )
    gradient_scratch = [pltpu.VMEM((half_rows, head_width), f32)] * 2
    d_lower, d_out, d_mean, d_query_lower, d_lower_done = call(
        attend_back_body,
        [
            shaped((half_rows, 2 * head_width), bf16),
            shaped((half_rows, head_width), bf16),
            lines,
            turned_shape,
        ],
        [scalars] + d_attn_blocks + [out_slice, query, kv_lower, choices, log_total, attended],
        [pltpu.VMEM((head_width, half_rows), bf16)] + gradient_scratch,
        scalars=1,
        cost=0,
        waits=[mixed_done],
    )
    back = lax.ppermute(d_lower, "yl", [(1, 0)])
    d_query, d_kv_own, d_query_done = call(
        attend_back_own_body,
        [shaped((half_rows, head_width), bf16), shaped((half_rows, 2 * head_width), f32)],
        [scalars, query, kv_own, log_total, d_out, d_mean, d_query_lower, cosine, sine],
        [
            pltpu.VMEM((head_width, half_rows), bf16),
            pltpu.VMEM((half_rows // QUERIES, head_width, QUERIES), f32),
        ]
        + gradient_scratch,
        scalars=1,
    )
    mixed_part, mixed_part_done = call(
        pair_body,
        [shaped((16, 32, width), bf16)],
        [mixed_mine, other_core(mixed_theirs)],
        cost=0,
        near=[1],
        near_outs=[0],
        waits=[d_query_done, feed_pieces],
    )
    mixer_pieces = swap(mixed_part, CHIPS)
    d_mixed, d_own, gain_shift, d_mixed_sum, *d_sent, _ = call(
        project_back_body,
        [
            shaped((half_rows, 3 * head_width), bf16),
            own_shape,
            shaped((2, width), f32),
            shaped((1, 3 * head_width), f32),
        ]
        + [part_shape] * 3,
        [back, d_kv_own, d_query, qkv_slice, cosine, sine] + token_blocks + [router_term1],
        waits=[mixed_part_done],
    )
    d_sent = [to_sender(part, k) for k, part in enumerate(d_sent, 1)]
    d_inputs, d_inputs_done = call(
        inputs_body,
        [own_shape],
        [d_own] + d_sent + [tokens, d_middle, line(attn_gain)],
        room=16,
    )
    result, result_done = call(
        result_body,
        [part_shape],
        [ffn_pre] + [to_sender(part, k) for k, part in ((1, f1), (2, f2), (3, f3))]
        + [line(down_bias), middle, width_gate],
        room=16,
        waits=[d_inputs_done],
    )

    feed_rows = block_sum(feed_pieces)
    down_grad = lax.ppermute(feed_rows[32:], ("x", "z"), flipped)
    mine, theirs, _ = call(
        project_weight_body,
        [shaped((8, 64, 3 * head_width + 256), bf16)] * 2,
        [scalars, low1_half, d_mixed, d_mixed_sum, gain_shift],
        scalars=1,
    )
    qkv_part, qkv_part_done = call(
        pair_body,
        [shaped((8, 64, 3 * head_width + 256), bf16)],
        [mine, other_core(theirs)],
        cost=0,
        near=[1],
        near_outs=[0],
        waits=[mixer_pieces],
    )
    qkv_part = swap(qkv_part.reshape(64, 8, -1), CHIPS + ("z",))
    qkv_grad, late, _ = call(
        project_sum_body,
        [shaped((8, 3 * width), f32), shaped((1, width), f32)],
        [qkv_part],
        near=[0],
    )

    shared, out_rows, _ = call(
        mixer_sum_body,
        [shaped((24, width), bf16), shaped((8, width), f32)],
        [mixer_pieces],
        near=[0],
    )
    out_grad_rows = lax.ppermute(out_rows, ("x", "z"), flipped)
    up_rows = feed_rows[:32].reshape(RING, 8, units).astype(bf16)
    from_ring = []
    for shift in range(RING):
        rows_of = lax.dynamic_index_in_dim(up_rows, (place + shift) % RING, 0, keepdims=False)
        block = jnp.concatenate([shared, rows_of], axis=0)
        if shift:
            block = lax.ppermute(block, "z", [(k, (k + shift) % RING) for k in range(RING)])
        from_ring.append(block)
    from_ring = jnp.take(jnp.stack(from_ring), ring_order, axis=0)
    early_sum = jnp.sum(from_ring[:, 16:24].astype(f32), axis=0).astype(bf16)
    up_grad = jnp.concatenate([from_ring[k, 24:] for k in range(RING)], axis=1).astype(f32)

    lanes = router_slice
    routers = jnp.concatenate(
        [
            jnp.concatenate([from_ring[k, :16, j * lanes : (j + 1) * lanes] for k in range(RING)], axis=1)
            for j in (0, 2, 1, 3)
        ]
        + [early_sum[:4], jnp.broadcast_to(late.astype(bf16), (4, width))],
        axis=0,
    )
    routers_mine = spread(routers, CHIPS, 16)
    routers_theirs = other_core(routers_mine)
    half_part = (8, 1, 64, router_width)

    def own_half(scalars):
        return (slice(None), pl.ds(scalars[0], 1))

    def other_half(scalars):
        return (slice(None), pl.ds(1 - scalars[0], 1))

    whole_shape = shaped((8, 2, 64, router_width), f32)
    width_in_grad, head_in_grad, early_mine, _ = call(
        routers_own_body,
        [whole_shape, whole_shape, shaped((8, 2, 8, width), f32)],
        [core_scalar, routers_mine],
        scalars=1,
        near=[1],
        waits=[result_done],
        partly={0: (half_part, own_half), 1: (half_part, own_half)},
    )
    vectors = [3 * width, width, RING * units, width, width, width, width, width]
    width_in_grad, head_in_grad, *vectors, head_out_grad, width_out_grad, prob_sums, _ = call(
        routers_body,
        [whole_shape, whole_shape]
        + [shaped((1, size), f32) for size in vectors]
        + [shaped((CHOICES, router_width), f32)] * 2
        + [shaped((1, 128), f32)],
        [core_scalar, routers_theirs, early_mine],
        [pltpu.VMEM((8, 2, 8, width), f32), pltpu.VMEM((8, 2, 2, 8, width), f32)],
        scalars=1,
        near=[1],
        partly={0: (half_part, other_half), 1: (half_part, other_half)},
        into=[width_in_grad, head_in_grad],
    )
    width_in_grad = width_in_grad.reshape(width, router_width)
    head_in_grad = head_in_grad.reshape(width, router_width)
    balance = CHOICES * jnp.sum(share * prob_sums / all_rows)

    return (
        result,
        balance,
        d_inputs,
        qkv_grad,
        out_grad_rows,
        up_grad,
        down_grad,
        *[vector.reshape(-1) for vector in vectors],
        head_in_grad,
        head_out_grad.T,
        width_in_grad,
        width_out_grad.T,
    )


def solution(mesh):
    fine = Mesh(mesh.devices.reshape(4, 2, 2, 2, 4), AXES)
    whole = P(AXES, None)
    vector = P(AXES)
    in_specs = (
        whole, whole, whole, P(), whole, P(), whole, P(), whole, P(),
        P(), P(), P(), P(), P(), P(), P(), P(), vector, vector, vector,
    )
    out_specs = (whole, P(), whole, whole, whole, whole, whole) + (P(),) * 12
    return jax.shard_map(local, mesh=fine, in_specs=in_specs, out_specs=out_specs, check_vma=False)
```
